128 devices in a mesh: lon: 8 (over z, y_hi), lat: 16 (over y_lo, x, core).
Axes of the slice: x: 4, y: 4 (y_hi: 2, y_lo: 2; y = y_hi * 2 + y_lo), z: 4, core: 2. Of those that a mesh axis runs over, the one named last changes fastest.
Arguments:
- atmos_state: bfloat16 [512, 512, 256], P('lat', 'lon'), may hold values from -6 to 6
- atmos_weights: bfloat16 [9, 256, 256], replicated, may hold values from -0.125 to 0.125
- flux_project: bfloat16 [256, 64], replicated, may hold values from -0.75 to 0.75
- source_row: int32 [512, 512, 4], P('lat', 'lon'), may hold values from 0 to 511, as said below
- source_col: int32 [512, 512, 4], P('lat', 'lon'), may hold values from 0 to 511, as said below
- intersection_weight: float32 [512, 512, 4], P('lat', 'lon'), may hold values from 0 to 1
- ocean_state: bfloat16 [512, 512, 256], P('lat', 'lon'), may hold values from -6 to 6
- flux_inject: bfloat16 [64, 256], replicated, may hold values from -0.75 to 0.75
- ocean_mask: int32 [512, 512], P('lat', 'lon'), may hold values 0 or 1
- ocean_weights: bfloat16 [9, 256, 256], replicated, may hold values from -0.125 to 0.125
- out_cotangent: bfloat16 [512, 512, 256], P('lat', 'lon'), may hold values from -6 to 6
Outputs:
- ocean_out: bfloat16 [512, 512, 256], P('lat', 'lon')
- grad_atmos: float32 [9, 256, 256], replicated
- grad_ocean: float32 [9, 256, 256], replicated
- grad_project: float32 [256, 64], replicated
- grad_inject: float32 [64, 256], replicated
The draws below stay inside these ranges and needn't reach their ends.
Inputs may be any that keep to these rules, and one draw needn't show every extreme that they name: `source_row`: entry k of ocean cell (j, i) names an atmosphere row within 2 rows of j; for ocean rows j >= 512 - 32 (the band beside the fold) within 32 rows of j; both reaches are attained. `source_col`: entry k of ocean cell (j, i) names an atmosphere column within 2 columns of i, counted cyclically; for ocean rows j >= 480 within 64 columns of i; both reaches are attained.
All inputs are finite; a program needn't handle non-finite values. No bound on the sum of `ocean_mask` on one device may be relied on, other than what follows from the above.
Results may differ from the reference program's by a relative error of at most 0.018.
Values may be sent and summed in bfloat16 or wider, within the bound.
No kernel may reach another device: no remote copies, remote signals or barrier semaphores. Data moves between devices by JAX's collectives and lax.ppermute only.
A program may use at most 128 MiB of HBM per device.

```python
import jax
import jax.numpy as jnp
from jax import lax

C = 256
F = 64
K = 4
TY = 32
TX = 64
NY = 512
NX = 512
N_LON = 8


def draw_source_row(key, part):
    base_rows = jnp.arange(NY, dtype=jnp.int32)[:, None, None]
    col_ids = jnp.arange(NX, dtype=jnp.int32)[None, :, None]
    entry_ids = jnp.arange(K, dtype=jnp.int32)[None, None, :]
    near = jax.random.randint(jax.random.fold_in(key, 11), (NY, NX, K), -2, 3, dtype=jnp.int32)
    wide = jax.random.randint(jax.random.fold_in(key, 13), (NY, NX, K), -TY, TY + 1, dtype=jnp.int32)
    in_band = base_rows >= NY - TY
    near = jnp.where((col_ids == 0) & (entry_ids == K - 1), jnp.int32(-2), near)
    wide = jnp.where((col_ids == 0) & (entry_ids == 0), jnp.int32(-TY), wide)
    offsets = jnp.where(in_band, wide, near)
    return jnp.clip(base_rows + offsets, 0, NY - 1).astype(jnp.int32)


def draw_source_col(key, part):
    base_rows = jnp.arange(NY, dtype=jnp.int32)[:, None, None]
    base_cols = jnp.arange(NX, dtype=jnp.int32)[None, :, None]
    entry_ids = jnp.arange(K, dtype=jnp.int32)[None, None, :]
    near = jax.random.randint(jax.random.fold_in(key, 23), (NY, NX, K), -2, 3, dtype=jnp.int32)
    wide = jax.random.randint(jax.random.fold_in(key, 29), (NY, NX, K), -TX, TX + 1, dtype=jnp.int32)
    in_band = base_rows >= NY - TY
    near = jnp.where((base_rows == 0) & (entry_ids == K - 1), jnp.int32(2), near)
    wide = jnp.where((base_rows == NY - 1) & (entry_ids == 0), jnp.int32(TX), wide)
    offsets = jnp.where(in_band, wide, near)
    return jnp.remainder(base_cols + offsets, NX).astype(jnp.int32)


def plant(entries, own_key, least, high):
    longest = entries.shape.index(max(entries.shape))
    spots = []
    for shift in (0, 1):
        where = [jax.random.randint(jax.random.fold_in(own_key, axis), (), 0, length) for axis, length in enumerate(entries.shape)]
        where[longest] = (where[longest] + shift) % entries.shape[longest]
        spots.append(tuple(where))
    return entries.at[spots[0]].set(least).at[spots[1]].set(high)


def steps_of(stream_key, shape, shards, low, high):
    def one(axis_at, blocks):
        steps = jax.random.uniform(jax.random.fold_in(jax.random.fold_in(stream_key, 6), axis_at), (blocks,), jnp.float32, low / len(shards), high / len(shards))
        return jnp.repeat(jnp.exp(steps), shape[axis_at] // blocks).reshape((-1,) + (1,) * (len(shape) - axis_at - 1))

    gain = one(*shards[0])
    for cut in shards[1:]:
        gain = gain * one(*cut)
    return gain


def normal_values(key, dims, spread, limit, pieces=(), kind=jnp.bfloat16):
    values = jax.random.normal(key, dims, jnp.float32) * spread
    if len(pieces) > 0:
        values = steps_of(key, dims, pieces, -0.22, 0.18) * values
    return jnp.clip(values, min=-limit, max=limit).astype(kind)


def setup_inputs(seed: int = 0) -> dict:
    arg_keys = jax.random.split(jax.random.key(seed), 12)
    atmos_state = normal_values(arg_keys[0], (NY, NX, C), 1.0, 6.0, ((0, 16), (1, 8)))
    atmos_weights = normal_values(arg_keys[1], (9, C, C), (9 * C) ** -0.5, 0.125)
    flux_project = normal_values(arg_keys[2], (C, F), (C // 4) ** -0.5, 0.75)
    source_row = draw_source_row(jax.random.fold_in(arg_keys[11], 71), 0)
    source_col = draw_source_col(jax.random.fold_in(arg_keys[11], 71), 0)
    intersection_weight = jnp.clip(1.0 * jax.random.uniform(arg_keys[5], (NY, NX, K), jnp.float32) ** steps_of(arg_keys[5], (NY, NX, K), ((0, 16), (1, 8)), -0.2, 0.2), 0.0, 1.0)
    ocean_state = normal_values(arg_keys[6], (NY, NX, C), 1.0, 6.0, ((0, 16), (1, 8)))
    flux_inject = normal_values(arg_keys[7], (F, C), F ** -0.5, 0.75)
    ocean_mask = plant((jax.random.randint(arg_keys[8], (NY, NX), 0, 4) < 3).astype(jnp.int32), jax.random.fold_in(arg_keys[8], 1), 0, 1)
    ocean_weights = normal_values(arg_keys[9], (9, C, C), (9 * C) ** -0.5, 0.125)
    out_cotangent = normal_values(arg_keys[10], (NY, NX, C), 1.0, 6.0, ((0, 16), (1, 8)))
    return {"atmos_state": atmos_state, "atmos_weights": atmos_weights, "flux_project": flux_project, "source_row": source_row, "source_col": source_col, "intersection_weight": intersection_weight, "ocean_state": ocean_state, "flux_inject": flux_inject, "ocean_mask": ocean_mask, "ocean_weights": ocean_weights, "out_cotangent": out_cotangent}


def pad_atmos(field):
    zero_row = jnp.zeros_like(field[:1])
    padded = jnp.concatenate([zero_row, field, zero_row], 0)
    return jnp.concatenate([padded[:, -1:], padded, padded[:, :1]], 1)

def pad_ocean(field):
    zero_row = jnp.zeros_like(field[:1])
    folded = field[-1:, ::-1]
    padded = jnp.concatenate([zero_row, field, folded], 0)
    return jnp.concatenate([padded[:, -1:], padded, padded[:, :1]], 1)

def silu_slope(value):
    sigma = jax.nn.sigmoid(value)
    return sigma * (1.0 + value * (1.0 - sigma))

def convolve(padded, weights):
    row_count = padded.shape[0] - 2
    col_count = padded.shape[1] - 2
    chans = weights.shape[2]
    total = jnp.zeros((row_count * col_count, chans), jnp.float32)
    for tap_index in range(9):
        row_off, col_off = divmod(tap_index, 3)
        window = padded[row_off:row_off + row_count, col_off:col_off + col_count].reshape(-1, padded.shape[2])
        total = total + jnp.dot(window, weights[tap_index], preferred_element_type=jnp.float32)
    return total.reshape(row_count, col_count, chans)

def kernel_grads(padded, delta):
    row_count, col_count, chans = delta.shape
    flat_delta = delta.reshape(-1, chans)
    result = []
    for tap_index in range(9):
        row_off, col_off = divmod(tap_index, 3)
        window = padded[row_off:row_off + row_count, col_off:col_off + col_count].reshape(-1, padded.shape[2])
        result.append(jnp.dot(window.T, flat_delta, preferred_element_type=jnp.float32))
    return jnp.stack(result)

def reference(atmos_state, atmos_weights, flux_project, source_row, source_col, intersection_weight, ocean_state, flux_inject, ocean_mask, ocean_weights, out_cotangent):
    land = ocean_mask.astype(jnp.float32)[..., None]
    atmos_padded = pad_atmos(atmos_state)
    atmos_pre = convolve(atmos_padded, atmos_weights)
    atmos_act = jax.nn.silu(atmos_pre).astype(jnp.bfloat16)
    flux = jnp.dot(atmos_act.reshape(-1, C), flux_project, preferred_element_type=jnp.float32).astype(jnp.bfloat16).reshape(NY, NX, F)
    picked = flux[source_row, source_col].astype(jnp.float32)
    remapped = lax.optimization_barrier(jnp.sum(intersection_weight[..., None] * picked, axis=2)).astype(jnp.bfloat16)
    injected = jnp.dot(remapped.reshape(-1, F), flux_inject, preferred_element_type=jnp.float32).reshape(NY, NX, C)
    mixed = (land * (ocean_state.astype(jnp.float32) + injected)).astype(jnp.bfloat16)
    ocean_padded = pad_ocean(mixed)
    ocean_pre = convolve(ocean_padded, ocean_weights)
    ocean_out = (land * jax.nn.silu(ocean_pre)).astype(jnp.bfloat16)
    ocean_delta = (out_cotangent.astype(jnp.float32) * land * silu_slope(ocean_pre)).astype(jnp.bfloat16)
    grad_ocean = kernel_grads(ocean_padded, ocean_delta)
    flat_delta = ocean_delta.reshape(-1, C)
    delta_pad = jnp.zeros((NY + 2, NX + 2, C), jnp.float32)
    for tap_index in range(9):
        row_off, col_off = divmod(tap_index, 3)
        contrib = lax.dot_general(flat_delta, ocean_weights[tap_index], (((1,), (1,)), ((), ())), preferred_element_type=jnp.float32).reshape(NY, NX, C)
        delta_pad = delta_pad.at[row_off:row_off + NY, col_off:col_off + NX].add(contrib)
    _, pullback = jax.vjp(pad_ocean, jnp.zeros((NY, NX, C), jnp.float32))
    ocean_back = pullback(delta_pad)[0]
    mixed_grad = (land * ocean_back).astype(jnp.bfloat16)
    flat_mixed = mixed_grad.reshape(-1, C)
    grad_inject = jnp.dot(remapped.reshape(-1, F).T, flat_mixed, preferred_element_type=jnp.float32)
    remap_grad = lax.dot_general(flat_mixed, flux_inject, (((1,), (1,)), ((), ())), preferred_element_type=jnp.float32).astype(jnp.bfloat16).reshape(NY, NX, F)
    tile_rows = (jnp.arange(NY, dtype=jnp.int32) // TY)[:, None, None]
    tile_cols = (jnp.arange(NX, dtype=jnp.int32) // TX)[None, :, None]
    tile_dr = source_row // TY - tile_rows
    tile_dc = jnp.remainder(source_col // TX - tile_cols + 1, N_LON) - 1
    entry_code = (tile_dr + 1) * 3 + tile_dc + 1
    flat_source = (source_row * NX + source_col).reshape(-1)
    contrib_all = intersection_weight[..., None] * remap_grad.astype(jnp.float32)[:, :, None, :]
    flux_sum = jnp.zeros((NY * NX, F), jnp.float32)
    for code_value in range(9):
        chosen = jnp.where((entry_code == code_value)[..., None], contrib_all, jnp.float32(0.0)).reshape(-1, F)
        credit = jnp.zeros((NY * NX, F), jnp.float32).at[flat_source].add(chosen)
        flux_sum = flux_sum + lax.optimization_barrier(credit.astype(jnp.bfloat16)).astype(jnp.float32)
    flux_grad = flux_sum.astype(jnp.bfloat16)
    flat_act = atmos_act.reshape(-1, C)
    grad_project = jnp.dot(flat_act.T, flux_grad, preferred_element_type=jnp.float32)
    act_grad = lax.dot_general(flux_grad, flux_project, (((1,), (1,)), ((), ())), preferred_element_type=jnp.float32).reshape(NY, NX, C)
    atmos_delta = (act_grad * silu_slope(atmos_pre)).astype(jnp.bfloat16)
    grad_atmos = kernel_grads(atmos_padded, atmos_delta)
    return (ocean_out, grad_atmos, grad_ocean, grad_project, grad_inject)
```

```python
import jax
import jax.numpy as jnp
from jax import lax
from jax.experimental import pallas as pl
from jax.experimental.pallas import tpu as pltpu
from jax.sharding import PartitionSpec as P

BF = jnp.bfloat16
F32 = jnp.float32
VLIM = 56 << 20
AXES = ("lon", "lat")
NEAR = 72
BAND = 192


def passed_along(x, axis, by):
    length = lax.axis_size(axis)
    pairs = [(i, i + by) for i in range(length) if 0 <= i + by < length]
    return lax.ppermute(x, axis, pairs)


def shifted(x, axis, by):
    length = lax.axis_size(axis)
    return lax.ppermute(x, axis, [(i, (i + by) % length) for i in range(length)])


def mirror_row(edge_row):
    length = lax.axis_size("lon")
    moved = lax.ppermute(edge_row, "lon", [(i, length - 1 - i) for i in range(length)])
    return moved[:, ::-1]


def pad_field(field, is_top, folding):
    south = passed_along(field[-1:], "lat", 1)
    north = passed_along(field[:1], "lat", -1)
    if folding:
        north = jnp.where(is_top, mirror_row(field[-1:]), north)
    padded = jnp.concatenate([south, field, north], 0)
    west = shifted(padded[:, -1:], "lon", 1)
    east = shifted(padded[:, :1], "lon", -1)
    return jnp.concatenate([west, padded, east], 1)


def silu_slope(value):
    sigma = jax.nn.sigmoid(value)
    return sigma * (1.0 + value * (1.0 - sigma))


def convolve(padded, weights, row_count, col_count):
    total = jnp.zeros((row_count * col_count, weights.shape[2]), F32)
    for tap_index in range(9):
        row_off, col_off = divmod(tap_index, 3)
        window = padded[row_off : row_off + row_count, col_off : col_off + col_count].reshape(
            row_count * col_count, -1
        )
        total = total + jnp.dot(window, weights[tap_index], preferred_element_type=F32)
    return total


def kernel_grads(padded, delta, row_count, col_count):
    result = []
    for tap_index in range(9):
        row_off, col_off = divmod(tap_index, 3)
        window = padded[row_off : row_off + row_count, col_off : col_off + col_count].reshape(
            row_count * col_count, -1
        )
        result.append(jnp.einsum("nc,nd->cd", window, delta, preferred_element_type=F32))
    return jnp.stack(result)


def transpose_conv(delta_pad, weights, is_top, row_count, col_count):
    dims = (((1,), (1,)), ((), ()))
    north = delta_pad[-1:]
    plain = jnp.concatenate([delta_pad[:-1], jnp.where(is_top, jnp.zeros_like(north), north)], 0)
    total = jnp.zeros((row_count * col_count, weights.shape[1]), F32)
    for tap_index in range(9):
        row_off, col_off = divmod(tap_index, 3)
        window = plain[
            2 - row_off : 2 - row_off + row_count, 2 - col_off : 2 - col_off + col_count
        ].reshape(row_count * col_count, -1)
        total = total + lax.dot_general(window, weights[tap_index], dims, preferred_element_type=F32)
    total = total.reshape(row_count, col_count, -1)
    seam_term = jnp.zeros((col_count, weights.shape[1]), F32)
    for col_off in range(3):
        seam_term = seam_term + lax.dot_general(
            north[0, col_off : col_off + col_count],
            weights[6 + col_off],
            dims,
            preferred_element_type=F32,
        )
    seam_term = jnp.where(is_top, seam_term, jnp.zeros_like(seam_term))
    return total.at[row_count - 1].add(seam_term)


def exchange(x, mask):
    count = lax.axis_size("lon") * lax.axis_size("lat")
    return lax.ppermute(x, AXES, [(i, i ^ mask) for i in range(count)])


def reduce_all(x):
    rank = lax.axis_index("lon") * lax.axis_size("lat") + lax.axis_index("lat")
    bit = lambda n: (rank >> n) & 1
    halving = [(1, bit(0)), (2, bit(1) ^ bit(2)), (8, bit(3) ^ bit(4)), (32, bit(5) ^ bit(6))]
    doubling = [6, 24, 96]
    v = x
    for mask, here in halving:
        half = v.shape[0] // 2
        keep = lax.dynamic_slice_in_dim(v, here * half, half)
        send = lax.dynamic_slice_in_dim(v, (1 - here) * half, half).astype(BF)
        v = keep + exchange(send, mask).astype(F32)
    for mask in doubling:
        mine = v.astype(BF)
        v = mine.astype(F32) + exchange(mine, mask).astype(F32)
    v = v.astype(BF)
    for mask, here in halving[::-1]:
        other = exchange(v, mask)
        v = jnp.where(here == 0, jnp.concatenate([v, other]), jnp.concatenate([other, v]))
    return v.astype(F32)


def reduce_pair(big, small):
    rows = jnp.concatenate([big.reshape(-1, 256), small, jnp.zeros((64, 256), F32)])
    total = reduce_all(rows)
    return total[: 9 * 256].reshape(9, 256, 256), total[9 * 256 : 9 * 256 + 64]


def lane_sign():
    lane = lax.broadcasted_iota(jnp.int32, (64, 128), 1)
    return jnp.where(lane < 64, jnp.float32(1.0), jnp.float32(-1.0))


def gather_kernel(top_ref, slot_ref, w_ref, ext_ref, halo_ref, low_ref, own_ref, west_ref, east_ref, out_ref, table, picked):
    top = top_ref[0]

    @pl.when(top == 0)
    def _():
        for r in range(20):
            table[r * NEAR : r * NEAR + 64, :] = ext_ref[r].astype(F32)
            table[r * NEAR + 64 : r * NEAR + 72, :] = halo_ref[r].astype(F32)

    @pl.when(top != 0)
    def _():
        for r in range(32):
            base = r * BAND
            table[base : base + 64, :] = (low_ref[r] if r < 16 else own_ref[r - 16]).astype(F32)
            table[base + 64 : base + 128, :] = west_ref[r].astype(F32)
            table[base + 128 : base + 192, :] = east_ref[r].astype(F32)

    def step(q, carry):
        base = pl.multiple_of(q * 64, 64)
        for u in range(64):
            at = slot_ref[q, u]
            picked[pl.ds(base + u, 1), :] = table[pl.ds(at, 1), :]
        return carry

    lax.fori_loop(0, 128, step, 0)
    sign = lane_sign()
    wt = w_ref[...].T
    for row in range(32):
        acc = jnp.zeros((64, 128), F32)
        for k in range(4):
            q = row * 4 + k
            factor = jnp.maximum(wt[:, q : q + 1] * sign, 0.0)
            acc = acc + factor * picked[q * 64 : q * 64 + 64, :]
        acc = acc + pltpu.roll(acc, 64, 1)
        out_ref[row * 64 : row * 64 + 64, :] = acc.astype(BF)


def gather_rows(top, slots, weights, ext, halo, low, own, west, east):
    smem = pl.BlockSpec(memory_space=pltpu.SMEM)
    vmem = pl.BlockSpec(memory_space=pltpu.VMEM)
    return pl.pallas_call(
        gather_kernel,
        name="gather_rows",
        out_shape=jax.ShapeDtypeStruct((2048, 128), BF),
        in_specs=[smem, smem] + [vmem] * 7,
        out_specs=vmem,
        scratch_shapes=[pltpu.VMEM((32 * BAND, 128), F32), pltpu.VMEM((8192, 128), F32)],
        compiler_params=pltpu.CompilerParams(vmem_limit_bytes=VLIM),
    )(top, slots, weights, ext, halo, low, own, west, east)


def scatter_kernel(top_ref, slot_ref, w_ref, g_ref, ext_ref, halo_ref, low_ref, west_ref, east_ref, t0, t1, t2, t3, parts):
    top = top_ref[0]
    tables = (t0, t1, t2, t3)

    def clear(count):
        def one(i, carry):
            base = pl.multiple_of(i * 96, 96)
            for t in tables:
                t[pl.ds(base, 96), :] = jnp.zeros((96, 128), F32)
            return carry

        lax.fori_loop(0, count // 96, one, 0)

    @pl.when(top == 0)
    def _():
        clear(20 * NEAR)

    @pl.when(top != 0)
    def _():
        clear(32 * BAND)

    sign = lane_sign()
    wt = w_ref[...].T
    for row in range(32):
        g = g_ref[row * 64 : row * 64 + 64, :].astype(F32)
        for k in range(4):
            q = row * 4 + k
            parts[q * 64 : q * 64 + 64, :] = jnp.maximum(wt[:, q : q + 1] * sign, 0.0) * g

    def step(row, carry):
        base = pl.multiple_of(row * 256, 256)
        for u in range(64):
            for k in range(4):
                at = slot_ref[row * 4 + k, u]
                t = tables[k]
                t[pl.ds(at, 1), :] = t[pl.ds(at, 1), :] + parts[pl.ds(base + k * 64 + u, 1), :]
        return carry

    lax.fori_loop(0, 32, step, 0)

    def total(start, size):
        where = pl.ds(start, size)
        return ((t0[where, :] + t1[where, :]) + (t2[where, :] + t3[where, :])).astype(BF)

    @pl.when(top == 0)
    def _():
        for r in range(20):
            ext_ref[r] = total(r * NEAR, 64)
            halo_ref[r] = total(r * NEAR + 64, 8)
        for r in range(16):
            low_ref[r] = jnp.zeros((64, 128), BF)
        for r in range(32):
            west_ref[r] = jnp.zeros((64, 128), BF)
            east_ref[r] = jnp.zeros((64, 128), BF)

    @pl.when(top != 0)
    def _():
        for r in range(20):
            halo_ref[r] = jnp.zeros((8, 128), BF)
        for r in range(4):
            ext_ref[16 + r] = jnp.zeros((64, 128), BF)
        for r in range(32):
            base = r * BAND
            if r < 16:
                low_ref[r] = total(base, 64)
            else:
                ext_ref[r - 16] = total(base, 64)
            west_ref[r] = total(base + 64, 64)
            east_ref[r] = total(base + 128, 64)


def scatter_rows(top, slots, weights, grads):
    smem = pl.BlockSpec(memory_space=pltpu.SMEM)
    vmem = pl.BlockSpec(memory_space=pltpu.VMEM)
    struct = lambda *shape: jax.ShapeDtypeStruct(shape, BF)
    return pl.pallas_call(
        scatter_kernel,
        name="scatter_rows",
        out_shape=(struct(20, 64, 128), struct(20, 8, 128), struct(16, 64, 128), struct(32, 64, 128), struct(32, 64, 128)),
        in_specs=[smem, smem, vmem, vmem],
        out_specs=(vmem,) * 5,
        scratch_shapes=[pltpu.VMEM((32 * BAND, 128), F32)] * 4 + [pltpu.VMEM((8192, 128), F32)],
        compiler_params=pltpu.CompilerParams(vmem_limit_bytes=VLIM),
    )(top, slots, weights, grads)


def band_lon(x, by):
    lons, lats = lax.axis_size("lon"), lax.axis_size("lat")
    return lax.ppermute(x, AXES, [(i * lats + lats - 1, ((i + by) % lons) * lats + lats - 1) for i in range(lons)])


def entry_slots(source_row, source_col, weight, is_top, row_count, col_count):
    nx = col_count * lax.axis_size("lon")
    row = source_row - lax.axis_index("lat") * row_count
    col = jnp.remainder(source_col - lax.axis_index("lon") * col_count + nx // 2, nx) - nx // 2
    half = row_count // 2
    inside = (row >= 0) & (row < row_count)
    wrapped = row & (row_count - 1)
    packed = wrapped & (half - 1)
    upper = wrapped >= half
    near_row = jnp.where(inside, packed, jnp.where(row < 0, packed + 4, packed + half))
    near_col = jnp.where((col >= 0) & (col < col_count), col, jnp.where(col < 0, col + col_count + 2, col + 2))
    band_row = jnp.where(row >= 0, packed + half, packed)
    band_col = jnp.where((col >= 0) & (col < col_count), col, jnp.where(col < 0, col + 2 * col_count, col + col_count))
    slot = jnp.where(is_top, band_row * BAND + band_col, near_row * NEAR + near_col)
    signed = jnp.where(upper, -weight, weight)
    order = lambda x: jnp.transpose(x, (0, 2, 1)).reshape(-1, col_count)
    return order(slot), order(signed)


def body(
    atmos_state,
    atmos_weights,
    flux_project,
    source_row,
    source_col,
    intersection_weight,
    ocean_state,
    flux_inject,
    ocean_mask,
    ocean_weights,
    out_cotangent,
):
    row_count, col_count, chans = atmos_state.shape
    flux_chans = flux_project.shape[1]
    cells = row_count * col_count
    half = cells // 2
    dims = (((1,), (1,)), ((), ()))
    lats = lax.axis_size("lat")
    is_top = lax.axis_index("lat") == lats - 1
    top = jnp.broadcast_to(is_top.astype(jnp.int32), (1,))
    land = ocean_mask.astype(F32)[..., None]
    slots, signed = entry_slots(source_row, source_col, intersection_weight, is_top, row_count, col_count)
    atmos_padded = pad_field(atmos_state, is_top, False)
    atmos_pre = convolve(atmos_padded, atmos_weights, row_count, col_count)
    atmos_act = jax.nn.silu(atmos_pre).astype(BF)
    flux = jnp.dot(atmos_act, flux_project, preferred_element_type=F32).astype(BF)
    own = jnp.concatenate([flux[:half], flux[half:]], 1).reshape(row_count // 2, col_count, 2 * flux_chans)
    south = passed_along(own[-2:], "lat", 1)
    north = passed_along(own[:2], "lat", -1)
    ext = jnp.concatenate([own, north, south], 0)
    west = shifted(ext[:, -2:], "lon", 1)
    east = shifted(ext[:, :2], "lon", -1)
    halo = jnp.concatenate([west, east, jnp.zeros((20, 4, 2 * flux_chans), BF)], 1)
    low = lax.ppermute(own, "lat", [(lats - 2, lats - 1)])
    two = jnp.concatenate([low, own], 0)
    band_west = band_lon(two, 1)
    band_east = band_lon(two, -1)
    remapped = gather_rows(top, slots, signed, ext, halo, low, own, band_west, band_east)
    inject_pad = jnp.concatenate([flux_inject, jnp.zeros_like(flux_inject)], 0)
    injected = jnp.dot(remapped, inject_pad, preferred_element_type=F32).reshape(row_count, col_count, chans)
    mixed = (land * (ocean_state.astype(F32) + injected)).astype(BF)
    ocean_padded = pad_field(mixed, is_top, True)
    ocean_pre = convolve(ocean_padded, ocean_weights, row_count, col_count).reshape(row_count, col_count, chans)
    ocean_out = (land * jax.nn.silu(ocean_pre)).astype(BF)
    ocean_delta = (out_cotangent.astype(F32) * land * silu_slope(ocean_pre)).astype(BF)
    grad_ocean = kernel_grads(ocean_padded, ocean_delta.reshape(cells, chans), row_count, col_count)
    delta_padded = pad_field(ocean_delta, is_top, True)
    ocean_back = transpose_conv(delta_padded, ocean_weights, is_top, row_count, col_count)
    mixed_grad = (land * ocean_back).astype(BF).reshape(cells, chans)
    grad_inject = jnp.einsum("nf,nc->fc", remapped, mixed_grad, preferred_element_type=F32)[:flux_chans]
    inject_two = jnp.concatenate([flux_inject, flux_inject], 0)
    remap_grad = lax.dot_general(mixed_grad, inject_two, dims, preferred_element_type=F32).astype(BF)
    ext, halo, low, out_west, out_east = scatter_rows(top, slots, signed, remap_grad)
    from_east = shifted(halo[:, :2], "lon", -1).astype(F32)
    from_west = shifted(halo[:, 2:4], "lon", 1).astype(F32)
    band_from_east = band_lon(out_west, -1).astype(F32)
    band_from_west = band_lon(out_east, 1).astype(F32)
    ext = ext.astype(F32)
    ext = ext.at[:, -2:].add(from_east).at[:, :2].add(from_west)
    own = ext[:16] + band_from_east[16:] + band_from_west[16:]
    low = low.astype(F32) + band_from_east[:16] + band_from_west[:16]
    from_south = passed_along(ext[16:18].astype(BF), "lat", 1).astype(F32)
    from_north = passed_along(ext[18:20].astype(BF), "lat", -1).astype(F32)
    from_band = lax.ppermute(low.astype(BF), "lat", [(lats - 1, lats - 2)]).astype(F32)
    own = own + from_band
    own = own.at[:2].add(from_south).at[-2:].add(from_north)
    own = own.astype(BF).reshape(half, 2 * flux_chans)
    flux_grad = jnp.concatenate([own[:, :flux_chans], own[:, flux_chans:]], 0)
    grad_project = jnp.einsum("nc,nf->fc", atmos_act, flux_grad, preferred_element_type=F32)
    act_grad = lax.dot_general(flux_grad, flux_project, dims, preferred_element_type=F32)
    atmos_delta = (act_grad * silu_slope(atmos_pre)).astype(BF)
    grad_atmos = kernel_grads(atmos_padded, atmos_delta, row_count, col_count)
    grad_ocean, grad_inject = reduce_pair(grad_ocean, grad_inject)
    grad_atmos, grad_project = reduce_pair(grad_atmos, grad_project)
    return (ocean_out, grad_atmos, grad_ocean, grad_project.T, grad_inject)


def solution(mesh):
    return jax.shard_map(
        body,
        mesh=mesh,
        in_specs=(
            P("lat", "lon", None),
            P(),
            P(),
            P("lat", "lon", None),
            P("lat", "lon", None),
            P("lat", "lon", None),
            P("lat", "lon", None),
            P(),
            P("lat", "lon"),
            P(),
            P("lat", "lon", None),
        ),
        out_specs=(P("lat", "lon", None), P(), P(), P(), P()),
        check_vma=False,
    )
```

```python
import jax
import jax.numpy as jnp
from jax import lax
from jax.experimental import pallas as pl
from jax.experimental.pallas import tpu as pltpu
from jax.sharding import PartitionSpec as P

BF = jnp.bfloat16
F32 = jnp.float32
VLIM = 56 << 20
AXES = ("lon", "lat")
NEAR = 72
BAND = 192


def passed_along(x, axis, by):
    length = lax.axis_size(axis)
    pairs = [(i, i + by) for i in range(length) if 0 <= i + by < length]
    return lax.ppermute(x, axis, pairs)


def shifted(x, axis, by):
    length = lax.axis_size(axis)
    return lax.ppermute(x, axis, [(i, (i + by) % length) for i in range(length)])


def mirror_row(edge_row):
    length = lax.axis_size("lon")
    moved = lax.ppermute(edge_row, "lon", [(i, length - 1 - i) for i in range(length)])
    return moved[:, ::-1]


def sigmoid(value):
    return 1.0 / (1.0 + jnp.exp(-value))


def silu_slope(value, sigma):
    return sigma * (1.0 + value * (1.0 - sigma))


VMEM = pl.BlockSpec(memory_space=pltpu.VMEM)
SMEM = pl.BlockSpec(memory_space=pltpu.SMEM)
PARAMS = pltpu.CompilerParams(vmem_limit_bytes=VLIM)
GRAD_ROWS = 2432


def call(kernel, name, outs, ins, scratch=()):
    specs = [SMEM if x.dtype == jnp.int32 and x.ndim <= 2 and x.shape[-1] in (1, 64) and x.shape[0] in (1, 128) else VMEM for x in ins]
    return pl.pallas_call(
        kernel,
        name=name,
        out_shape=tuple(jax.ShapeDtypeStruct(shape, kind) for shape, kind in outs),
        in_specs=specs,
        out_specs=(VMEM,) * len(outs),
        scratch_shapes=list(scratch),
        compiler_params=PARAMS,
    )(*ins)


def build_windows(dst, rows, row_of, west_of, east_of, first=0):
    at = lax.broadcasted_iota(jnp.int32, (64, 256), 0)
    for r in range(rows):
        value = row_of(r)
        wide = value.astype(F32)
        left = jnp.where(at == 0, west_of(r).astype(F32), pltpu.roll(wide, 1, 0))
        right = jnp.where(at == 63, east_of(r).astype(F32), pltpu.roll(wide, 63, 0))
        here = pl.ds((first + r) * 64, 64)
        dst[here, 0:256] = left.astype(BF)
        dst[here, 256:512] = value
        dst[here, 512:768] = right.astype(BF)


def conv_rows(windows, w, start, count):
    acc = jnp.dot(windows[start : start + count, :], w[0], preferred_element_type=F32)
    for r in (1, 2):
        acc += jnp.dot(windows[start + r * 64 : start + r * 64 + count, :], w[r], preferred_element_type=F32)
    return acc


def dot_rows(a, b):
    return lax.dot_general(a, b, (((0,), (0,)), ((), ())), preferred_element_type=F32)


def edges_kernel(a_ref, c_ref, m_ref, low_ref, high_ref, cols_ref, cols):
    land = m_ref[...].astype(F32).T
    for r in range(32):
        a = a_ref[r].astype(F32)
        c = c_ref[r].astype(F32) * land[:, r : r + 1]
        if r == 0:
            low_ref[0], low_ref[1] = a_ref[r], c.astype(BF)
        if r == 31:
            high_ref[0], high_ref[1] = a_ref[r], c.astype(BF)
        cols[0, r : r + 1, :] = a[0:1]
        cols[1, r : r + 1, :] = c[0:1]
        cols[2, r : r + 1, :] = a[63:64]
        cols[3, r : r + 1, :] = c[63:64]
    cols_ref[...] = cols[...].astype(BF)


def atmos_kernel(x_ref, s_ref, n_ref, we_ref, ea_ref, w_ref, p_ref, act_ref, slope_ref, own_ref, windows):
    build_windows(
        windows,
        34,
        lambda r: s_ref[...] if r == 0 else (n_ref[...] if r == 33 else x_ref[r - 1]),
        lambda r: we_ref[r : r + 1, :],
        lambda r: ea_ref[r : r + 1, :],
    )
    for b in range(2):
        packed = jnp.zeros((512, 128), F32)
        for h in range(2):
            start = h * 1024 + b * 512
            pre = conv_rows(windows, w_ref, start, 512)
            sigma = sigmoid(pre)
            act = (pre * sigma).astype(BF)
            act_ref[start : start + 512, :] = act
            slope_ref[start : start + 512, :] = silu_slope(pre, sigma).astype(BF)
            packed += jnp.dot(act, p_ref[h], preferred_element_type=F32)
        own_ref[b * 512 : b * 512 + 512, :] = packed.astype(BF)


def ocean_kernel(
    top_ref, x_ref, s_ref, n_ref, cols_ref, we_ref, ea_ref, c_ref, cs_ref, cn_ref, cw_ref, ce_ref, m_ref, rem_ref,
    w_ref, wn_ref, wt_ref, wtn_ref, inj_ref, out_ref, remap_ref, grads_ref,
    windows, sides, north, deltas, dwin, dsides, back,
):
    land = m_ref[...].astype(F32).T
    build_windows(
        windows,
        36,
        lambda r: s_ref[r] if r < 2 else (n_ref[r - 34] if r >= 34 else x_ref[r - 2]),
        lambda r: we_ref[1, r : r + 1, :],
        lambda r: ea_ref[0, r : r + 1, :],
    )
    sides[...] = jnp.zeros_like(sides)
    for side, columns in ((0, (we_ref[0], we_ref[1], cols_ref[0])), (1, (cols_ref[3], ea_ref[0], ea_ref[1]))):
        for q in range(3):
            sides[side, 0:36, q * 256 : q * 256 + 256] = columns[q].astype(F32)

    def side_rows(start, count):
        return jnp.concatenate([sides[0, start : start + count, :], sides[1, start : start + count, :]], 0).astype(BF)

    pre = jnp.zeros((80, 256), F32)
    for r in range(3):
        lhs = jnp.concatenate([windows[(33 + r - 0) * 64 : (34 + r) * 64, :], side_rows(33 + r, 8)], 0)
        pre += jnp.dot(lhs, wn_ref[r], preferred_element_type=F32)
    slope = silu_slope(pre, sigmoid(pre))
    d_north = (cn_ref[...].astype(F32) * slope[0:64]).astype(BF)
    side_pre = jnp.zeros((80, 256), F32)
    for r in range(3):
        side_pre += jnp.dot(side_rows(r, 40), w_ref[r], preferred_element_type=F32)
    side_slope = silu_slope(side_pre, sigmoid(side_pre))
    at = lax.broadcasted_iota(jnp.int32, (40, 256), 0)
    for side, cot in ((0, cw_ref), (1, ce_ref)):
        corner = slope[64 + side * 8 : 65 + side * 8]
        here = jnp.where(at == 33, corner, side_slope[side * 40 : side * 40 + 40])
        dsides[side] = jnp.zeros((40, 256), F32)
        dsides[side, 0:34, :] = cot[...].astype(F32) * here[0:34]
    pre = conv_rows(windows, w_ref, 0, 64)
    d_south = (cs_ref[...].astype(F32) * silu_slope(pre, sigmoid(pre))).astype(BF)
    for b in range(4):
        pre = conv_rows(windows, w_ref, 64 + b * 512, 512)
        sigma = sigmoid(pre)
        act = pre * sigma
        slope = silu_slope(pre, sigma)
        for u in range(8):
            r = b * 8 + u
            here = slice(u * 64, u * 64 + 64)
            wet = land[:, r : r + 1]
            out_ref[r] = (wet * act[here]).astype(BF)
            deltas[r * 64 : r * 64 + 64, :] = (c_ref[r].astype(F32) * wet * slope[here]).astype(BF)
    dry = jnp.zeros((64, 256), BF)
    build_windows(
        dwin,
        34,
        lambda r: d_south if r == 0 else (dry if r == 33 else deltas[r * 64 - 64 : r * 64, :]),
        lambda r: dsides[0, r : r + 1, :] if r < 33 else dry[0:1],
        lambda r: dsides[1, r : r + 1, :] if r < 33 else dry[0:1],
    )
    build_windows(north, 1, lambda r: d_north, lambda r: dsides[0, 33:34, :], lambda r: dsides[1, 33:34, :])
    beyond = jnp.dot(north[...], wtn_ref[...], preferred_element_type=F32)
    for b in range(4):
        total = conv_rows(dwin, wt_ref, b * 512, 512)
        for u in range(8):
            r = b * 8 + u
            value = total[u * 64 : u * 64 + 64]
            if r == 31:
                value = value + beyond
            back[r * 64 : r * 64 + 64, :] = (land[:, r : r + 1] * value).astype(BF)
        remap_ref[b * 512 : b * 512 + 512, :] = jnp.dot(
            back[b * 512 : b * 512 + 512, :], inj_ref[...], preferred_element_type=F32
        ).astype(BF)
    for r in range(3):
        grads_ref[r * 768 : r * 768 + 768, :] = dot_rows(windows[(r + 1) * 64 : (r + 1) * 64 + 2048, :], deltas[...])
    grads_ref[2304:2368, :] = dot_rows(rem_ref[...], back[...])[0:64]
    grads_ref[2368:2432, :] = jnp.zeros((64, 256), F32)


def atmos_back_kernel(x_ref, s_ref, n_ref, we_ref, ea_ref, act_ref, slope_ref, own_ref, p_ref, grads_ref, windows, deltas):
    build_windows(
        windows,
        34,
        lambda r: s_ref[...] if r == 0 else (n_ref[...] if r == 33 else x_ref[r - 1]),
        lambda r: we_ref[r : r + 1, :],
        lambda r: ea_ref[r : r + 1, :],
    )
    for h in range(2):
        here = slice(h * 1024, h * 1024 + 1024)
        back = jnp.dot(own_ref[...], p_ref[h], preferred_element_type=F32)
        deltas[here, :] = (back * slope_ref[here, :].astype(F32)).astype(BF)
    for r in range(3):
        grads_ref[r * 768 : r * 768 + 768, :] = dot_rows(windows[r * 64 : r * 64 + 2048, :], deltas[...])
    lower = dot_rows(own_ref[...], act_ref[0:1024, :])
    upper = dot_rows(own_ref[...], act_ref[1024:2048, :])
    grads_ref[2304:2368, :] = lower[0:64] + upper[64:128]
    grads_ref[2368:2432, :] = jnp.zeros((64, 256), F32)


def exchange(x, mask):
    count = lax.axis_size("lon") * lax.axis_size("lat")
    return lax.ppermute(x, AXES, [(i, i ^ mask) for i in range(count)])


def reduce_all(x):
    rank = lax.axis_index("lon") * lax.axis_size("lat") + lax.axis_index("lat")
    bit = lambda n: (rank >> n) & 1
    halving = [(1, bit(0)), (2, bit(1) ^ bit(2)), (8, bit(3) ^ bit(4)), (32, bit(5) ^ bit(6))]
    doubling = [6, 24, 96]
    v = x
    for mask, here in halving:
        half = v.shape[0] // 2
        keep = lax.dynamic_slice_in_dim(v, here * half, half)
        send = lax.dynamic_slice_in_dim(v, (1 - here) * half, half).astype(BF)
        v = keep + exchange(send, mask).astype(F32)
    for mask in doubling:
        mine = v.astype(BF)
        v = mine.astype(F32) + exchange(mine, mask).astype(F32)
    v = v.astype(BF)
    for mask, here in halving[::-1]:
        other = exchange(v, mask)
        v = jnp.where(here == 0, jnp.concatenate([v, other]), jnp.concatenate([other, v]))
    return v.astype(F32)


def lane_sign():
    lane = lax.broadcasted_iota(jnp.int32, (64, 128), 1)
    return jnp.where(lane < 64, jnp.float32(1.0), jnp.float32(-1.0))


def gather_kernel(
    top_ref, slot_ref, w_ref, ext_ref, halo_ref, low_ref, own_ref, west_ref, east_ref, o_ref, m_ref, inj_ref,
    out_ref, mixed_ref, cols_ref, table, picked, cols,
):
    top = top_ref[0]

    @pl.when(top == 0)
    def _():
        for r in range(20):
            table[r * NEAR : r * NEAR + 64, :] = ext_ref[r].astype(F32)
            table[r * NEAR + 64 : r * NEAR + 72, :] = halo_ref[r].astype(F32)

    @pl.when(top != 0)
    def _():
        for r in range(32):
            base = r * BAND
            table[base : base + 64, :] = (low_ref[r] if r < 16 else own_ref[r - 16]).astype(F32)
            table[base + 64 : base + 128, :] = west_ref[r].astype(F32)
            table[base + 128 : base + 192, :] = east_ref[r].astype(F32)

    def step(q, carry):
        base = pl.multiple_of(q * 64, 64)
        for u in range(64):
            at = slot_ref[q, u]
            picked[pl.ds(base + u, 1), :] = table[pl.ds(at, 1), :]
        return carry

    lax.fori_loop(0, 128, step, 0)
    sign = lane_sign()
    wt = w_ref[...].T
    for row in range(32):
        acc = jnp.zeros((64, 128), F32)
        for k in range(4):
            q = row * 4 + k
            factor = jnp.maximum(wt[:, q : q + 1] * sign, 0.0)
            acc = acc + factor * picked[q * 64 : q * 64 + 64, :]
        acc = acc + pltpu.roll(acc, 64, 1)
        out_ref[row * 64 : row * 64 + 64, :] = acc.astype(BF)
    land = m_ref[...].astype(F32).T
    for b in range(4):
        injected = jnp.dot(out_ref[b * 512 : b * 512 + 512, :], inj_ref[...], preferred_element_type=F32)
        for u in range(8):
            r = b * 8 + u
            value = land[:, r : r + 1] * (o_ref[r].astype(F32) + injected[u * 64 : u * 64 + 64])
            mixed_ref[r] = value.astype(BF)
            for c, i in enumerate((0, 1, 62, 63)):
                cols[c, r : r + 1, :] = value[i : i + 1]
    cols_ref[...] = cols[...].astype(BF)


def scatter_kernel(top_ref, slot_ref, w_ref, g_ref, ext_ref, halo_ref, low_ref, west_ref, east_ref, t0, t1, t2, t3, parts):
    top = top_ref[0]
    tables = (t0, t1, t2, t3)

    def clear(count):
        def one(i, carry):
            base = pl.multiple_of(i * 96, 96)
            for t in tables:
                t[pl.ds(base, 96), :] = jnp.zeros((96, 128), F32)
            return carry

        lax.fori_loop(0, count // 96, one, 0)

    @pl.when(top == 0)
    def _():
        clear(20 * NEAR)

    @pl.when(top != 0)
    def _():
        clear(32 * BAND)

    sign = lane_sign()
    wt = w_ref[...].T
    for row in range(32):
        g = g_ref[row * 64 : row * 64 + 64, :].astype(F32)
        for k in range(4):
            q = row * 4 + k
            parts[q * 64 : q * 64 + 64, :] = jnp.maximum(wt[:, q : q + 1] * sign, 0.0) * g

    def step(row, carry):
        base = pl.multiple_of(row * 256, 256)
        for u in range(64):
            for k in range(4):
                at = slot_ref[row * 4 + k, u]
                t = tables[k]
                t[pl.ds(at, 1), :] = t[pl.ds(at, 1), :] + parts[pl.ds(base + k * 64 + u, 1), :]
        return carry

    lax.fori_loop(0, 32, step, 0)

    def total(start, size):
        where = pl.ds(start, size)
        return ((t0[where, :] + t1[where, :]) + (t2[where, :] + t3[where, :])).astype(BF)

    @pl.when(top == 0)
    def _():
        for r in range(20):
            ext_ref[r] = total(r * NEAR, 64)
            halo_ref[r] = total(r * NEAR + 64, 8)
        for r in range(16):
            low_ref[r] = jnp.zeros((64, 128), BF)
        for r in range(32):
            west_ref[r] = jnp.zeros((64, 128), BF)
            east_ref[r] = jnp.zeros((64, 128), BF)

    @pl.when(top != 0)
    def _():
        for r in range(20):
            halo_ref[r] = jnp.zeros((8, 128), BF)
        for r in range(4):
            ext_ref[16 + r] = jnp.zeros((64, 128), BF)
        for r in range(32):
            base = r * BAND
            if r < 16:
                low_ref[r] = total(base, 64)
            else:
                ext_ref[r - 16] = total(base, 64)
            west_ref[r] = total(base + 64, 64)
            east_ref[r] = total(base + 128, 64)


def scatter_rows(top, slots, weights, grads):
    smem = pl.BlockSpec(memory_space=pltpu.SMEM)
    vmem = pl.BlockSpec(memory_space=pltpu.VMEM)
    struct = lambda *shape: jax.ShapeDtypeStruct(shape, BF)
    return pl.pallas_call(
        scatter_kernel,
        name="scatter_rows",
        out_shape=(struct(20, 64, 128), struct(20, 8, 128), struct(16, 64, 128), struct(32, 64, 128), struct(32, 64, 128)),
        in_specs=[smem, smem, vmem, vmem],
        out_specs=(vmem,) * 5,
        scratch_shapes=[pltpu.VMEM((32 * BAND, 128), F32)] * 4 + [pltpu.VMEM((8192, 128), F32)],
        compiler_params=pltpu.CompilerParams(vmem_limit_bytes=VLIM),
    )(top, slots, weights, grads)


def band_lon(x, by):
    lons, lats = lax.axis_size("lon"), lax.axis_size("lat")
    return lax.ppermute(x, AXES, [(i * lats + lats - 1, ((i + by) % lons) * lats + lats - 1) for i in range(lons)])


def entry_slots(source_row, source_col, weight, is_top, row_count, col_count):
    nx = col_count * lax.axis_size("lon")
    row = source_row - lax.axis_index("lat") * row_count
    col = jnp.remainder(source_col - lax.axis_index("lon") * col_count + nx // 2, nx) - nx // 2
    half = row_count // 2
    inside = (row >= 0) & (row < row_count)
    wrapped = row & (row_count - 1)
    packed = wrapped & (half - 1)
    upper = wrapped >= half
    near_row = jnp.where(inside, packed, jnp.where(row < 0, packed + 4, packed + half))
    near_col = jnp.where((col >= 0) & (col < col_count), col, jnp.where(col < 0, col + col_count + 2, col + 2))
    band_row = jnp.where(row >= 0, packed + half, packed)
    band_col = jnp.where((col >= 0) & (col < col_count), col, jnp.where(col < 0, col + 2 * col_count, col + col_count))
    slot = jnp.where(is_top, band_row * BAND + band_col, near_row * NEAR + near_col)
    signed = jnp.where(upper, -weight, weight)
    order = lambda x: jnp.transpose(x, (0, 2, 1)).reshape(-1, col_count)
    return order(slot), order(signed)


def body(
    atmos_state,
    atmos_weights,
    flux_project,
    source_row,
    source_col,
    intersection_weight,
    ocean_state,
    flux_inject,
    ocean_mask,
    ocean_weights,
    out_cotangent,
):
    row_count, col_count, chans = atmos_state.shape
    flux_chans = flux_project.shape[1]
    cells = row_count * col_count
    half = cells // 2
    lats = lax.axis_size("lat")
    is_top = lax.axis_index("lat") == lats - 1
    top = jnp.broadcast_to(is_top.astype(jnp.int32), (1,))
    low, high, cols = call(
        edges_kernel,
        "edges",
        (((2, 64, 256), BF), ((2, 64, 256), BF), ((4, 32, 256), BF)),
        (atmos_state, out_cotangent, ocean_mask),
        [pltpu.VMEM((4, 32, 256), F32)],
    )
    south = passed_along(high, "lat", 1)
    north = passed_along(low, "lat", -1)
    mirrored = mirror_row(high[1:])
    north = jnp.stack([north[0], jnp.where(is_top, mirrored[0], north[1])])
    ends = lambda x: jnp.stack([x[0, 0], x[1, 0], x[0, -1], x[1, -1]])[:, None]
    cols = jnp.concatenate([ends(south), cols, ends(north)], 1)
    west = shifted(cols[2:], "lon", 1)
    east = shifted(cols[:2], "lon", -1)
    slots, signed = entry_slots(source_row, source_col, intersection_weight, is_top, row_count, col_count)
    zeros = jnp.zeros_like(flux_project)
    project = jnp.stack([jnp.concatenate([flux_project, zeros], 1), jnp.concatenate([zeros, flux_project], 1)])
    project_back = jnp.transpose(project, (0, 2, 1))
    inject_pad = jnp.concatenate([flux_inject, jnp.zeros_like(flux_inject)], 0)
    inject_back = jnp.concatenate([flux_inject, flux_inject], 0).T
    atmos_w = atmos_weights.reshape(3, 3 * chans, chans)
    ocean_w = ocean_weights.reshape(3, 3 * chans, chans)
    turned = ocean_weights[::-1]
    north_w = jnp.where(is_top, turned, ocean_weights).reshape(3, 3 * chans, chans)
    back_w = jnp.transpose(turned, (0, 2, 1))
    ahead_w = jnp.transpose(ocean_weights[6:], (0, 2, 1))
    north_back_w = jnp.where(is_top, ahead_w, back_w[6:]).reshape(3 * chans, chans)
    back_w = back_w.reshape(3, 3 * chans, chans)
    act, slope, own = call(
        atmos_kernel,
        "atmos",
        (((cells, chans), BF), ((cells, chans), BF), ((half, 2 * flux_chans), BF)),
        (atmos_state, south[0], north[0], west[0], east[0], atmos_w, project),
        [pltpu.VMEM((34 * 64, 768), BF)],
    )
    own = own.reshape(row_count // 2, col_count, 2 * flux_chans)
    flux_south = passed_along(own[-2:], "lat", 1)
    flux_north = passed_along(own[:2], "lat", -1)
    low_tile = lax.ppermute(own, "lat", [(lats - 2, lats - 1)])
    two = jnp.concatenate([low_tile, own], 0)
    band_west = band_lon(two, 1)
    band_east = band_lon(two, -1)
    ext = jnp.concatenate([own, flux_north, flux_south], 0)
    flux_west = shifted(ext[:, -2:], "lon", 1)
    flux_east = shifted(ext[:, :2], "lon", -1)
    halo = jnp.concatenate([flux_west, flux_east, jnp.zeros((20, 4, 2 * flux_chans), BF)], 1)
    remapped, mixed, cols = call(
        gather_kernel,
        "gather_mix",
        (((cells, 128), BF), ((32, 64, 256), BF), ((4, 32, 256), BF)),
        (top, slots, signed, ext, halo, low_tile, own, band_west, band_east, ocean_state, ocean_mask, inject_pad),
        [pltpu.VMEM((32 * BAND, 128), F32), pltpu.VMEM((8192, 128), F32), pltpu.VMEM((4, 32, 256), F32)],
    )
    mixed_south = passed_along(mixed[-2:], "lat", 1)
    mixed_north = passed_along(mixed[:2], "lat", -1)
    mixed_north = jnp.where(is_top, mirror_row(mixed[-2:])[::-1], mixed_north)
    ends = lambda x: jnp.stack([x[:, 0], x[:, 1], x[:, -2], x[:, -1]])
    cols = jnp.concatenate([ends(mixed_south), cols, ends(mixed_north)], 1)
    mixed_west = shifted(cols[2:], "lon", 1)
    mixed_east = shifted(cols[:2], "lon", -1)
    ocean_out, remap_grad, ocean_grads = call(
        ocean_kernel,
        "ocean",
        (((32, 64, 256), BF), ((cells, 128), BF), ((GRAD_ROWS, chans), F32)),
        (
            top, mixed, mixed_south, mixed_north, cols, mixed_west, mixed_east,
            out_cotangent, south[1], north[1], west[1], east[1], ocean_mask, remapped,
            ocean_w, north_w, back_w, north_back_w, inject_back,
        ),
        [
            pltpu.VMEM((36 * 64, 768), BF),
            pltpu.VMEM((2, 48, 768), F32),
            pltpu.VMEM((64, 768), BF),
            pltpu.VMEM((cells, 256), BF),
            pltpu.VMEM((34 * 64, 768), BF),
            pltpu.VMEM((2, 40, 256), F32),
            pltpu.VMEM((cells, 256), BF),
        ],
    )
    ext, halo, low_tile, out_west, out_east = scatter_rows(top, slots, signed, remap_grad)
    from_east = shifted(halo[:, :2], "lon", -1).astype(F32)
    from_west = shifted(halo[:, 2:4], "lon", 1).astype(F32)
    band_from_east = band_lon(out_west, -1).astype(F32)
    band_from_west = band_lon(out_east, 1).astype(F32)
    ext = ext.astype(F32)
    ext = ext.at[:, -2:].add(from_east).at[:, :2].add(from_west)
    own = ext[:16] + band_from_east[16:] + band_from_west[16:]
    low_tile = low_tile.astype(F32) + band_from_east[:16] + band_from_west[:16]
    from_south = passed_along(ext[16:18].astype(BF), "lat", 1).astype(F32)
    from_north = passed_along(ext[18:20].astype(BF), "lat", -1).astype(F32)
    from_band = lax.ppermute(low_tile.astype(BF), "lat", [(lats - 1, lats - 2)]).astype(F32)
    own = own + from_band
    own = own.at[:2].add(from_south).at[-2:].add(from_north)
    own = own.astype(BF).reshape(half, 2 * flux_chans)
    (atmos_grads,) = call(
        atmos_back_kernel,
        "atmos_back",
        (((GRAD_ROWS, chans), F32),),
        (atmos_state, south[0], north[0], west[0], east[0], act, slope, own, project_back),
        [pltpu.VMEM((34 * 64, 768), BF), pltpu.VMEM((cells, 256), BF)],
    )
    ocean_grads = reduce_all(ocean_grads)
    atmos_grads = reduce_all(atmos_grads)
    split = lambda g: (g[: 9 * chans].reshape(9, chans, chans), g[9 * chans : 9 * chans + flux_chans])
    grad_ocean, grad_inject = split(ocean_grads)
    grad_atmos, grad_project = split(atmos_grads)
    return (ocean_out, grad_atmos, grad_ocean, grad_project.T, grad_inject)


def solution(mesh):
    return jax.shard_map(
        body,
        mesh=mesh,
        in_specs=(
            P("lat", "lon", None),
            P(),
            P(),
            P("lat", "lon", None),
            P("lat", "lon", None),
            P("lat", "lon", None),
            P("lat", "lon", None),
            P(),
            P("lat", "lon"),
            P(),
            P("lat", "lon", None),
        ),
        out_specs=(P("lat", "lon", None), P(), P(), P(), P()),
        check_vma=False,
    )
```

```python
import jax
import jax.numpy as jnp
from jax import lax
from jax.experimental import pallas as pl
from jax.experimental.pallas import tpu as pltpu
from jax.sharding import PartitionSpec as P

BF = jnp.bfloat16
F32 = jnp.float32
VLIM = 56 << 20
AXES = ("lon", "lat")
NEAR = 72
BAND = 192


def passed_along(x, axis, by):
    length = lax.axis_size(axis)
    pairs = [(i, i + by) for i in range(length) if 0 <= i + by < length]
    return lax.ppermute(x, axis, pairs)


def shifted(x, axis, by):
    length = lax.axis_size(axis)
    return lax.ppermute(x, axis, [(i, (i + by) % length) for i in range(length)])


def mirrored(x):
    lons, lats = lax.axis_size("lon"), lax.axis_size("lat")
    edge = lats - 1
    return lax.ppermute(x, AXES, [(i * lats + edge, (lons - 1 - i) * lats + edge) for i in range(lons)])


def lon_below_band(x, by):
    lons, lats = lax.axis_size("lon"), lax.axis_size("lat")
    return lax.ppermute(
        x, AXES, [(i * lats + j, ((i + by) % lons) * lats + j) for i in range(lons) for j in range(lats - 1)]
    )


def sigmoid(value):
    return 1.0 / (1.0 + jnp.exp(-value))


def silu_slope(value, sigma):
    return sigma * (1.0 + value * (1.0 - sigma))


VMEM = pl.BlockSpec(memory_space=pltpu.VMEM)
SMEM = pl.BlockSpec(memory_space=pltpu.SMEM)
PARAMS = pltpu.CompilerParams(vmem_limit_bytes=VLIM)
GRAD_ROWS = 2432


def call(kernel, name, outs, ins, scratch=(), scalars=0, specs=None, grid=None):
    if specs is None:
        specs = [SMEM] * scalars + [VMEM] * (len(ins) - scalars)
    extra = {} if grid is None else {"grid": grid}
    return pl.pallas_call(
        kernel,
        name=name,
        out_shape=tuple(jax.ShapeDtypeStruct(shape, kind) for shape, kind in outs),
        in_specs=specs,
        out_specs=(VMEM,) * len(outs),
        scratch_shapes=list(scratch),
        compiler_params=PARAMS,
        **extra,
    )(*ins)


def turned_row(row):
    a = lax.broadcasted_iota(jnp.int32, (64, 64), 0)
    b = lax.broadcasted_iota(jnp.int32, (64, 64), 1)
    flip = jnp.where(a + b == 63, jnp.float32(1.0), jnp.float32(0.0)).astype(BF)
    return jnp.dot(flip, row, preferred_element_type=F32)


def build_windows(dst, rows, row_of, west_of, east_of, first=0):
    at = lax.broadcasted_iota(jnp.int32, (64, 256), 0)
    for r in range(rows):
        value = row_of(r)
        wide = value.astype(F32)
        left = jnp.where(at == 0, west_of(r).astype(F32), pltpu.roll(wide, 1, 0))
        right = jnp.where(at == 63, east_of(r).astype(F32), pltpu.roll(wide, 63, 0))
        here = pl.ds((first + r) * 64, 64)
        dst[here, 0:256] = left.astype(BF)
        dst[here, 256:512] = value
        dst[here, 512:768] = right.astype(BF)


def conv_rows(windows, w, start, count):
    acc = jnp.dot(windows[start : start + count, :], w[0], preferred_element_type=F32)
    for r in (1, 2):
        acc += jnp.dot(windows[start + r * 64 : start + r * 64 + count, :], w[r], preferred_element_type=F32)
    return acc


def dot_rows(a, b):
    return lax.dot_general(a, b, (((0,), (0,)), ((), ())), preferred_element_type=F32)


def edges_kernel(
    top_ref, a0_ref, a1_ref, c0_ref, c1_ref, m_ref, s_ref, n_ref, mir_ref, cols_ref, cn_ref, cols
):
    top = top_ref[0] != 0
    land = m_ref[...].astype(F32).T
    for r in range(32):
        here = slice(r + 1, r + 2)
        cols[0, here, :] = a0_ref[r, 0:1].astype(F32)
        cols[1, here, :] = c0_ref[r, 0:1].astype(F32) * land[0:1, r : r + 1]
        cols[2, here, :] = a1_ref[r, 15:16].astype(F32)
        cols[3, here, :] = c1_ref[r, 15:16].astype(F32) * land[63:64, r : r + 1]
    cn = jnp.where(top, turned_row(mir_ref[...]), n_ref[1].astype(F32))
    cn_ref[...] = cn.astype(BF)
    for k, (row, i) in enumerate(((s_ref[0], 0), (s_ref[1], 0), (s_ref[0], 63), (s_ref[1], 63))):
        cols[k, 0:1, :] = row[i : i + 1].astype(F32)
    north = n_ref[0].astype(F32)
    for k, (row, i) in enumerate(((north, 0), (cn, 0), (north, 63), (cn, 63))):
        cols[k, 33:34, :] = row[i : i + 1]
    cols_ref[...] = cols[...].astype(BF)


def mixed_edges_kernel(top_ref, cols_in, s_ref, n_ref, mir_ref, cols_ref, north_ref, cols):
    top = top_ref[0] != 0
    for r in range(2):
        s = s_ref[r].astype(F32)
        n = jnp.where(top, turned_row(mir_ref[1 - r]), n_ref[r].astype(F32))
        north_ref[r] = n.astype(BF)
        for k, i in enumerate((0, 1, 62, 63)):
            cols[k, r : r + 1, :] = s[i : i + 1]
            cols[k, 34 + r : 35 + r, :] = n[i : i + 1]
    for k in range(4):
        cols[k, 2:34, :] = cols_in[k].astype(F32)
    cols_ref[...] = cols[...].astype(BF)


def atmos_kernel(x_ref, s_ref, n_ref, we_ref, ea_ref, w_ref, p_ref, act_ref, slope_ref, own_ref, windows):
    build_windows(
        windows,
        34,
        lambda r: s_ref[...] if r == 0 else (n_ref[...] if r == 33 else x_ref[r - 1]),
        lambda r: we_ref[r : r + 1, :],
        lambda r: ea_ref[r : r + 1, :],
    )
    for b in range(2):
        packed = jnp.zeros((512, 128), F32)
        for h in range(2):
            start = h * 1024 + b * 512
            pre = conv_rows(windows, w_ref, start, 512)
            sigma = sigmoid(pre)
            act = (pre * sigma).astype(BF)
            act_ref[start : start + 512, :] = act
            slope_ref[start : start + 512, :] = silu_slope(pre, sigma).astype(BF)
            packed += jnp.dot(act, p_ref[h], preferred_element_type=F32)
        own_ref[b * 512 : b * 512 + 512, :] = packed.astype(BF)


def ocean_kernel(
    x_ref, s_ref, n_ref, cols_ref, we_ref, ea_ref, c_ref, cs_ref, cn_ref, cw_ref, ce_ref, m_ref, rem_ref,
    w_ref, wn_ref, wt_ref, wtn_ref, inj_ref, out_ref, remap_ref, grads_ref,
    windows, sides, north, deltas, dwin, dsides, back,
):
    land = m_ref[...].astype(F32).T
    build_windows(
        windows,
        36,
        lambda r: s_ref[r] if r < 2 else (n_ref[r - 34] if r >= 34 else x_ref[r - 2]),
        lambda r: we_ref[1, r : r + 1, :],
        lambda r: ea_ref[0, r : r + 1, :],
    )
    sides[...] = jnp.zeros_like(sides)
    for side, columns in ((0, (we_ref[0], we_ref[1], cols_ref[0])), (1, (cols_ref[3], ea_ref[0], ea_ref[1]))):
        for q in range(3):
            sides[side, 0:36, q * 256 : q * 256 + 256] = columns[q].astype(F32)

    def side_rows(start, count):
        return jnp.concatenate([sides[0, start : start + count, :], sides[1, start : start + count, :]], 0).astype(BF)

    pre = jnp.zeros((80, 256), F32)
    for r in range(3):
        lhs = jnp.concatenate([windows[(33 + r) * 64 : (34 + r) * 64, :], side_rows(33 + r, 8)], 0)
        pre += jnp.dot(lhs, wn_ref[r], preferred_element_type=F32)
    slope = silu_slope(pre, sigmoid(pre))
    d_north = (cn_ref[...].astype(F32) * slope[0:64]).astype(BF)
    side_pre = jnp.zeros((80, 256), F32)
    for r in range(3):
        side_pre += jnp.dot(side_rows(r, 40), w_ref[r], preferred_element_type=F32)
    side_slope = silu_slope(side_pre, sigmoid(side_pre))
    at = lax.broadcasted_iota(jnp.int32, (40, 256), 0)
    for side, cot in ((0, cw_ref), (1, ce_ref)):
        corner = slope[64 + side * 8 : 65 + side * 8]
        here = jnp.where(at == 33, corner, side_slope[side * 40 : side * 40 + 40])
        dsides[side] = jnp.zeros((40, 256), F32)
        dsides[side, 0:34, :] = cot[...].astype(F32) * here[0:34]
    pre = conv_rows(windows, w_ref, 0, 64)
    d_south = (cs_ref[...].astype(F32) * silu_slope(pre, sigmoid(pre))).astype(BF)
    for b in range(4):
        pre = conv_rows(windows, w_ref, 64 + b * 512, 512)
        sigma = sigmoid(pre)
        act = pre * sigma
        slope = silu_slope(pre, sigma)
        for u in range(8):
            r = b * 8 + u
            here = slice(u * 64, u * 64 + 64)
            wet = land[:, r : r + 1]
            out_ref[r] = (wet * act[here]).astype(BF)
            deltas[r * 64 : r * 64 + 64, :] = (c_ref[r].astype(F32) * wet * slope[here]).astype(BF)
    dry = jnp.zeros((64, 256), BF)
    build_windows(
        dwin,
        34,
        lambda r: d_south if r == 0 else (dry if r == 33 else deltas[r * 64 - 64 : r * 64, :]),
        lambda r: dsides[0, r : r + 1, :] if r < 33 else dry[0:1],
        lambda r: dsides[1, r : r + 1, :] if r < 33 else dry[0:1],
    )
    build_windows(north, 1, lambda r: d_north, lambda r: dsides[0, 33:34, :], lambda r: dsides[1, 33:34, :])
    beyond = jnp.dot(north[...], wtn_ref[...], preferred_element_type=F32)
    for b in range(4):
        total = conv_rows(dwin, wt_ref, b * 512, 512)
        for u in range(8):
            r = b * 8 + u
            value = total[u * 64 : u * 64 + 64]
            if r == 31:
                value = value + beyond
            back[r * 64 : r * 64 + 64, :] = (land[:, r : r + 1] * value).astype(BF)
        remap_ref[b * 512 : b * 512 + 512, :] = jnp.dot(
            back[b * 512 : b * 512 + 512, :], inj_ref[...], preferred_element_type=F32
        ).astype(BF)
    for r in range(3):
        grads_ref[r * 768 : r * 768 + 768, :] = dot_rows(windows[(r + 1) * 64 : (r + 1) * 64 + 2048, :], deltas[...])
    grads_ref[2304:2368, :] = dot_rows(rem_ref[...], back[...])[0:64]
    grads_ref[2368:2432, :] = jnp.zeros((64, 256), F32)


def credit_rows_kernel(n_ref, s_ref, e_ref, w_ref, n_out, s_out):
    for r in range(2):
        for src, dst, first in ((n_ref, n_out, 16), (s_ref, s_out, 18)):
            dst[r] = src[r]
            dst[r, 0:2] = (src[r, 0:2].astype(F32) + w_ref[first + r].astype(F32)).astype(BF)
            dst[r, 62:64] = (src[r, 62:64].astype(F32) + e_ref[first + r].astype(F32)).astype(BF)


def atmos_back_kernel(
    x_ref, s_ref, n_ref, we_ref, ea_ref, act_ref, slope_ref, own_ref, cw_ref, ce_ref, cs_ref, cn_ref, bw_ref, be_ref,
    low_ref, p_ref, grads_ref, windows, deltas, total, credit,
):
    build_windows(
        windows,
        34,
        lambda r: s_ref[...] if r == 0 else (n_ref[...] if r == 33 else x_ref[r - 1]),
        lambda r: we_ref[r : r + 1, :],
        lambda r: ea_ref[r : r + 1, :],
    )
    for r in range(16):
        value = own_ref[r].astype(F32) + bw_ref[16 + r].astype(F32) + be_ref[16 + r].astype(F32) + low_ref[r].astype(F32)
        if r < 2:
            value += cs_ref[r].astype(F32)
        if r >= 14:
            value += cn_ref[r - 14].astype(F32)
        total[...] = value
        total[0:2, :] += cw_ref[r].astype(F32)
        total[62:64, :] += ce_ref[r].astype(F32)
        credit[r * 64 : r * 64 + 64, :] = total[...].astype(BF)
    for h in range(2):
        here = slice(h * 1024, h * 1024 + 1024)
        back = jnp.dot(credit[...], p_ref[h], preferred_element_type=F32)
        deltas[here, :] = (back * slope_ref[here, :].astype(F32)).astype(BF)
    for r in range(3):
        grads_ref[r * 768 : r * 768 + 768, :] = dot_rows(windows[r * 64 : r * 64 + 2048, :], deltas[...])
    lower = dot_rows(credit[...], act_ref[0:1024, :])
    upper = dot_rows(credit[...], act_ref[1024:2048, :])
    grads_ref[2304:2368, :] = lower[0:64] + upper[64:128]
    grads_ref[2368:2432, :] = jnp.zeros((64, 256), F32)


def exchange(x, mask):
    count = lax.axis_size("lon") * lax.axis_size("lat")
    return lax.ppermute(x, AXES, [(i, i ^ mask) for i in range(count)])


def reduce_all(x, order):
    rank = lax.axis_index("lon") * lax.axis_size("lat") + lax.axis_index("lat")
    bit = lambda n: (rank >> n) & 1
    axes = [(2, bit(1) ^ bit(2)), (8, bit(3) ^ bit(4)), (32, bit(5) ^ bit(6))]
    halving = [(1, bit(0))] + [axes[i] for i in order]
    doubling = [(6, 24, 96)[i] for i in order]
    v = x
    for mask, here in halving:
        half = v.shape[0] // 2
        keep = lax.dynamic_slice_in_dim(v, here * half, half)
        send = lax.dynamic_slice_in_dim(v, (1 - here) * half, half).astype(BF)
        v = keep + exchange(send, mask).astype(F32)
    for mask in doubling:
        mine = v.astype(BF)
        v = mine.astype(F32) + exchange(mine, mask).astype(F32)
    v = v.astype(BF)
    for mask, here in halving[::-1]:
        other = exchange(v, mask)
        v = jnp.where(here == 0, jnp.concatenate([v, other]), jnp.concatenate([other, v]))
    return v.astype(F32)


def lane_sign():
    lane = lax.broadcasted_iota(jnp.int32, (64, 128), 1)
    return jnp.where(lane < 64, jnp.float32(1.0), jnp.float32(-1.0))


def gather_kernel(
    top_ref, slot_ref, w_ref, fn_ref, fs_ref, fw_ref, fe_ref, low_ref, own_ref, west_ref, east_ref, o_ref, m_ref, inj_ref,
    out_ref, mixed_ref, cols_ref, table, picked, cols,
):
    top = top_ref[0]

    @pl.when(top == 0)
    def _():
        for r in range(20):
            rows = own_ref[r] if r < 16 else (fn_ref[r - 16] if r < 18 else fs_ref[r - 18])
            table[r * NEAR : r * NEAR + 64, :] = rows.astype(F32)
            table[r * NEAR + 64 : r * NEAR + 66, :] = fw_ref[r].astype(F32)
            table[r * NEAR + 66 : r * NEAR + 68, :] = fe_ref[r].astype(F32)

    @pl.when(top != 0)
    def _():
        for r in range(32):
            base = r * BAND
            table[base : base + 64, :] = (low_ref[r] if r < 16 else own_ref[r - 16]).astype(F32)
            table[base + 64 : base + 128, :] = west_ref[r].astype(F32)
            table[base + 128 : base + 192, :] = east_ref[r].astype(F32)

    def step(q, carry):
        base = pl.multiple_of(q * 64, 64)
        for u in range(64):
            at = slot_ref[q, u]
            picked[pl.ds(base + u, 1), :] = table[pl.ds(at, 1), :]
        return carry

    lax.fori_loop(0, 128, step, 0)
    sign = lane_sign()
    wt = w_ref[...].T
    for row in range(32):
        acc = jnp.zeros((64, 128), F32)
        for k in range(4):
            q = row * 4 + k
            factor = jnp.maximum(wt[:, q : q + 1] * sign, 0.0)
            acc = acc + factor * picked[q * 64 : q * 64 + 64, :]
        acc = acc + pltpu.roll(acc, 64, 1)
        out_ref[row * 64 : row * 64 + 64, :] = acc.astype(BF)
    land = m_ref[...].astype(F32).T
    for b in range(4):
        injected = jnp.dot(out_ref[b * 512 : b * 512 + 512, :], inj_ref[...], preferred_element_type=F32)
        for u in range(8):
            r = b * 8 + u
            value = land[:, r : r + 1] * (o_ref[r].astype(F32) + injected[u * 64 : u * 64 + 64])
            mixed_ref[r] = value.astype(BF)
            for c, i in enumerate((0, 1, 62, 63)):
                cols[c, r : r + 1, :] = value[i : i + 1]
    cols_ref[...] = cols[...].astype(BF)


def scatter_kernel(
    top_ref, slot_ref, w_ref, g_ref, own_ref, n_ref, s_ref, w_out, e_out, low_ref, west_ref, east_ref, t0, t1, t2, t3, parts
):
    top = top_ref[0]
    tables = (t0, t1, t2, t3)

    def clear(count):
        def one(i, carry):
            base = pl.multiple_of(i * 96, 96)
            for t in tables:
                t[pl.ds(base, 96), :] = jnp.zeros((96, 128), F32)
            return carry

        lax.fori_loop(0, count // 96, one, 0)

    @pl.when(top == 0)
    def _():
        clear(20 * NEAR)

    @pl.when(top != 0)
    def _():
        clear(32 * BAND)

    sign = lane_sign()
    wt = w_ref[...].T
    for row in range(32):
        g = g_ref[row * 64 : row * 64 + 64, :].astype(F32)
        for k in range(4):
            q = row * 4 + k
            parts[q * 64 : q * 64 + 64, :] = jnp.maximum(wt[:, q : q + 1] * sign, 0.0) * g

    def step(row, carry):
        base = pl.multiple_of(row * 256, 256)
        for u in range(64):
            for k in range(4):
                at = slot_ref[row * 4 + k, u]
                t = tables[k]
                t[pl.ds(at, 1), :] = t[pl.ds(at, 1), :] + parts[pl.ds(base + k * 64 + u, 1), :]
        return carry

    lax.fori_loop(0, 32, step, 0)

    def total(start, size):
        where = pl.ds(start, size)
        return ((t0[where, :] + t1[where, :]) + (t2[where, :] + t3[where, :])).astype(BF)

    @pl.when(top == 0)
    def _():
        for r in range(20):
            rows = total(r * NEAR, 64)
            if r < 16:
                own_ref[r] = rows
            elif r < 18:
                n_ref[r - 16] = rows
            else:
                s_ref[r - 18] = rows
            w_out[r] = total(r * NEAR + 64, 2)
            e_out[r] = total(r * NEAR + 66, 2)

    @pl.when(top != 0)
    def _():
        for r in range(2):
            n_ref[r] = jnp.zeros((64, 128), BF)
            s_ref[r] = jnp.zeros((64, 128), BF)
        w_out[...] = jnp.zeros_like(w_out)
        e_out[...] = jnp.zeros_like(e_out)
        for r in range(32):
            base = r * BAND
            if r < 16:
                low_ref[r] = total(base, 64)
            else:
                own_ref[r - 16] = total(base, 64)
            west_ref[r] = total(base + 64, 64)
            east_ref[r] = total(base + 128, 64)


def band_lon(x, by):
    lons, lats = lax.axis_size("lon"), lax.axis_size("lat")
    return lax.ppermute(x, AXES, [(i * lats + lats - 1, ((i + by) % lons) * lats + lats - 1) for i in range(lons)])


def entry_slots(source_row, source_col, weight, is_top, row_count, col_count):
    nx = col_count * lax.axis_size("lon")
    row = source_row - lax.axis_index("lat") * row_count
    col = jnp.remainder(source_col - lax.axis_index("lon") * col_count + nx // 2, nx) - nx // 2
    half = row_count // 2
    inside = (row >= 0) & (row < row_count)
    wrapped = row & (row_count - 1)
    packed = wrapped & (half - 1)
    upper = wrapped >= half
    near_row = jnp.where(inside, packed, jnp.where(row < 0, packed + 4, packed + half))
    near_col = jnp.where((col >= 0) & (col < col_count), col, jnp.where(col < 0, col + col_count + 2, col + 2))
    band_row = jnp.where(row >= 0, packed + half, packed)
    band_col = jnp.where((col >= 0) & (col < col_count), col, jnp.where(col < 0, col + 2 * col_count, col + col_count))
    slot = jnp.where(is_top, band_row * BAND + band_col, near_row * NEAR + near_col)
    signed = jnp.where(upper, -weight, weight)
    order = lambda x: jnp.transpose(x, (0, 2, 1)).reshape(-1, col_count)
    return order(slot), order(signed)


def body(
    atmos_state,
    atmos_weights,
    flux_project,
    source_row,
    source_col,
    intersection_weight,
    ocean_state,
    flux_inject,
    ocean_mask,
    ocean_weights,
    out_cotangent,
):
    row_count, col_count, chans = atmos_state.shape
    flux_chans = flux_project.shape[1]
    cells = row_count * col_count
    half = cells // 2
    lats = lax.axis_size("lat")
    is_top = lax.axis_index("lat") == lats - 1
    top = jnp.broadcast_to(is_top.astype(jnp.int32), (1,))
    wet = ocean_mask.astype(BF)[..., None]
    south = passed_along(jnp.stack([atmos_state[-1], out_cotangent[-1] * wet[-1]]), "lat", 1)
    north = passed_along(jnp.stack([atmos_state[0], out_cotangent[0] * wet[0]]), "lat", -1)
    mirror = mirrored(out_cotangent[-1] * wet[-1])
    left = pl.BlockSpec((32, 16, 256), lambda i: (0, 0, 0))
    right = pl.BlockSpec((32, 16, 256), lambda i: (0, 3, 0))
    cols, cot_north = call(
        edges_kernel,
        "edges",
        (((4, 34, 256), BF), ((64, 256), BF)),
        (top, atmos_state, atmos_state, out_cotangent, out_cotangent, ocean_mask, south, north, mirror),
        [pltpu.VMEM((4, 34, 256), F32)],
        specs=[SMEM, left, right, left, right] + [VMEM] * 4,
        grid=(1,),
    )
    west = shifted(cols[2:], "lon", 1)
    east = shifted(cols[:2], "lon", -1)
    slots, signed = entry_slots(source_row, source_col, intersection_weight, is_top, row_count, col_count)
    zeros = jnp.zeros_like(flux_project)
    project = jnp.stack([jnp.concatenate([flux_project, zeros], 1), jnp.concatenate([zeros, flux_project], 1)])
    project_back = jnp.transpose(project, (0, 2, 1))
    inject_pad = jnp.concatenate([flux_inject, jnp.zeros_like(flux_inject)], 0)
    inject_back = jnp.concatenate([flux_inject, flux_inject], 0).T
    atmos_w = atmos_weights.reshape(3, 3 * chans, chans)
    ocean_w = ocean_weights.reshape(3, 3 * chans, chans)
    turned = ocean_weights[::-1]
    north_w = jnp.where(is_top, turned, ocean_weights).reshape(3, 3 * chans, chans)
    back_w = jnp.transpose(turned, (0, 2, 1))
    ahead_w = jnp.transpose(ocean_weights[6:], (0, 2, 1))
    north_back_w = jnp.where(is_top, ahead_w, back_w[6:]).reshape(3 * chans, chans)
    back_w = back_w.reshape(3, 3 * chans, chans)
    act, slope, own = call(
        atmos_kernel,
        "atmos",
        (((cells, chans), BF), ((cells, chans), BF), ((half, 2 * flux_chans), BF)),
        (atmos_state, south[0], north[0], west[0], east[0], atmos_w, project),
        [pltpu.VMEM((34 * 64, 768), BF)],
    )
    own = own.reshape(row_count // 2, col_count, 2 * flux_chans)
    low_tile = lax.ppermute(own, "lat", [(lats - 2, lats - 1)])
    flux_south = lax.ppermute(own[-2:], "lat", [(i, i + 1) for i in range(lats - 2)])
    flux_north = passed_along(own[:2], "lat", -1)
    two = jnp.concatenate([low_tile, own], 0)
    band_west = band_lon(two, 1)
    band_east = band_lon(two, -1)
    side = lambda at: jnp.concatenate([own[:, at], flux_north[:, at], flux_south[:, at]], 0)
    flux_west = lon_below_band(side(slice(-2, None)), 1)
    flux_east = lon_below_band(side(slice(0, 2)), -1)
    remapped, mixed, cols = call(
        gather_kernel,
        "gather_mix",
        (((cells, 128), BF), ((32, 64, 256), BF), ((4, 32, 256), BF)),
        (top, slots, signed, flux_north, flux_south, flux_west, flux_east, low_tile, own, band_west, band_east,
         ocean_state, ocean_mask, inject_pad),
        [pltpu.VMEM((32 * BAND, 128), F32), pltpu.VMEM((8192, 128), F32), pltpu.VMEM((4, 32, 256), F32)],
        scalars=2,
    )
    mixed_south = passed_along(mixed[-2:], "lat", 1)
    mixed_north = passed_along(mixed[:2], "lat", -1)
    mirror = mirrored(mixed[-2:])
    cols, mixed_north = call(
        mixed_edges_kernel,
        "mixed_edges",
        (((4, 36, 256), BF), ((2, 64, 256), BF)),
        (top, cols, mixed_south, mixed_north, mirror),
        [pltpu.VMEM((4, 36, 256), F32)],
        scalars=1,
    )
    mixed_west = shifted(cols[2:], "lon", 1)
    mixed_east = shifted(cols[:2], "lon", -1)
    ocean_out, remap_grad, ocean_grads = call(
        ocean_kernel,
        "ocean",
        (((32, 64, 256), BF), ((cells, 128), BF), ((GRAD_ROWS, chans), F32)),
        (
            mixed, mixed_south, mixed_north, cols, mixed_west, mixed_east,
            out_cotangent, south[1], cot_north, west[1], east[1], ocean_mask, remapped,
            ocean_w, north_w, back_w, north_back_w, inject_back,
        ),
        [
            pltpu.VMEM((36 * 64, 768), BF),
            pltpu.VMEM((2, 48, 768), F32),
            pltpu.VMEM((64, 768), BF),
            pltpu.VMEM((cells, 256), BF),
            pltpu.VMEM((34 * 64, 768), BF),
            pltpu.VMEM((2, 40, 256), F32),
            pltpu.VMEM((cells, 256), BF),
        ],
    )
    struct = lambda *shape: (shape, BF)
    own, to_north, to_south, to_west, to_east, low_tile, band_west, band_east = call(
        scatter_kernel,
        "scatter_rows",
        (struct(16, 64, 128), struct(2, 64, 128), struct(2, 64, 128), struct(20, 2, 128), struct(20, 2, 128),
         struct(16, 64, 128), struct(32, 64, 128), struct(32, 64, 128)),
        (top, slots, signed, remap_grad),
        [pltpu.VMEM((32 * BAND, 128), F32)] * 4 + [pltpu.VMEM((8192, 128), F32)],
        scalars=2,
    )
    band_from_east = band_lon(band_west, -1)
    band_from_west = band_lon(band_east, 1)
    from_east = lon_below_band(to_west, -1)
    from_west = lon_below_band(to_east, 1)
    to_north, to_south = call(
        credit_rows_kernel, "credit_rows", (struct(2, 64, 128),) * 2, (to_north, to_south, from_east, from_west)
    )
    low_tile = low_tile.astype(F32) + band_from_east[:16].astype(F32) + band_from_west[:16].astype(F32)
    from_south = passed_along(to_north, "lat", 1)
    from_north = lax.ppermute(to_south, "lat", [(i, i - 1) for i in range(1, lats - 1)])
    from_band = lax.ppermute(low_tile.astype(BF), "lat", [(lats - 1, lats - 2)])
    (atmos_grads,) = call(
        atmos_back_kernel,
        "atmos_back",
        (((GRAD_ROWS, chans), F32),),
        (atmos_state, south[0], north[0], west[0], east[0], act, slope, own, from_west, from_east, from_south, from_north,
         band_from_west, band_from_east, from_band, project_back),
        [pltpu.VMEM((34 * 64, 768), BF), pltpu.VMEM((cells, 256), BF), pltpu.VMEM((64, 128), F32), pltpu.VMEM((half, 128), BF)],
    )
    ocean_grads = reduce_all(ocean_grads, (0, 1, 2))
    atmos_grads = reduce_all(atmos_grads, (1, 2, 0))
    split = lambda g: (g[: 9 * chans].reshape(9, chans, chans), g[9 * chans : 9 * chans + flux_chans])
    grad_ocean, grad_inject = split(ocean_grads)
    grad_atmos, grad_project = split(atmos_grads)
    return (ocean_out, grad_atmos, grad_ocean, grad_project.T, grad_inject)


def solution(mesh):
    return jax.shard_map(
        body,
        mesh=mesh,
        in_specs=(
            P("lat", "lon", None),
            P(),
            P(),
            P("lat", "lon", None),
            P("lat", "lon", None),
            P("lat", "lon", None),
            P("lat", "lon", None),
            P(),
            P("lat", "lon"),
            P(),
            P("lat", "lon", None),
        ),
        out_specs=(P("lat", "lon", None), P(), P(), P(), P()),
        check_vma=False,
    )
```

```python
import jax
import jax.numpy as jnp
from jax import lax
from jax.experimental import pallas as pl
from jax.experimental.pallas import tpu as pltpu
from jax.sharding import PartitionSpec as P

BF = jnp.bfloat16
F32 = jnp.float32
VLIM = 56 << 20
AXES = ("lon", "lat")
NEAR = 72
BAND = 192


def passed_along(x, axis, by):
    length = lax.axis_size(axis)
    pairs = [(i, i + by) for i in range(length) if 0 <= i + by < length]
    return lax.ppermute(x, axis, pairs)


def shifted(x, axis, by):
    length = lax.axis_size(axis)
    return lax.ppermute(x, axis, [(i, (i + by) % length) for i in range(length)])


def mirrored(x):
    lons, lats = lax.axis_size("lon"), lax.axis_size("lat")
    edge = lats - 1
    return lax.ppermute(x, AXES, [(i * lats + edge, (lons - 1 - i) * lats + edge) for i in range(lons)])


def lon_below_band(x, by):
    lons, lats = lax.axis_size("lon"), lax.axis_size("lat")
    return lax.ppermute(
        x, AXES, [(i * lats + j, ((i + by) % lons) * lats + j) for i in range(lons) for j in range(lats - 1)]
    )


def sigmoid(value):
    return 1.0 / (1.0 + jnp.exp(-value))


def silu_slope(value, sigma):
    return sigma * (1.0 + value * (1.0 - sigma))


VMEM = pl.BlockSpec(memory_space=pltpu.VMEM)
SMEM = pl.BlockSpec(memory_space=pltpu.SMEM)
PARAMS = pltpu.CompilerParams(vmem_limit_bytes=VLIM)
GRAD_ROWS = 2400


def call(kernel, name, outs, ins, scratch=(), scalars=0, specs=None, grid=None):
    if specs is None:
        specs = [SMEM] * scalars + [VMEM] * (len(ins) - scalars)
    extra = {} if grid is None else {"grid": grid}
    return pl.pallas_call(
        kernel,
        name=name,
        out_shape=tuple(jax.ShapeDtypeStruct(shape, kind) for shape, kind in outs),
        in_specs=specs,
        out_specs=(VMEM,) * len(outs),
        scratch_shapes=list(scratch),
        compiler_params=PARAMS,
        **extra,
    )(*ins)


def turned_row(row):
    a = lax.broadcasted_iota(jnp.int32, (64, 64), 0)
    b = lax.broadcasted_iota(jnp.int32, (64, 64), 1)
    flip = jnp.where(a + b == 63, jnp.float32(1.0), jnp.float32(0.0)).astype(BF)
    return jnp.dot(flip, row, preferred_element_type=F32)


def build_windows(dst, rows, row_of, west_of, east_of, turned=False):
    first, last = (512, 0) if turned else (0, 512)
    at = lax.broadcasted_iota(jnp.int32, (64, 256), 0)
    for r in range(rows):
        value = row_of(r)
        wide = value.astype(F32)
        left = jnp.where(at == 0, west_of(r).astype(F32), pltpu.roll(wide, 1, 0))
        right = jnp.where(at == 63, east_of(r).astype(F32), pltpu.roll(wide, 63, 0))
        here = slice(r * 64, r * 64 + 64)
        dst[here, first : first + 256] = left.astype(BF)
        dst[here, 256:512] = value
        dst[here, last : last + 256] = right.astype(BF)


def conv_rows(windows, w, start, count, turned=False):
    acc = jnp.zeros((count, 256), F32)
    for r in range(3):
        taps = w[2 - r if turned else r]
        acc += jnp.dot(windows[start + r * 64 : start + r * 64 + count, :], taps, preferred_element_type=F32)
    return acc


def dot_back(a, b):
    return lax.dot_general(a, b, (((1,), (1,)), ((), ())), preferred_element_type=F32)


def turned_lanes(x):
    return jnp.concatenate([x[:, 512:768], x[:, 256:512], x[:, 0:256]], 1)


def put_half(core, keep_ref, send_ref, here, value):
    low, high = value[:, 0:128], value[:, 128:256]
    keep_ref[here, :] = jnp.where(core == 0, low, high)
    send_ref[here, :] = jnp.where(core == 0, high, low).astype(BF)


def dot_rows(a, b):
    return lax.dot_general(a, b, (((0,), (0,)), ((), ())), preferred_element_type=F32)


def rows_kernel(a0_ref, a1_ref, c0_ref, c1_ref, m_ref, low_ref, high_ref):
    land = m_ref[...].astype(F32).T
    low_ref[0], high_ref[0] = a0_ref[0], a1_ref[0]
    low_ref[1] = (c0_ref[0].astype(F32) * land[:, 0:1]).astype(BF)
    high_ref[1] = (c1_ref[0].astype(F32) * land[:, 31:32]).astype(BF)


def edges_kernel(
    top_ref, a0_ref, a1_ref, c0_ref, c1_ref, m_ref, s_ref, n_ref, mir_ref, first_ref, last_ref, cn_ref, cols
):
    top = top_ref[0] != 0
    land = m_ref[...].astype(F32).T
    for r in range(32):
        here = slice(r + 1, r + 2)
        cols[0, here, :] = a0_ref[r, 0:1].astype(F32)
        cols[1, here, :] = c0_ref[r, 0:1].astype(F32) * land[0:1, r : r + 1]
        cols[2, here, :] = a1_ref[r, 15:16].astype(F32)
        cols[3, here, :] = c1_ref[r, 15:16].astype(F32) * land[63:64, r : r + 1]
    cn = jnp.where(top, turned_row(mir_ref[1]), n_ref[1].astype(F32))
    cn_ref[...] = cn.astype(BF)
    for k, (row, i) in enumerate(((s_ref[0], 0), (s_ref[1], 0), (s_ref[0], 63), (s_ref[1], 63))):
        cols[k, 0:1, :] = row[i : i + 1].astype(F32)
    north = n_ref[0].astype(F32)
    for k, (row, i) in enumerate(((north, 0), (cn, 0), (north, 63), (cn, 63))):
        cols[k, 33:34, :] = row[i : i + 1]
    first_ref[...] = cols[0:2].astype(BF)
    last_ref[...] = cols[2:4].astype(BF)


def mixed_edges_kernel(top_ref, cols_in, s_ref, n_ref, mir_ref, first_ref, last_ref, north_ref, cols):
    top = top_ref[0] != 0
    for r in range(2):
        s = s_ref[r].astype(F32)
        n = jnp.where(top, turned_row(mir_ref[1 - r]), n_ref[r].astype(F32))
        north_ref[r] = n.astype(BF)
        for k, i in enumerate((0, 1, 62, 63)):
            cols[k, r : r + 1, :] = s[i : i + 1]
            cols[k, 34 + r : 35 + r, :] = n[i : i + 1]
    for k in range(4):
        cols[k, 2:34, :] = cols_in[k].astype(F32)
    first_ref[...] = cols[0:2].astype(BF)
    last_ref[...] = cols[2:4].astype(BF)


def atmos_windows(windows, x_ref, s_ref, n_ref, we_ref, ea_ref):
    build_windows(
        windows,
        34,
        lambda r: s_ref[0] if r == 0 else (n_ref[0] if r == 33 else x_ref[r - 1]),
        lambda r: we_ref[0, r : r + 1, :],
        lambda r: ea_ref[0, r : r + 1, :],
    )


def packed_maps(p_ref):
    p = p_ref[...]
    zeros = jnp.zeros_like(p)
    return jnp.concatenate([p, zeros], 0), jnp.concatenate([zeros, p], 0)


def atmos_kernel(
    x_ref, s_ref, n_ref, we_ref, ea_ref, w_ref, p_ref, act_ref, slope_ref, own_ref, low_ref, high_ref, first_ref, last_ref, windows
):
    atmos_windows(windows, x_ref, s_ref, n_ref, we_ref, ea_ref)
    maps = packed_maps(p_ref)
    for b in range(2):
        packed = jnp.zeros((512, 128), F32)
        for h in range(2):
            start = h * 1024 + b * 512
            pre = conv_rows(windows, w_ref, start, 512)
            sigma = sigmoid(pre)
            act = (pre * sigma).astype(BF)
            act_ref[start : start + 512, :] = act
            slope_ref[start : start + 512, :] = silu_slope(pre, sigma).astype(BF)
            packed += dot_back(act, maps[h])
        for u in range(8):
            r = b * 8 + u
            row = packed[u * 64 : u * 64 + 64].astype(BF)
            own_ref[r] = row
            first_ref[r] = row[0:2]
            last_ref[r] = row[62:64]
            if r < 2:
                low_ref[r] = row
            if r >= 14:
                high_ref[r - 14] = row


def ocean_kernel(
    flag_ref, x_ref, s_ref, n_ref, first_ref, last_ref, we_ref, ea_ref, c_ref, cs_ref, cn_ref, cw_ref, ce_ref, m_ref, rem_ref,
    w_ref, wt_ref, inj_ref, out_ref, remap_ref, keep_ref, send_ref,
    windows, sides, north, turned_north, deltas, dwin, dsides, back,
):
    top, core = flag_ref[0] != 0, flag_ref[1]
    land = m_ref[...].astype(F32).T
    build_windows(
        windows,
        36,
        lambda r: s_ref[r] if r < 2 else (n_ref[r - 34] if r >= 34 else x_ref[r - 2]),
        lambda r: we_ref[1, r : r + 1, :],
        lambda r: ea_ref[0, r : r + 1, :],
    )
    sides[...] = jnp.zeros_like(sides)
    for side, columns in ((0, (we_ref[0], we_ref[1], first_ref[0])), (1, (last_ref[1], ea_ref[0], ea_ref[1]))):
        for q in range(3):
            sides[side, 0:36, q * 256 : q * 256 + 256] = columns[q].astype(F32)

    def side_rows(start, count):
        return jnp.concatenate([sides[0, start : start + count, :], sides[1, start : start + count, :]], 0).astype(BF)

    pre = jnp.zeros((80, 256), F32)
    lines = [jnp.concatenate([windows[(33 + r) * 64 : (34 + r) * 64, :], side_rows(33 + r, 8)], 0) for r in range(3)]
    for r in range(3):
        pre += jnp.dot(jnp.where(top, turned_lanes(lines[2 - r]), lines[r]), w_ref[r], preferred_element_type=F32)
    slope = silu_slope(pre, sigmoid(pre))
    d_north = (cn_ref[...].astype(F32) * slope[0:64]).astype(BF)
    side_pre = jnp.zeros((80, 256), F32)
    for r in range(3):
        side_pre += jnp.dot(side_rows(r, 40), w_ref[r], preferred_element_type=F32)
    side_slope = silu_slope(side_pre, sigmoid(side_pre))
    at = lax.broadcasted_iota(jnp.int32, (40, 256), 0)
    for side, cot in ((0, cw_ref), (1, ce_ref)):
        corner = slope[64 + side * 8 : 65 + side * 8]
        here = jnp.where(at == 33, corner, side_slope[side * 40 : side * 40 + 40])
        dsides[side] = jnp.zeros((40, 256), F32)
        dsides[side, 0:34, :] = cot[1].astype(F32) * here[0:34]
    pre = conv_rows(windows, w_ref, 0, 64)
    d_south = (cs_ref[1].astype(F32) * silu_slope(pre, sigmoid(pre))).astype(BF)
    for b in range(4):
        pre = conv_rows(windows, w_ref, 64 + b * 512, 512)
        sigma = sigmoid(pre)
        act = pre * sigma
        slope = silu_slope(pre, sigma)
        for u in range(8):
            r = b * 8 + u
            here = slice(u * 64, u * 64 + 64)
            wet = land[:, r : r + 1]
            out_ref[r] = (wet * act[here]).astype(BF)
            deltas[r * 64 : r * 64 + 64, :] = (c_ref[r].astype(F32) * wet * slope[here]).astype(BF)
    dry = jnp.zeros((64, 256), BF)
    build_windows(
        dwin,
        34,
        lambda r: d_south if r == 0 else (dry if r == 33 else deltas[r * 64 - 64 : r * 64, :]),
        lambda r: dsides[0, r : r + 1, :] if r < 33 else dry[0:1],
        lambda r: dsides[1, r : r + 1, :] if r < 33 else dry[0:1],
        turned=True,
    )
    for dst, turned in ((north, False), (turned_north, True)):
        build_windows(
            dst, 1, lambda r: d_north, lambda r: dsides[0, 33:34, :], lambda r: dsides[1, 33:34, :], turned=turned
        )
    beyond = jnp.dot(
        jnp.where(top, north[...], turned_north[...]), wt_ref[jnp.where(top, 2, 0)], preferred_element_type=F32
    )
    inject = jnp.concatenate([inj_ref[...], inj_ref[...]], 0)
    for b in range(4):
        total = conv_rows(dwin, wt_ref, b * 512, 512, turned=True)
        for u in range(8):
            r = b * 8 + u
            value = total[u * 64 : u * 64 + 64]
            if r == 31:
                value = value + beyond
            back[r * 64 : r * 64 + 64, :] = (land[:, r : r + 1] * value).astype(BF)
        remap_ref[b * 512 : b * 512 + 512, :] = dot_back(back[b * 512 : b * 512 + 512, :], inject).astype(BF)
    for r in range(3):
        value = dot_rows(windows[(r + 1) * 64 : (r + 1) * 64 + 2048, :], deltas[...])
        put_half(core, keep_ref, send_ref, slice(r * 768, r * 768 + 768), value)
    tail = jnp.concatenate([dot_rows(rem_ref[...], back[...])[0:64], jnp.zeros((32, 256), F32)], 0)
    put_half(core, keep_ref, send_ref, slice(2304, 2400), tail)


def credit_rows_kernel(n_ref, s_ref, e_ref, w_ref, n_out, s_out):
    for r in range(2):
        for src, dst, first in ((n_ref, n_out, 16), (s_ref, s_out, 18)):
            dst[r] = src[r]
            dst[r, 0:2] = (src[r, 0:2].astype(F32) + w_ref[first + r].astype(F32)).astype(BF)
            dst[r, 62:64] = (src[r, 62:64].astype(F32) + e_ref[first + r].astype(F32)).astype(BF)


def atmos_back_kernel(
    flag_ref, x_ref, s_ref, n_ref, we_ref, ea_ref, act_ref, slope_ref, own_ref, cw_ref, ce_ref, cs_ref, cn_ref, bw_ref, be_ref,
    low_ref, p_ref, keep_ref, send_ref, windows, deltas, total, credit,
):
    core = flag_ref[1]
    atmos_windows(windows, x_ref, s_ref, n_ref, we_ref, ea_ref)
    maps = packed_maps(p_ref)
    for r in range(16):
        value = own_ref[r].astype(F32) + bw_ref[16 + r].astype(F32) + be_ref[16 + r].astype(F32) + low_ref[r].astype(F32)
        if r < 2:
            value += cs_ref[r].astype(F32)
        if r >= 14:
            value += cn_ref[r - 14].astype(F32)
        total[...] = value
        total[0:2, :] += cw_ref[r].astype(F32)
        total[62:64, :] += ce_ref[r].astype(F32)
        credit[r * 64 : r * 64 + 64, :] = total[...].astype(BF)
    for h in range(2):
        here = slice(h * 1024, h * 1024 + 1024)
        back = jnp.dot(credit[...], maps[h], preferred_element_type=F32)
        deltas[here, :] = (back * slope_ref[here, :].astype(F32)).astype(BF)
    for r in range(3):
        value = dot_rows(windows[r * 64 : r * 64 + 2048, :], deltas[...])
        put_half(core, keep_ref, send_ref, slice(r * 768, r * 768 + 768), value)
    lower = dot_rows(credit[...], act_ref[0:1024, :])
    upper = dot_rows(credit[...], act_ref[1024:2048, :])
    tail = jnp.concatenate([lower[0:64] + upper[64:128], jnp.zeros((32, 256), F32)], 0)
    put_half(core, keep_ref, send_ref, slice(2304, 2400), tail)


def exchange(x, mask):
    count = lax.axis_size("lon") * lax.axis_size("lat")
    return lax.ppermute(x, AXES, [(i, i ^ mask) for i in range(count)])


def reduce_streams(streams, orders):
    rank = lax.axis_index("lon") * lax.axis_size("lat") + lax.axis_index("lat")
    bit = lambda n: (rank >> n) & 1
    near = [(2, bit(1) ^ bit(2)), (8, bit(3) ^ bit(4)), (32, bit(5) ^ bit(6))]
    far = (6, 24, 96)
    count = range(len(streams))
    for level in range(3):
        steps = [near[orders[i][level]] for i in count]
        half = streams[0].shape[0] // 2
        keep = [lax.dynamic_slice_in_dim(streams[i], steps[i][1] * half, half) for i in count]
        send = [lax.dynamic_slice_in_dim(streams[i], (1 - steps[i][1]) * half, half).astype(BF) for i in count]
        streams = [keep[i] + exchange(send[i], steps[i][0]).astype(F32) for i in count]
    streams = [s.astype(BF) for s in streams]
    for level in range(3):
        got = [exchange(streams[i], far[orders[i][level]]) for i in count]
        streams = [(streams[i].astype(F32) + got[i].astype(F32)).astype(BF) for i in count]
    for level in (2, 1, 0):
        steps = [near[orders[i][level]] for i in count]
        got = [exchange(streams[i], steps[i][0]) for i in count]
        streams = [
            jnp.where(
                steps[i][1] == 0,
                jnp.concatenate([streams[i], got[i]]),
                jnp.concatenate([got[i], streams[i]]),
            )
            for i in count
        ]
    return streams


def lane_sign():
    lane = lax.broadcasted_iota(jnp.int32, (64, 128), 1)
    return jnp.where(lane < 64, jnp.float32(1.0), jnp.float32(-1.0))


def gather_kernel(
    top_ref, slot_ref, w_ref, fn_ref, fs_ref, fw_ref, fe_ref, low_ref, own_ref, west_ref, east_ref, west_low, east_low, o_ref, m_ref, inj_ref,
    out_ref, mixed_ref, cols_ref, first_ref, last_ref, table, picked, cols,
):
    top = top_ref[0]

    @pl.when(top == 0)
    def _():
        for r in range(20):
            rows = own_ref[r] if r < 16 else (fn_ref[r - 16] if r < 18 else fs_ref[r - 18])
            table[r * NEAR : r * NEAR + 64, :] = rows.astype(F32)
            table[r * NEAR + 64 : r * NEAR + 66, :] = fw_ref[r].astype(F32)
            table[r * NEAR + 66 : r * NEAR + 68, :] = fe_ref[r].astype(F32)

    @pl.when(top != 0)
    def _():
        for r in range(32):
            base = r * BAND
            table[base : base + 64, :] = (low_ref[r] if r < 16 else own_ref[r - 16]).astype(F32)
            table[base + 64 : base + 128, :] = (west_low[r] if r < 16 else west_ref[r - 16]).astype(F32)
            table[base + 128 : base + 192, :] = (east_low[r] if r < 16 else east_ref[r - 16]).astype(F32)

    def step(q, carry):
        base = pl.multiple_of(q * 64, 64)
        for u in range(64):
            at = slot_ref[q, u]
            picked[pl.ds(base + u, 1), :] = table[pl.ds(at, 1), :]
        return carry

    lax.fori_loop(0, 128, step, 0)
    sign = lane_sign()
    wt = w_ref[...].T
    for row in range(32):
        acc = jnp.zeros((64, 128), F32)
        for k in range(4):
            q = row * 4 + k
            factor = jnp.maximum(wt[:, q : q + 1] * sign, 0.0)
            acc = acc + factor * picked[q * 64 : q * 64 + 64, :]
        acc = acc + pltpu.roll(acc, 64, 1)
        out_ref[row * 64 : row * 64 + 64, :] = acc.astype(BF)
    land = m_ref[...].astype(F32).T
    inject = jnp.concatenate([inj_ref[...], jnp.zeros_like(inj_ref[...])], 0)
    for b in range(4):
        injected = jnp.dot(out_ref[b * 512 : b * 512 + 512, :], inject, preferred_element_type=F32)
        for u in range(8):
            r = b * 8 + u
            value = land[:, r : r + 1] * (o_ref[r].astype(F32) + injected[u * 64 : u * 64 + 64])
            mixed_ref[r] = value.astype(BF)
            if r < 2:
                first_ref[r] = value.astype(BF)
            if r >= 30:
                last_ref[r - 30] = value.astype(BF)
            for c, i in enumerate((0, 1, 62, 63)):
                cols[c, r : r + 1, :] = value[i : i + 1]
    cols_ref[...] = cols[...].astype(BF)


def scatter_kernel(
    top_ref, slot_ref, w_ref, g_ref, own_ref, n_ref, s_ref, w_out, e_out, low_ref, west_ref, east_ref, t0, t1, t2, t3, parts
):
    top = top_ref[0]
    tables = (t0, t1, t2, t3)

    def clear(count):
        def one(i, carry):
            base = pl.multiple_of(i * 96, 96)
            for t in tables:
                t[pl.ds(base, 96), :] = jnp.zeros((96, 128), F32)
            return carry

        lax.fori_loop(0, count // 96, one, 0)

    @pl.when(top == 0)
    def _():
        clear(20 * NEAR)

    @pl.when(top != 0)
    def _():
        clear(32 * BAND)

    sign = lane_sign()
    wt = w_ref[...].T
    for row in range(32):
        g = g_ref[row * 64 : row * 64 + 64, :].astype(F32)
        for k in range(4):
            q = row * 4 + k
            parts[q * 64 : q * 64 + 64, :] = jnp.maximum(wt[:, q : q + 1] * sign, 0.0) * g

    def step(row, carry):
        base = pl.multiple_of(row * 256, 256)
        for u in range(64):
            for k in range(4):
                at = slot_ref[row * 4 + k, u]
                t = tables[k]
                t[pl.ds(at, 1), :] = t[pl.ds(at, 1), :] + parts[pl.ds(base + k * 64 + u, 1), :]
        return carry

    lax.fori_loop(0, 32, step, 0)

    def total(start, size):
        where = pl.ds(start, size)
        return ((t0[where, :] + t1[where, :]) + (t2[where, :] + t3[where, :])).astype(BF)

    @pl.when(top == 0)
    def _():
        for r in range(20):
            rows = total(r * NEAR, 64)
            if r < 16:
                own_ref[r] = rows
            elif r < 18:
                n_ref[r - 16] = rows
            else:
                s_ref[r - 18] = rows
            w_out[r] = total(r * NEAR + 64, 2)
            e_out[r] = total(r * NEAR + 66, 2)

    @pl.when(top != 0)
    def _():
        for r in range(2):
            n_ref[r] = jnp.zeros((64, 128), BF)
            s_ref[r] = jnp.zeros((64, 128), BF)
        w_out[...] = jnp.zeros_like(w_out)
        e_out[...] = jnp.zeros_like(e_out)
        for r in range(32):
            base = r * BAND
            if r < 16:
                low_ref[r] = total(base, 64)
            else:
                own_ref[r - 16] = total(base, 64)
            west_ref[r] = total(base + 64, 64)
            east_ref[r] = total(base + 128, 64)


def band_lon(x, by):
    lons, lats = lax.axis_size("lon"), lax.axis_size("lat")
    return lax.ppermute(x, AXES, [(i * lats + lats - 1, ((i + by) % lons) * lats + lats - 1) for i in range(lons)])


def entry_slots(source_row, source_col, weight, is_top, row_count, col_count):
    nx = col_count * lax.axis_size("lon")
    row = source_row - lax.axis_index("lat") * row_count
    col = jnp.remainder(source_col - lax.axis_index("lon") * col_count + nx // 2, nx) - nx // 2
    half = row_count // 2
    inside = (row >= 0) & (row < row_count)
    wrapped = row & (row_count - 1)
    packed = wrapped & (half - 1)
    upper = wrapped >= half
    near_row = jnp.where(inside, packed, jnp.where(row < 0, packed + 4, packed + half))
    near_col = jnp.where((col >= 0) & (col < col_count), col, jnp.where(col < 0, col + col_count + 2, col + 2))
    band_row = jnp.where(row >= 0, packed + half, packed)
    band_col = jnp.where((col >= 0) & (col < col_count), col, jnp.where(col < 0, col + 2 * col_count, col + col_count))
    slot = jnp.where(is_top, band_row * BAND + band_col, near_row * NEAR + near_col)
    signed = jnp.where(upper, -weight, weight)
    order = lambda x: jnp.transpose(x, (0, 2, 1)).reshape(-1, col_count)
    return order(slot), order(signed)


def body(
    atmos_state,
    atmos_weights,
    flux_project,
    source_row,
    source_col,
    intersection_weight,
    ocean_state,
    flux_inject,
    ocean_mask,
    ocean_weights,
    out_cotangent,
):
    row_count, col_count, chans = atmos_state.shape
    flux_chans = flux_project.shape[1]
    cells = row_count * col_count
    half = cells // 2
    lats = lax.axis_size("lat")
    is_top = lax.axis_index("lat") == lats - 1
    core = lax.rem(lax.axis_index("lat"), 2)
    top = jnp.broadcast_to(is_top.astype(jnp.int32), (1,))
    flags = jnp.stack([is_top.astype(jnp.int32), core])
    struct = lambda *shape: (shape, BF)
    block = lambda shape, at: pl.BlockSpec(shape, lambda i: (at[0], at[1], 0))
    row = (1, 64, 256)
    low, high = call(
        rows_kernel,
        "rows",
        (struct(2, 64, 256), struct(2, 64, 256)),
        (atmos_state, atmos_state, out_cotangent, out_cotangent, ocean_mask),
        specs=[block(row, (0, 0)), block(row, (31, 0)), block(row, (0, 0)), block(row, (31, 0)), VMEM],
        grid=(1,),
    )
    south = passed_along(high, "lat", 1)
    north = passed_along(low, "lat", -1)
    mirror = mirrored(high)
    slab = (32, 16, 256)
    first, last, cot_north = call(
        edges_kernel,
        "edges",
        (struct(2, 34, 256), struct(2, 34, 256), struct(64, 256)),
        (top, atmos_state, atmos_state, out_cotangent, out_cotangent, ocean_mask, south, north, mirror),
        [pltpu.VMEM((4, 34, 256), F32)],
        specs=[SMEM, block(slab, (0, 0)), block(slab, (0, 3)), block(slab, (0, 0)), block(slab, (0, 3))] + [VMEM] * 4,
        grid=(1,),
    )
    west = shifted(last, "lon", 1)
    east = shifted(first, "lon", -1)
    project = flux_project.T
    atmos_w = atmos_weights.reshape(3, 3 * chans, chans)
    ocean_w = ocean_weights.reshape(3, 3 * chans, chans)
    act, slope, own, flux_low, flux_high, first, last = call(
        atmos_kernel,
        "atmos",
        (struct(cells, chans), struct(cells, chans), struct(16, 64, 128), struct(2, 64, 128), struct(2, 64, 128),
         struct(16, 2, 128), struct(16, 2, 128)),
        (atmos_state, south, north, west, east, atmos_w, project),
        [pltpu.VMEM((34 * 64, 768), BF)],
    )
    low_tile = lax.ppermute(own, "lat", [(lats - 2, lats - 1)])
    flux_south = lax.ppermute(flux_high, "lat", [(i, i + 1) for i in range(lats - 2)])
    flux_north = passed_along(flux_low, "lat", -1)
    band_west = band_lon(own, 1)
    band_east = band_lon(own, -1)
    low_west = band_lon(low_tile, 1)
    low_east = band_lon(low_tile, -1)
    flux_west = lon_below_band(jnp.concatenate([last, flux_north[:, -2:], flux_south[:, -2:]], 0), 1)
    flux_east = lon_below_band(jnp.concatenate([first, flux_north[:, :2], flux_south[:, :2]], 0), -1)
    late = lax.optimization_barrier((own, source_row, source_col, intersection_weight, ocean_weights))
    slots, signed = entry_slots(*late[1:4], is_top, row_count, col_count)
    back_w = jnp.transpose(late[4], (0, 2, 1)).reshape(3, 3 * chans, chans)
    remapped, mixed, cols, low, high = call(
        gather_kernel,
        "gather_mix",
        (struct(cells, 128), struct(32, 64, 256), struct(4, 32, 256), struct(2, 64, 256), struct(2, 64, 256)),
        (top, slots, signed, flux_north, flux_south, flux_west, flux_east, low_tile, own, band_west, band_east,
         low_west, low_east, ocean_state, ocean_mask, flux_inject),
        [pltpu.VMEM((32 * BAND, 128), F32), pltpu.VMEM((8192, 128), F32), pltpu.VMEM((4, 32, 256), F32)],
        scalars=2,
    )
    mixed_south = passed_along(high, "lat", 1)
    mixed_north = passed_along(low, "lat", -1)
    mirror = mirrored(high)
    first, last, mixed_north = call(
        mixed_edges_kernel,
        "mixed_edges",
        (struct(2, 36, 256), struct(2, 36, 256), struct(2, 64, 256)),
        (top, cols, mixed_south, mixed_north, mirror),
        [pltpu.VMEM((4, 36, 256), F32)],
        scalars=1,
    )
    mixed_west = shifted(last, "lon", 1)
    mixed_east = shifted(first, "lon", -1)
    halves = ((GRAD_ROWS, 128), F32), ((GRAD_ROWS, 128), BF)
    ocean_out, remap_grad, ocean_keep, ocean_send = call(
        ocean_kernel,
        "ocean",
        (struct(32, 64, 256), struct(cells, 128)) + halves,
        (
            flags, mixed, mixed_south, mixed_north, first, last, mixed_west, mixed_east,
            out_cotangent, south, cot_north, west, east, ocean_mask, remapped, ocean_w, back_w, flux_inject,
        ),
        [
            pltpu.VMEM((36 * 64, 768), BF),
            pltpu.VMEM((2, 48, 768), F32),
            pltpu.VMEM((64, 768), BF),
            pltpu.VMEM((64, 768), BF),
            pltpu.VMEM((cells, 256), BF),
            pltpu.VMEM((34 * 64, 768), BF),
            pltpu.VMEM((2, 40, 256), F32),
            pltpu.VMEM((cells, 256), BF),
        ],
        scalars=1,
    )
    own, to_north, to_south, to_west, to_east, low_tile, band_west, band_east = call(
        scatter_kernel,
        "scatter_rows",
        (struct(16, 64, 128), struct(2, 64, 128), struct(2, 64, 128), struct(20, 2, 128), struct(20, 2, 128),
         struct(16, 64, 128), struct(32, 64, 128), struct(32, 64, 128)),
        (top, slots, signed, remap_grad),
        [pltpu.VMEM((32 * BAND, 128), F32)] * 4 + [pltpu.VMEM((8192, 128), F32)],
        scalars=2,
    )
    band_from_east = band_lon(band_west, -1)
    band_from_west = band_lon(band_east, 1)
    from_east = lon_below_band(to_west, -1)
    from_west = lon_below_band(to_east, 1)
    to_north, to_south = call(
        credit_rows_kernel, "credit_rows", (struct(2, 64, 128),) * 2, (to_north, to_south, from_east, from_west)
    )
    low_tile = low_tile.astype(F32) + band_from_east[:16].astype(F32) + band_from_west[:16].astype(F32)
    from_south = passed_along(to_north, "lat", 1)
    from_north = lax.ppermute(to_south, "lat", [(i, i - 1) for i in range(1, lats - 1)])
    from_band = lax.ppermute(low_tile.astype(BF), "lat", [(lats - 1, lats - 2)])
    atmos_keep, atmos_send = call(
        atmos_back_kernel,
        "atmos_back",
        halves,
        (flags, atmos_state, south, north, west, east, act, slope, own, from_west, from_east, from_south, from_north,
         band_from_west, band_from_east, from_band, project),
        [pltpu.VMEM((34 * 64, 768), BF), pltpu.VMEM((cells, 256), BF), pltpu.VMEM((64, 128), F32), pltpu.VMEM((half, 128), BF)],
        scalars=1,
    )
    ocean = ocean_keep + exchange(ocean_send, 1).astype(F32)
    atmos = atmos_keep + exchange(atmos_send, 1).astype(F32)
    cut = 1600
    rest = GRAD_ROWS - cut
    sums = reduce_streams(
        [ocean[:cut], jnp.concatenate([ocean[cut:], atmos[:rest]]), atmos[rest:]], ((0, 1, 2), (1, 2, 0), (2, 0, 1))
    )
    ocean = jnp.concatenate([sums[0], sums[1][:rest]])
    atmos = jnp.concatenate([sums[1][rest:], sums[2]])

    def joined(mine):
        other = exchange(mine, 1)
        pair = jnp.concatenate([jnp.where(core == 0, mine, other), jnp.where(core == 0, other, mine)], 1).astype(F32)
        return pair[: 9 * chans].reshape(9, chans, chans), pair[9 * chans : 9 * chans + flux_chans]

    grad_ocean, grad_inject = joined(ocean)
    grad_atmos, grad_project = joined(atmos)
    return (ocean_out, grad_atmos, grad_ocean, grad_project.T, grad_inject)


def solution(mesh):
    return jax.shard_map(
        body,
        mesh=mesh,
        in_specs=(
            P("lat", "lon", None),
            P(),
            P(),
            P("lat", "lon", None),
            P("lat", "lon", None),
            P("lat", "lon", None),
            P("lat", "lon", None),
            P(),
            P("lat", "lon"),
            P(),
            P("lat", "lon", None),
        ),
        out_specs=(P("lat", "lon", None), P(), P(), P(), P()),
        check_vma=False,
    )
```

```python
import jax
import jax.numpy as jnp
from jax import lax
from jax.experimental import pallas as pl
from jax.experimental.pallas import tpu as pltpu
from jax.sharding import PartitionSpec as P

BF = jnp.bfloat16
F32 = jnp.float32
VLIM = 56 << 20
AXES = ("lon", "lat")
NEAR = 72
BAND = 192


def passed_along(x, axis, by):
    length = lax.axis_size(axis)
    pairs = [(i, i + by) for i in range(length) if 0 <= i + by < length]
    return lax.ppermute(x, axis, pairs)


def shifted(x, axis, by):
    length = lax.axis_size(axis)
    return lax.ppermute(x, axis, [(i, (i + by) % length) for i in range(length)])


def lat_pairs(inner, outer):
    lons, lats = lax.axis_size("lon"), lax.axis_size("lat")
    at = lambda i, j: i * lats + j
    inside = [(at(i, j), at(i, j ^ 1)) for i in range(lons) for j in range(lats)]
    across = [(at(i, j), at(i, j + 1 if j % 2 else j - 1)) for i in range(lons) for j in range(1, lats - 1)]
    across += [(at(i, lats - 1), at(lons - 1 - i, lats - 1)) for i in range(lons)]
    return lax.ppermute(inner, AXES, inside), lax.ppermute(outer, AXES, across)


def lon_below_band(x, by):
    lons, lats = lax.axis_size("lon"), lax.axis_size("lat")
    return lax.ppermute(
        x, AXES, [(i * lats + j, ((i + by) % lons) * lats + j) for i in range(lons) for j in range(lats - 1)]
    )


def sigmoid(value):
    return 1.0 / (1.0 + jnp.exp(-value))


def silu_slope(value, sigma):
    return sigma * (1.0 + value * (1.0 - sigma))


VMEM = pl.BlockSpec(memory_space=pltpu.VMEM)
SMEM = pl.BlockSpec(memory_space=pltpu.SMEM)
PARAMS = pltpu.CompilerParams(vmem_limit_bytes=VLIM)
GRAD_ROWS = 2400


def call(kernel, name, outs, ins, scratch=(), scalars=0, specs=None, grid=None):
    if specs is None:
        specs = [SMEM] * scalars + [VMEM] * (len(ins) - scalars)
    extra = {} if grid is None else {"grid": grid}
    return pl.pallas_call(
        kernel,
        name=name,
        out_shape=tuple(jax.ShapeDtypeStruct(shape, kind) for shape, kind in outs),
        in_specs=specs,
        out_specs=(VMEM,) * len(outs),
        scratch_shapes=list(scratch),
        compiler_params=PARAMS,
        **extra,
    )(*ins)


def turned_row(row):
    a = lax.broadcasted_iota(jnp.int32, (64, 64), 0)
    b = lax.broadcasted_iota(jnp.int32, (64, 64), 1)
    flip = jnp.where(a + b == 63, jnp.float32(1.0), jnp.float32(0.0)).astype(BF)
    return jnp.dot(flip, row, preferred_element_type=F32)


def build_windows(dst, rows, row_of, west_of, east_of, turned=False):
    first, last = (512, 0) if turned else (0, 512)
    at = lax.broadcasted_iota(jnp.int32, (64, 256), 0)
    for r in range(rows):
        value = row_of(r)
        wide = value.astype(F32)
        left = jnp.where(at == 0, west_of(r).astype(F32), pltpu.roll(wide, 1, 0))
        right = jnp.where(at == 63, east_of(r).astype(F32), pltpu.roll(wide, 63, 0))
        here = slice(r * 64, r * 64 + 64)
        dst[here, first : first + 256] = left.astype(BF)
        dst[here, 256:512] = value
        dst[here, last : last + 256] = right.astype(BF)


def conv_rows(windows, w, start, count, turned=False):
    acc = jnp.zeros((count, 256), F32)
    for r in range(3):
        taps = w[2 - r if turned else r]
        acc += jnp.dot(windows[start + r * 64 : start + r * 64 + count, :], taps, preferred_element_type=F32)
    return acc


def dot_back(a, b):
    return lax.dot_general(a, b, (((1,), (1,)), ((), ())), preferred_element_type=F32)


def turned_lanes(x):
    return jnp.concatenate([x[:, 512:768], x[:, 256:512], x[:, 0:256]], 1)


def put_half(core, keep_ref, send_ref, here, value):
    low, high = value[:, 0:128], value[:, 128:256]
    keep_ref[here, :] = jnp.where(core == 0, low, high)
    send_ref[here, :] = jnp.where(core == 0, high, low).astype(BF)


def dot_rows(a, b):
    return lax.dot_general(a, b, (((0,), (0,)), ((), ())), preferred_element_type=F32)


def put_pair(odd, inner_ref, outer_ref, r, low, high):
    inner_ref[r] = jnp.where(odd, low, high)
    outer_ref[r] = jnp.where(odd, high, low)


def rows_kernel(flag_ref, a0_ref, a1_ref, c0_ref, c1_ref, m_ref, inner_ref, outer_ref):
    odd = flag_ref[1] != 0
    land = m_ref[...].astype(F32).T
    put_pair(odd, inner_ref, outer_ref, 0, a0_ref[0], a1_ref[0])
    low = (c0_ref[0].astype(F32) * land[:, 0:1]).astype(BF)
    high = (c1_ref[0].astype(F32) * land[:, 31:32]).astype(BF)
    put_pair(odd, inner_ref, outer_ref, 1, low, high)


def edges_kernel(
    flag_ref, a0_ref, a1_ref, c0_ref, c1_ref, m_ref, inner_ref, outer_ref, first_ref, last_ref, s_ref, n_ref, cols
):
    top, odd = flag_ref[0] != 0, flag_ref[1] != 0
    land = m_ref[...].astype(F32).T
    for r in range(2):
        s_ref[r] = jnp.where(odd, inner_ref[r], outer_ref[r])
    north = jnp.where(odd, outer_ref[0], inner_ref[0]).astype(F32)
    north = jnp.where(top, jnp.zeros_like(north), north)
    cn = jnp.where(odd, outer_ref[1], inner_ref[1])
    cn = jnp.where(top, turned_row(cn), cn.astype(F32))
    n_ref[0], n_ref[1] = north.astype(BF), cn.astype(BF)
    for r in range(32):
        here = slice(r + 1, r + 2)
        cols[0, here, :] = a0_ref[r, 0:1].astype(F32)
        cols[1, here, :] = c0_ref[r, 0:1].astype(F32) * land[0:1, r : r + 1]
        cols[2, here, :] = a1_ref[r, 15:16].astype(F32)
        cols[3, here, :] = c1_ref[r, 15:16].astype(F32) * land[63:64, r : r + 1]
    for k, (row, i) in enumerate(((s_ref[0], 0), (s_ref[1], 0), (s_ref[0], 63), (s_ref[1], 63))):
        cols[k, 0:1, :] = row[i : i + 1].astype(F32)
    for k, (row, i) in enumerate(((north, 0), (cn, 0), (north, 63), (cn, 63))):
        cols[k, 33:34, :] = row[i : i + 1]
    first_ref[...] = cols[0:2].astype(BF)
    last_ref[...] = cols[2:4].astype(BF)


def mixed_edges_kernel(flag_ref, cols_in, inner_ref, outer_ref, first_ref, last_ref, south_ref, north_ref, cols):
    top, odd = flag_ref[0] != 0, flag_ref[1] != 0
    for r in range(2):
        south_ref[r] = jnp.where(odd, inner_ref[r], outer_ref[r])
        s = south_ref[r].astype(F32)
        n = jnp.where(odd, outer_ref[r], inner_ref[r]).astype(F32)
        n = jnp.where(top, turned_row(outer_ref[1 - r]), n)
        north_ref[r] = n.astype(BF)
        for k, i in enumerate((0, 1, 62, 63)):
            cols[k, r : r + 1, :] = s[i : i + 1]
            cols[k, 34 + r : 35 + r, :] = n[i : i + 1]
    for k in range(4):
        cols[k, 2:34, :] = cols_in[k].astype(F32)
    first_ref[...] = cols[0:2].astype(BF)
    last_ref[...] = cols[2:4].astype(BF)


def atmos_windows(windows, x_ref, s_ref, n_ref, we_ref, ea_ref):
    build_windows(
        windows,
        34,
        lambda r: s_ref[0] if r == 0 else (n_ref[0] if r == 33 else x_ref[r - 1]),
        lambda r: we_ref[0, r : r + 1, :],
        lambda r: ea_ref[0, r : r + 1, :],
    )


def packed_maps(p_ref):
    p = p_ref[...]
    zeros = jnp.zeros_like(p)
    return jnp.concatenate([p, zeros], 0), jnp.concatenate([zeros, p], 0)


def atmos_kernel(
    x_ref, s_ref, n_ref, we_ref, ea_ref, w_ref, p_ref, act_ref, slope_ref, own_ref, low_ref, high_ref, first_ref, last_ref, windows
):
    atmos_windows(windows, x_ref, s_ref, n_ref, we_ref, ea_ref)
    maps = packed_maps(p_ref)
    for b in range(2):
        packed = jnp.zeros((512, 128), F32)
        for h in range(2):
            start = h * 1024 + b * 512
            pre = conv_rows(windows, w_ref, start, 512)
            sigma = sigmoid(pre)
            act = (pre * sigma).astype(BF)
            act_ref[start : start + 512, :] = act
            slope_ref[start : start + 512, :] = silu_slope(pre, sigma).astype(BF)
            packed += dot_back(act, maps[h])
        for u in range(8):
            r = b * 8 + u
            row = packed[u * 64 : u * 64 + 64].astype(BF)
            own_ref[r] = row
            first_ref[r] = row[0:2]
            last_ref[r] = row[62:64]
            if r < 2:
                low_ref[r] = row
            if r >= 14:
                high_ref[r - 14] = row


def ocean_kernel(
    flag_ref, x_ref, s_ref, n_ref, first_ref, last_ref, we_ref, ea_ref, c_ref, cs_ref, cn_ref, cw_ref, ce_ref, m_ref, rem_ref,
    w_ref, wt_ref, inj_ref, out_ref, remap_ref, keep_ref, send_ref,
    windows, sides, north, turned_north, deltas, dwin, dsides, back,
):
    top, core = flag_ref[0] != 0, flag_ref[1]
    land = m_ref[...].astype(F32).T
    build_windows(
        windows,
        36,
        lambda r: s_ref[r] if r < 2 else (n_ref[r - 34] if r >= 34 else x_ref[r - 2]),
        lambda r: we_ref[1, r : r + 1, :],
        lambda r: ea_ref[0, r : r + 1, :],
    )
    sides[...] = jnp.zeros_like(sides)
    for side, columns in ((0, (we_ref[0], we_ref[1], first_ref[0])), (1, (last_ref[1], ea_ref[0], ea_ref[1]))):
        for q in range(3):
            sides[side, 0:36, q * 256 : q * 256 + 256] = columns[q].astype(F32)

    def side_rows(start, count):
        return jnp.concatenate([sides[0, start : start + count, :], sides[1, start : start + count, :]], 0).astype(BF)

    pre = jnp.zeros((80, 256), F32)
    lines = [jnp.concatenate([windows[(33 + r) * 64 : (34 + r) * 64, :], side_rows(33 + r, 8)], 0) for r in range(3)]
    for r in range(3):
        pre += jnp.dot(jnp.where(top, turned_lanes(lines[2 - r]), lines[r]), w_ref[r], preferred_element_type=F32)
    slope = silu_slope(pre, sigmoid(pre))
    d_north = (cn_ref[1].astype(F32) * slope[0:64]).astype(BF)
    side_pre = jnp.zeros((80, 256), F32)
    for r in range(3):
        side_pre += jnp.dot(side_rows(r, 40), w_ref[r], preferred_element_type=F32)
    side_slope = silu_slope(side_pre, sigmoid(side_pre))
    at = lax.broadcasted_iota(jnp.int32, (40, 256), 0)
    for side, cot in ((0, cw_ref), (1, ce_ref)):
        corner = slope[64 + side * 8 : 65 + side * 8]
        here = jnp.where(at == 33, corner, side_slope[side * 40 : side * 40 + 40])
        dsides[side] = jnp.zeros((40, 256), F32)
        dsides[side, 0:34, :] = cot[1].astype(F32) * here[0:34]
    pre = conv_rows(windows, w_ref, 0, 64)
    d_south = (cs_ref[1].astype(F32) * silu_slope(pre, sigmoid(pre))).astype(BF)
    for b in range(4):
        pre = conv_rows(windows, w_ref, 64 + b * 512, 512)
        sigma = sigmoid(pre)
        act = pre * sigma
        slope = silu_slope(pre, sigma)
        for u in range(8):
            r = b * 8 + u
            here = slice(u * 64, u * 64 + 64)
            wet = land[:, r : r + 1]
            out_ref[r] = (wet * act[here]).astype(BF)
            deltas[r * 64 : r * 64 + 64, :] = (c_ref[r].astype(F32) * wet * slope[here]).astype(BF)
    dry = jnp.zeros((64, 256), BF)
    build_windows(
        dwin,
        34,
        lambda r: d_south if r == 0 else (dry if r == 33 else deltas[r * 64 - 64 : r * 64, :]),
        lambda r: dsides[0, r : r + 1, :] if r < 33 else dry[0:1],
        lambda r: dsides[1, r : r + 1, :] if r < 33 else dry[0:1],
        turned=True,
    )
    for dst, turned in ((north, False), (turned_north, True)):
        build_windows(
            dst, 1, lambda r: d_north, lambda r: dsides[0, 33:34, :], lambda r: dsides[1, 33:34, :], turned=turned
        )
    beyond = jnp.dot(
        jnp.where(top, north[...], turned_north[...]), wt_ref[jnp.where(top, 2, 0)], preferred_element_type=F32
    )
    inject = jnp.concatenate([inj_ref[...], inj_ref[...]], 0)
    for b in range(4):
        total = conv_rows(dwin, wt_ref, b * 512, 512, turned=True)
        for u in range(8):
            r = b * 8 + u
            value = total[u * 64 : u * 64 + 64]
            if r == 31:
                value = value + beyond
            back[r * 64 : r * 64 + 64, :] = (land[:, r : r + 1] * value).astype(BF)
        remap_ref[b * 512 : b * 512 + 512, :] = dot_back(back[b * 512 : b * 512 + 512, :], inject).astype(BF)
    for r in range(3):
        value = dot_rows(windows[(r + 1) * 64 : (r + 1) * 64 + 2048, :], deltas[...])
        put_half(core, keep_ref, send_ref, slice(r * 768, r * 768 + 768), value)
    tail = jnp.concatenate([dot_rows(rem_ref[...], back[...])[0:64], jnp.zeros((32, 256), F32)], 0)
    put_half(core, keep_ref, send_ref, slice(2304, 2400), tail)


def credit_rows_kernel(n_ref, s_ref, e_ref, w_ref, n_out, s_out):
    for r in range(2):
        for src, dst, first in ((n_ref, n_out, 16), (s_ref, s_out, 18)):
            dst[r] = src[r]
            dst[r, 0:2] = (src[r, 0:2].astype(F32) + w_ref[first + r].astype(F32)).astype(BF)
            dst[r, 62:64] = (src[r, 62:64].astype(F32) + e_ref[first + r].astype(F32)).astype(BF)


def atmos_back_kernel(
    flag_ref, x_ref, s_ref, n_ref, we_ref, ea_ref, act_ref, slope_ref, own_ref, cw_ref, ce_ref, cs_ref, cn_ref, bw_ref, be_ref,
    low_ref, p_ref, keep_ref, send_ref, windows, deltas, total, credit,
):
    core = flag_ref[1]
    atmos_windows(windows, x_ref, s_ref, n_ref, we_ref, ea_ref)
    maps = packed_maps(p_ref)
    for r in range(16):
        value = own_ref[r].astype(F32) + bw_ref[16 + r].astype(F32) + be_ref[16 + r].astype(F32) + low_ref[r].astype(F32)
        if r < 2:
            value += cs_ref[r].astype(F32)
        if r >= 14:
            value += cn_ref[r - 14].astype(F32)
        total[...] = value
        total[0:2, :] += cw_ref[r].astype(F32)
        total[62:64, :] += ce_ref[r].astype(F32)
        credit[r * 64 : r * 64 + 64, :] = total[...].astype(BF)
    for h in range(2):
        here = slice(h * 1024, h * 1024 + 1024)
        back = jnp.dot(credit[...], maps[h], preferred_element_type=F32)
        deltas[here, :] = (back * slope_ref[here, :].astype(F32)).astype(BF)
    for r in range(3):
        value = dot_rows(windows[r * 64 : r * 64 + 2048, :], deltas[...])
        put_half(core, keep_ref, send_ref, slice(r * 768, r * 768 + 768), value)
    lower = dot_rows(credit[...], act_ref[0:1024, :])
    upper = dot_rows(credit[...], act_ref[1024:2048, :])
    tail = jnp.concatenate([lower[0:64] + upper[64:128], jnp.zeros((32, 256), F32)], 0)
    put_half(core, keep_ref, send_ref, slice(2304, 2400), tail)


def exchange(x, mask):
    count = lax.axis_size("lon") * lax.axis_size("lat")
    return lax.ppermute(x, AXES, [(i, i ^ mask) for i in range(count)])


def reduce_streams(streams, orders):
    rank = lax.axis_index("lon") * lax.axis_size("lat") + lax.axis_index("lat")
    bit = lambda n: (rank >> n) & 1
    near = [(2, bit(1) ^ bit(2)), (8, bit(3) ^ bit(4)), (32, bit(5) ^ bit(6))]
    far = (6, 24, 96)
    count = range(len(streams))
    for level in range(3):
        steps = [near[orders[i][level]] for i in count]
        half = streams[0].shape[0] // 2
        keep = [lax.dynamic_slice_in_dim(streams[i], steps[i][1] * half, half) for i in count]
        send = [lax.dynamic_slice_in_dim(streams[i], (1 - steps[i][1]) * half, half).astype(BF) for i in count]
        streams = [keep[i] + exchange(send[i], steps[i][0]).astype(F32) for i in count]
    streams = [s.astype(BF) for s in streams]
    for level in range(3):
        got = [exchange(streams[i], far[orders[i][level]]) for i in count]
        streams = [(streams[i].astype(F32) + got[i].astype(F32)).astype(BF) for i in count]
    for level in (2, 1, 0):
        steps = [near[orders[i][level]] for i in count]
        got = [exchange(streams[i], steps[i][0]) for i in count]
        streams = [
            jnp.where(
                steps[i][1] == 0,
                jnp.concatenate([streams[i], got[i]]),
                jnp.concatenate([got[i], streams[i]]),
            )
            for i in count
        ]
    return streams


def lane_sign():
    lane = lax.broadcasted_iota(jnp.int32, (64, 128), 1)
    return jnp.where(lane < 64, jnp.float32(1.0), jnp.float32(-1.0))


def gather_kernel(
    flag_ref, slot_ref, w_ref, fn_ref, fs_ref, fw_ref, fe_ref, low_ref, own_ref, west_ref, east_ref, o_ref, m_ref, inj_ref,
    out_ref, mixed_ref, cols_ref, inner_ref, outer_ref, table, picked, cols,
):
    top = flag_ref[0]
    odd = flag_ref[1] != 0

    @pl.when(top == 0)
    def _():
        for r in range(20):
            rows = own_ref[r] if r < 16 else (fn_ref[r - 16] if r < 18 else fs_ref[r - 18])
            table[r * NEAR : r * NEAR + 64, :] = rows.astype(F32)
            table[r * NEAR + 64 : r * NEAR + 66, :] = fw_ref[r].astype(F32)
            table[r * NEAR + 66 : r * NEAR + 68, :] = fe_ref[r].astype(F32)

    @pl.when(top != 0)
    def _():
        for r in range(32):
            base = r * BAND
            table[base : base + 64, :] = (low_ref[r] if r < 16 else own_ref[r - 16]).astype(F32)
            table[base + 64 : base + 128, :] = west_ref[r].astype(F32)
            table[base + 128 : base + 192, :] = east_ref[r].astype(F32)

    def step(q, carry):
        base = pl.multiple_of(q * 64, 64)
        for u in range(64):
            at = slot_ref[q, u]
            picked[pl.ds(base + u, 1), :] = table[pl.ds(at, 1), :]
        return carry

    lax.fori_loop(0, 128, step, 0)
    sign = lane_sign()
    wt = w_ref[...].T
    for row in range(32):
        acc = jnp.zeros((64, 128), F32)
        for k in range(4):
            q = row * 4 + k
            factor = jnp.maximum(wt[:, q : q + 1] * sign, 0.0)
            acc = acc + factor * picked[q * 64 : q * 64 + 64, :]
        acc = acc + pltpu.roll(acc, 64, 1)
        out_ref[row * 64 : row * 64 + 64, :] = acc.astype(BF)
    land = m_ref[...].astype(F32).T
    inject = jnp.concatenate([inj_ref[...], jnp.zeros_like(inj_ref[...])], 0)
    for b in range(4):
        injected = jnp.dot(out_ref[b * 512 : b * 512 + 512, :], inject, preferred_element_type=F32)
        for u in range(8):
            r = b * 8 + u
            value = land[:, r : r + 1] * (o_ref[r].astype(F32) + injected[u * 64 : u * 64 + 64])
            mixed_ref[r] = value.astype(BF)
            for c, i in enumerate((0, 1, 62, 63)):
                cols[c, r : r + 1, :] = value[i : i + 1]
    for r in range(2):
        put_pair(odd, inner_ref, outer_ref, r, mixed_ref[r], mixed_ref[30 + r])
    cols_ref[...] = cols[...].astype(BF)


def scatter_kernel(
    top_ref, slot_ref, w_ref, g_ref, own_ref, n_ref, s_ref, w_out, e_out, low_ref, west_ref, east_ref, t0, t1, t2, t3, parts
):
    top = top_ref[0]
    tables = (t0, t1, t2, t3)

    def clear(count):
        def one(i, carry):
            base = pl.multiple_of(i * 96, 96)
            for t in tables:
                t[pl.ds(base, 96), :] = jnp.zeros((96, 128), F32)
            return carry

        lax.fori_loop(0, count // 96, one, 0)

    @pl.when(top == 0)
    def _():
        clear(20 * NEAR)

    @pl.when(top != 0)
    def _():
        clear(32 * BAND)

    sign = lane_sign()
    wt = w_ref[...].T
    for row in range(32):
        g = g_ref[row * 64 : row * 64 + 64, :].astype(F32)
        for k in range(4):
            q = row * 4 + k
            parts[q * 64 : q * 64 + 64, :] = jnp.maximum(wt[:, q : q + 1] * sign, 0.0) * g

    def step(row, carry):
        base = pl.multiple_of(row * 256, 256)
        for u in range(64):
            for k in range(4):
                at = slot_ref[row * 4 + k, u]
                t = tables[k]
                t[pl.ds(at, 1), :] = t[pl.ds(at, 1), :] + parts[pl.ds(base + k * 64 + u, 1), :]
        return carry

    lax.fori_loop(0, 32, step, 0)

    def total(start, size):
        where = pl.ds(start, size)
        return ((t0[where, :] + t1[where, :]) + (t2[where, :] + t3[where, :])).astype(BF)

    @pl.when(top == 0)
    def _():
        for r in range(20):
            rows = total(r * NEAR, 64)
            if r < 16:
                own_ref[r] = rows
            elif r < 18:
                n_ref[r - 16] = rows
            else:
                s_ref[r - 18] = rows
            w_out[r] = total(r * NEAR + 64, 2)
            e_out[r] = total(r * NEAR + 66, 2)

    @pl.when(top != 0)
    def _():
        for r in range(2):
            n_ref[r] = jnp.zeros((64, 128), BF)
            s_ref[r] = jnp.zeros((64, 128), BF)
        w_out[...] = jnp.zeros_like(w_out)
        e_out[...] = jnp.zeros_like(e_out)
        for r in range(32):
            base = r * BAND
            if r < 16:
                low_ref[r] = total(base, 64)
            else:
                own_ref[r - 16] = total(base, 64)
            west_ref[r] = total(base + 64, 64)
            east_ref[r] = total(base + 128, 64)


def band_lon(x, by):
    lons, lats = lax.axis_size("lon"), lax.axis_size("lat")
    return lax.ppermute(x, AXES, [(i * lats + lats - 1, ((i + by) % lons) * lats + lats - 1) for i in range(lons)])


def entry_slots(source_row, source_col, weight, is_top, row_count, col_count):
    nx = col_count * lax.axis_size("lon")
    row = source_row - lax.axis_index("lat") * row_count
    col = jnp.remainder(source_col - lax.axis_index("lon") * col_count + nx // 2, nx) - nx // 2
    half = row_count // 2
    inside = (row >= 0) & (row < row_count)
    wrapped = row & (row_count - 1)
    packed = wrapped & (half - 1)
    upper = wrapped >= half
    near_row = jnp.where(inside, packed, jnp.where(row < 0, packed + 4, packed + half))
    near_col = jnp.where((col >= 0) & (col < col_count), col, jnp.where(col < 0, col + col_count + 2, col + 2))
    band_row = jnp.where(row >= 0, packed + half, packed)
    band_col = jnp.where((col >= 0) & (col < col_count), col, jnp.where(col < 0, col + 2 * col_count, col + col_count))
    slot = jnp.where(is_top, band_row * BAND + band_col, near_row * NEAR + near_col)
    signed = jnp.where(upper, -weight, weight)
    order = lambda x: jnp.transpose(x, (0, 2, 1)).reshape(-1, col_count)
    return order(slot), order(signed)


def body(
    atmos_state,
    atmos_weights,
    flux_project,
    source_row,
    source_col,
    intersection_weight,
    ocean_state,
    flux_inject,
    ocean_mask,
    ocean_weights,
    out_cotangent,
):
    row_count, col_count, chans = atmos_state.shape
    flux_chans = flux_project.shape[1]
    cells = row_count * col_count
    half = cells // 2
    lats = lax.axis_size("lat")
    is_top = lax.axis_index("lat") == lats - 1
    core = lax.rem(lax.axis_index("lat"), 2)
    flags = jnp.stack([is_top.astype(jnp.int32), core])
    struct = lambda *shape: (shape, BF)
    block = lambda shape, at: pl.BlockSpec(shape, lambda i: (at[0], at[1], 0))
    row = (1, 64, 256)
    inner, outer = call(
        rows_kernel,
        "rows",
        (struct(2, 64, 256), struct(2, 64, 256)),
        (flags, atmos_state, atmos_state, out_cotangent, out_cotangent, ocean_mask),
        specs=[SMEM, block(row, (0, 0)), block(row, (31, 0)), block(row, (0, 0)), block(row, (31, 0)), VMEM],
        grid=(1,),
    )
    inner, outer = lat_pairs(inner, outer)
    slab = (32, 16, 256)
    first, last, south, north = call(
        edges_kernel,
        "edges",
        (struct(2, 34, 256), struct(2, 34, 256), struct(2, 64, 256), struct(2, 64, 256)),
        (flags, atmos_state, atmos_state, out_cotangent, out_cotangent, ocean_mask, inner, outer),
        [pltpu.VMEM((4, 34, 256), F32)],
        specs=[SMEM, block(slab, (0, 0)), block(slab, (0, 3)), block(slab, (0, 0)), block(slab, (0, 3))] + [VMEM] * 3,
        grid=(1,),
    )
    west = shifted(last, "lon", 1)
    east = shifted(first, "lon", -1)
    project = flux_project.T
    atmos_w = atmos_weights.reshape(3, 3 * chans, chans)
    ocean_w = ocean_weights.reshape(3, 3 * chans, chans)
    act, slope, own, flux_low, flux_high, first, last = call(
        atmos_kernel,
        "atmos",
        (struct(cells, chans), struct(cells, chans), struct(16, 64, 128), struct(2, 64, 128), struct(2, 64, 128),
         struct(16, 2, 128), struct(16, 2, 128)),
        (atmos_state, south, north, west, east, atmos_w, project),
        [pltpu.VMEM((34 * 64, 768), BF)],
    )
    low_tile = lax.ppermute(own, "lat", [(lats - 2, lats - 1)])
    flux_south = lax.ppermute(flux_high, "lat", [(i, i + 1) for i in range(lats - 2)])
    flux_north = passed_along(flux_low, "lat", -1)
    two = jnp.concatenate([low_tile, own], 0)
    band_west = band_lon(two, 1)
    band_east = band_lon(two, -1)
    flux_west = lon_below_band(jnp.concatenate([last, flux_north[:, -2:], flux_south[:, -2:]], 0), 1)
    flux_east = lon_below_band(jnp.concatenate([first, flux_north[:, :2], flux_south[:, :2]], 0), -1)
    late = lax.optimization_barrier((own, source_row, source_col, intersection_weight, ocean_weights))
    slots, signed = entry_slots(*late[1:4], is_top, row_count, col_count)
    back_w = jnp.transpose(late[4], (0, 2, 1)).reshape(3, 3 * chans, chans)
    remapped, mixed, cols, inner, outer = call(
        gather_kernel,
        "gather_mix",
        (struct(cells, 128), struct(32, 64, 256), struct(4, 32, 256), struct(2, 64, 256), struct(2, 64, 256)),
        (flags, slots, signed, flux_north, flux_south, flux_west, flux_east, low_tile, own, band_west, band_east,
         ocean_state, ocean_mask, flux_inject),
        [pltpu.VMEM((32 * BAND, 128), F32), pltpu.VMEM((8192, 128), F32), pltpu.VMEM((4, 32, 256), F32)],
        scalars=2,
    )
    inner, outer = lat_pairs(inner, outer)
    first, last, mixed_south, mixed_north = call(
        mixed_edges_kernel,
        "mixed_edges",
        (struct(2, 36, 256), struct(2, 36, 256), struct(2, 64, 256), struct(2, 64, 256)),
        (flags, cols, inner, outer),
        [pltpu.VMEM((4, 36, 256), F32)],
        scalars=1,
    )
    mixed_west = shifted(last, "lon", 1)
    mixed_east = shifted(first, "lon", -1)
    halves = ((GRAD_ROWS, 128), F32), ((GRAD_ROWS, 128), BF)
    ocean_out, remap_grad, ocean_keep, ocean_send = call(
        ocean_kernel,
        "ocean",
        (struct(32, 64, 256), struct(cells, 128)) + halves,
        (
            flags, mixed, mixed_south, mixed_north, first, last, mixed_west, mixed_east,
            out_cotangent, south, north, west, east, ocean_mask, remapped, ocean_w, back_w, flux_inject,
        ),
        [
            pltpu.VMEM((36 * 64, 768), BF),
            pltpu.VMEM((2, 48, 768), F32),
            pltpu.VMEM((64, 768), BF),
            pltpu.VMEM((64, 768), BF),
            pltpu.VMEM((cells, 256), BF),
            pltpu.VMEM((34 * 64, 768), BF),
            pltpu.VMEM((2, 40, 256), F32),
            pltpu.VMEM((cells, 256), BF),
        ],
        scalars=1,
    )
    own, to_north, to_south, to_west, to_east, low_tile, band_west, band_east = call(
        scatter_kernel,
        "scatter_rows",
        (struct(16, 64, 128), struct(2, 64, 128), struct(2, 64, 128), struct(20, 2, 128), struct(20, 2, 128),
         struct(16, 64, 128), struct(32, 64, 128), struct(32, 64, 128)),
        (flags, slots, signed, remap_grad),
        [pltpu.VMEM((32 * BAND, 128), F32)] * 4 + [pltpu.VMEM((8192, 128), F32)],
        scalars=2,
    )
    band_from_east = band_lon(band_west, -1)
    band_from_west = band_lon(band_east, 1)
    from_east = lon_below_band(to_west, -1)
    from_west = lon_below_band(to_east, 1)
    to_north, to_south = call(
        credit_rows_kernel, "credit_rows", (struct(2, 64, 128),) * 2, (to_north, to_south, from_east, from_west)
    )
    low_tile = low_tile.astype(F32) + band_from_east[:16].astype(F32) + band_from_west[:16].astype(F32)
    from_south = passed_along(to_north, "lat", 1)
    from_north = lax.ppermute(to_south, "lat", [(i, i - 1) for i in range(1, lats - 1)])
    from_band = lax.ppermute(low_tile.astype(BF), "lat", [(lats - 1, lats - 2)])
    atmos_keep, atmos_send = call(
        atmos_back_kernel,
        "atmos_back",
        halves,
        (flags, atmos_state, south, north, west, east, act, slope, own, from_west, from_east, from_south, from_north,
         band_from_west, band_from_east, from_band, project),
        [pltpu.VMEM((34 * 64, 768), BF), pltpu.VMEM((cells, 256), BF), pltpu.VMEM((64, 128), F32), pltpu.VMEM((half, 128), BF)],
        scalars=1,
    )
    ocean_keep, ocean_send, atmos_keep, atmos_send = lax.optimization_barrier(
        (ocean_keep, ocean_send, atmos_keep, atmos_send)
    )
    ocean = ocean_keep + exchange(ocean_send, 1).astype(F32)
    atmos = atmos_keep + exchange(atmos_send, 1).astype(F32)
    cut = 1600
    rest = GRAD_ROWS - cut
    sums = reduce_streams(
        [ocean[:cut], jnp.concatenate([ocean[cut:], atmos[:rest]]), atmos[rest:]], ((0, 1, 2), (1, 2, 0), (2, 0, 1))
    )
    ocean = jnp.concatenate([sums[0], sums[1][:rest]])
    atmos = jnp.concatenate([sums[1][rest:], sums[2]])

    def joined(mine):
        other = exchange(mine, 1)
        pair = jnp.concatenate([jnp.where(core == 0, mine, other), jnp.where(core == 0, other, mine)], 1).astype(F32)
        return pair[: 9 * chans].reshape(9, chans, chans), pair[9 * chans : 9 * chans + flux_chans]

    grad_ocean, grad_inject = joined(ocean)
    grad_atmos, grad_project = joined(atmos)
    return (ocean_out, grad_atmos, grad_ocean, grad_project.T, grad_inject)


def solution(mesh):
    return jax.shard_map(
        body,
        mesh=mesh,
        in_specs=(
            P("lat", "lon", None),
            P(),
            P(),
            P("lat", "lon", None),
            P("lat", "lon", None),
            P("lat", "lon", None),
            P("lat", "lon", None),
            P(),
            P("lat", "lon"),
            P(),
            P("lat", "lon", None),
        ),
        out_specs=(P("lat", "lon", None), P(), P(), P(), P()),
        check_vma=False,
    )
```

```python
import jax
import jax.numpy as jnp
from jax import lax
from jax.experimental import pallas as pl
from jax.experimental.pallas import tpu as pltpu
from jax.sharding import PartitionSpec as P

BF = jnp.bfloat16
F32 = jnp.float32
VLIM = 56 << 20
AXES = ("lon", "lat")
NEAR = 72
BAND = 192


def lat_pairs(inner, outer, fold):
    lons, lats = lax.axis_size("lon"), lax.axis_size("lat")
    at = lambda i, j: i * lats + j
    inside = [(at(i, j), at(i, j ^ 1)) for i in range(lons) for j in range(lats)]
    across = [(at(i, j), at(i, j + 1 if j % 2 else j - 1)) for i in range(lons) for j in range(1, lats - 1)]
    if fold:
        across += [(at(i, lats - 1), at(lons - 1 - i, lats - 1)) for i in range(lons)]
    return lax.ppermute(inner, AXES, inside), lax.ppermute(outer, AXES, across)


def lon_pairs(inner, outer, first=0, last=None):
    lons, lats = lax.axis_size("lon"), lax.axis_size("lat")
    here = range(first, lats if last is None else last)
    inside = [(i * lats + j, (i ^ 1) * lats + j) for i in range(lons) for j in here]
    across = [(i * lats + j, ((i + 1 if i % 2 else i - 1) % lons) * lats + j) for i in range(lons) for j in here]
    return lax.ppermute(inner, AXES, inside), lax.ppermute(outer, AXES, across)


def sigmoid(value):
    return 1.0 / (1.0 + jnp.exp(-value))


def silu_slope(value, sigma):
    return sigma * (1.0 + value * (1.0 - sigma))


VMEM = pl.BlockSpec(memory_space=pltpu.VMEM)
SMEM = pl.BlockSpec(memory_space=pltpu.SMEM)
PARAMS = pltpu.CompilerParams(vmem_limit_bytes=VLIM)
GRAD_ROWS = 2400


def call(kernel, name, outs, ins, scratch=(), scalars=0, specs=None, grid=None):
    if specs is None:
        specs = [SMEM] * scalars + [VMEM] * (len(ins) - scalars)
    extra = {} if grid is None else {"grid": grid}
    return pl.pallas_call(
        kernel,
        name=name,
        out_shape=tuple(jax.ShapeDtypeStruct(shape, kind) for shape, kind in outs),
        in_specs=specs,
        out_specs=(VMEM,) * len(outs),
        scratch_shapes=list(scratch),
        compiler_params=PARAMS,
        **extra,
    )(*ins)


def turned_row(row):
    a = lax.broadcasted_iota(jnp.int32, (64, 64), 0)
    b = lax.broadcasted_iota(jnp.int32, (64, 64), 1)
    flip = jnp.where(a + b == 63, jnp.float32(1.0), jnp.float32(0.0)).astype(BF)
    return jnp.dot(flip, row, preferred_element_type=F32)


def build_windows(dst, rows, row_of, west_of, east_of, turned=False):
    first, last = (512, 0) if turned else (0, 512)
    at = lax.broadcasted_iota(jnp.int32, (64, 256), 0)
    for r in range(rows):
        value = row_of(r)
        wide = value.astype(F32)
        left = jnp.where(at == 0, west_of(r).astype(F32), pltpu.roll(wide, 1, 0))
        right = jnp.where(at == 63, east_of(r).astype(F32), pltpu.roll(wide, 63, 0))
        here = slice(r * 64, r * 64 + 64)
        dst[here, first : first + 256] = left.astype(BF)
        dst[here, 256:512] = value
        dst[here, last : last + 256] = right.astype(BF)


def conv_rows(windows, w, start, count, turned=False):
    acc = jnp.zeros((count, 256), F32)
    for r in range(3):
        taps = w[2 - r if turned else r]
        acc += jnp.dot(windows[start + r * 64 : start + r * 64 + count, :], taps, preferred_element_type=F32)
    return acc


def dot_back(a, b):
    return lax.dot_general(a, b, (((1,), (1,)), ((), ())), preferred_element_type=F32)


def turned_lanes(x):
    return jnp.concatenate([x[:, 512:768], x[:, 256:512], x[:, 0:256]], 1)


def put_half(core, keep_ref, send_ref, here, value):
    low, high = value[:, 0:128], value[:, 128:256]
    keep_ref[here, :] = jnp.where(core == 0, low, high)
    send_ref[here, :] = jnp.where(core == 0, high, low).astype(BF)


def dot_rows(a, b):
    return lax.dot_general(a, b, (((0,), (0,)), ((), ())), preferred_element_type=F32)


def put_pair(odd, inner_ref, outer_ref, r, low, high):
    inner_ref[r] = jnp.where(odd, low, high)
    outer_ref[r] = jnp.where(odd, high, low)


def rows_kernel(flag_ref, a0_ref, a1_ref, c0_ref, c1_ref, m_ref, inner_ref, outer_ref):
    odd = flag_ref[1] != 0
    land = m_ref[...].astype(F32).T
    put_pair(odd, inner_ref, outer_ref, 0, a0_ref[0], a1_ref[0])
    low = (c0_ref[0].astype(F32) * land[:, 0:1]).astype(BF)
    high = (c1_ref[0].astype(F32) * land[:, 31:32]).astype(BF)
    put_pair(odd, inner_ref, outer_ref, 1, low, high)


def edges_kernel(
    flag_ref, a0_ref, a1_ref, c0_ref, c1_ref, m_ref, inner_ref, outer_ref, inner_out, outer_out, s_ref, n_ref, cols
):
    top, odd = flag_ref[0] != 0, flag_ref[1] != 0
    land = m_ref[...].astype(F32).T
    for r in range(2):
        s_ref[r] = jnp.where(odd, inner_ref[r], outer_ref[r])
    north = jnp.where(odd, outer_ref[0], inner_ref[0]).astype(F32)
    north = jnp.where(top, jnp.zeros_like(north), north)
    cn = jnp.where(odd, outer_ref[1], inner_ref[1])
    cn = jnp.where(top, turned_row(cn), cn.astype(F32))
    n_ref[0], n_ref[1] = north.astype(BF), cn.astype(BF)
    for r in range(32):
        here = slice(r + 1, r + 2)
        cols[0, here, :] = a0_ref[r, 0:1].astype(F32)
        cols[1, here, :] = c0_ref[r, 0:1].astype(F32) * land[0:1, r : r + 1]
        cols[2, here, :] = a1_ref[r, 15:16].astype(F32)
        cols[3, here, :] = c1_ref[r, 15:16].astype(F32) * land[63:64, r : r + 1]
    for k, (row, i) in enumerate(((s_ref[0], 0), (s_ref[1], 0), (s_ref[0], 63), (s_ref[1], 63))):
        cols[k, 0:1, :] = row[i : i + 1].astype(F32)
    for k, (row, i) in enumerate(((north, 0), (cn, 0), (north, 63), (cn, 63))):
        cols[k, 33:34, :] = row[i : i + 1]
    put_pair(flag_ref[2] != 0, inner_out, outer_out, slice(0, 2), cols[0:2].astype(BF), cols[2:4].astype(BF))


def mixed_edges_kernel(
    flag_ref, cols_in, inner_ref, outer_ref, inner_out, outer_out, first_ref, last_ref, south_ref, north_ref, cols
):
    top, odd = flag_ref[0] != 0, flag_ref[1] != 0
    for r in range(2):
        south_ref[r] = jnp.where(odd, inner_ref[r], outer_ref[r])
        s = south_ref[r].astype(F32)
        n = jnp.where(odd, outer_ref[r], inner_ref[r]).astype(F32)
        n = jnp.where(top, turned_row(outer_ref[1 - r]), n)
        north_ref[r] = n.astype(BF)
        for k, i in enumerate((0, 1, 62, 63)):
            cols[k, r : r + 1, :] = s[i : i + 1]
            cols[k, 34 + r : 35 + r, :] = n[i : i + 1]
    for k in range(4):
        cols[k, 2:34, :] = cols_in[k].astype(F32)
    first_ref[...] = cols[0].astype(BF)
    last_ref[...] = cols[3].astype(BF)
    put_pair(flag_ref[2] != 0, inner_out, outer_out, slice(0, 2), cols[0:2].astype(BF), cols[2:4].astype(BF))


def flux_edges_kernel(flag_ref, first_ref, last_ref, inner_ref, outer_ref, south_ref, north_ref, inner_out, outer_out):
    odd, east_odd = flag_ref[1] != 0, flag_ref[2] != 0
    for r in range(20):
        if r < 16:
            first, last = first_ref[r], last_ref[r]
        else:
            a, b = (inner_ref, outer_ref) if r >= 18 else (outer_ref, inner_ref)
            row = jnp.where(odd, a[r % 2], b[r % 2])
            (north_ref if r < 18 else south_ref)[r % 2] = row
            first, last = row[0:2], row[62:64]
        put_pair(east_odd, inner_out, outer_out, r, first, last)


def atmos_windows(flag_ref, windows, x_ref, s_ref, n_ref, in_ref, out_ref):
    odd = flag_ref[2] != 0
    west = jnp.where(odd, in_ref[0].astype(F32), out_ref[0].astype(F32))
    east = jnp.where(odd, out_ref[0].astype(F32), in_ref[0].astype(F32))
    build_windows(
        windows,
        34,
        lambda r: s_ref[0] if r == 0 else (n_ref[0] if r == 33 else x_ref[r - 1]),
        lambda r: west[r : r + 1, :],
        lambda r: east[r : r + 1, :],
    )


def packed_maps(p_ref):
    p = p_ref[...]
    zeros = jnp.zeros_like(p)
    return jnp.concatenate([p, zeros], 0), jnp.concatenate([zeros, p], 0)


def atmos_kernel(
    flag_ref, x_ref, s_ref, n_ref, in_ref, out_ref, w_ref, p_ref,
    act_ref, slope_ref, own_ref, inner_out, outer_out, first_ref, last_ref, windows,
):
    atmos_windows(flag_ref, windows, x_ref, s_ref, n_ref, in_ref, out_ref)
    maps = packed_maps(p_ref)
    for b in range(2):
        packed = jnp.zeros((512, 128), F32)
        for h in range(2):
            start = h * 1024 + b * 512
            pre = conv_rows(windows, w_ref, start, 512)
            sigma = sigmoid(pre)
            act = (pre * sigma).astype(BF)
            act_ref[start : start + 512, :] = act
            slope_ref[start : start + 512, :] = silu_slope(pre, sigma).astype(BF)
            packed += dot_back(act, maps[h])
        for u in range(8):
            r = b * 8 + u
            row = packed[u * 64 : u * 64 + 64].astype(BF)
            own_ref[r] = row
            first_ref[r] = row[0:2]
            last_ref[r] = row[62:64]
    for r in range(2):
        put_pair(flag_ref[1] != 0, inner_out, outer_out, r, own_ref[r], own_ref[14 + r])


def ocean_kernel(
    flag_ref, x_ref, s_ref, n_ref, first_ref, last_ref, in_ref, beyond_ref, c_ref, cs_ref, cn_ref, ci_ref, co_ref, m_ref, rem_ref,
    w_ref, wt_ref, inj_ref, out_ref, remap_ref, keep_ref, send_ref,
    windows, sides, north, turned_north, deltas, dwin, dsides, back,
):
    top, core, odd = flag_ref[0] != 0, flag_ref[1], flag_ref[2] != 0
    west = [jnp.where(odd, in_ref[k].astype(F32), beyond_ref[k].astype(F32)) for k in range(2)]
    east = [jnp.where(odd, beyond_ref[k].astype(F32), in_ref[k].astype(F32)) for k in range(2)]
    cot_west = jnp.where(odd, ci_ref[1].astype(F32), co_ref[1].astype(F32))
    cot_east = jnp.where(odd, co_ref[1].astype(F32), ci_ref[1].astype(F32))
    land = m_ref[...].astype(F32).T
    build_windows(
        windows,
        36,
        lambda r: s_ref[r] if r < 2 else (n_ref[r - 34] if r >= 34 else x_ref[r - 2]),
        lambda r: west[1][r : r + 1, :],
        lambda r: east[0][r : r + 1, :],
    )
    sides[...] = jnp.zeros_like(sides)
    for side, columns in ((0, (west[0], west[1], first_ref[...])), (1, (last_ref[...], east[0], east[1]))):
        for q in range(3):
            sides[side, 0:36, q * 256 : q * 256 + 256] = columns[q].astype(F32)

    def side_rows(start, count):
        return jnp.concatenate([sides[0, start : start + count, :], sides[1, start : start + count, :]], 0).astype(BF)

    pre = jnp.zeros((80, 256), F32)
    lines = [jnp.concatenate([windows[(33 + r) * 64 : (34 + r) * 64, :], side_rows(33 + r, 8)], 0) for r in range(3)]
    for r in range(3):
        pre += jnp.dot(jnp.where(top, turned_lanes(lines[2 - r]), lines[r]), w_ref[r], preferred_element_type=F32)
    slope = silu_slope(pre, sigmoid(pre))
    d_north = (cn_ref[1].astype(F32) * slope[0:64]).astype(BF)
    side_pre = jnp.zeros((80, 256), F32)
    for r in range(3):
        side_pre += jnp.dot(side_rows(r, 40), w_ref[r], preferred_element_type=F32)
    side_slope = silu_slope(side_pre, sigmoid(side_pre))
    at = lax.broadcasted_iota(jnp.int32, (40, 256), 0)
    for side, cot in ((0, cot_west), (1, cot_east)):
        corner = slope[64 + side * 8 : 65 + side * 8]
        here = jnp.where(at == 33, corner, side_slope[side * 40 : side * 40 + 40])
        dsides[side] = jnp.zeros((40, 256), F32)
        dsides[side, 0:34, :] = cot * here[0:34]
    pre = conv_rows(windows, w_ref, 0, 64)
    d_south = (cs_ref[1].astype(F32) * silu_slope(pre, sigmoid(pre))).astype(BF)
    for b in range(4):
        pre = conv_rows(windows, w_ref, 64 + b * 512, 512)
        sigma = sigmoid(pre)
        act = pre * sigma
        slope = silu_slope(pre, sigma)
        for u in range(8):
            r = b * 8 + u
            here = slice(u * 64, u * 64 + 64)
            wet = land[:, r : r + 1]
            out_ref[r] = (wet * act[here]).astype(BF)
            deltas[r * 64 : r * 64 + 64, :] = (c_ref[r].astype(F32) * wet * slope[here]).astype(BF)
    dry = jnp.zeros((64, 256), BF)
    build_windows(
        dwin,
        34,
        lambda r: d_south if r == 0 else (dry if r == 33 else deltas[r * 64 - 64 : r * 64, :]),
        lambda r: dsides[0, r : r + 1, :] if r < 33 else dry[0:1],
        lambda r: dsides[1, r : r + 1, :] if r < 33 else dry[0:1],
        turned=True,
    )
    for dst, turned in ((north, False), (turned_north, True)):
        build_windows(
            dst, 1, lambda r: d_north, lambda r: dsides[0, 33:34, :], lambda r: dsides[1, 33:34, :], turned=turned
        )
    beyond = jnp.dot(
        jnp.where(top, north[...], turned_north[...]), wt_ref[jnp.where(top, 2, 0)], preferred_element_type=F32
    )
    inject = jnp.concatenate([inj_ref[...], inj_ref[...]], 0)
    for b in range(4):
        total = conv_rows(dwin, wt_ref, b * 512, 512, turned=True)
        for u in range(8):
            r = b * 8 + u
            value = total[u * 64 : u * 64 + 64]
            if r == 31:
                value = value + beyond
            back[r * 64 : r * 64 + 64, :] = (land[:, r : r + 1] * value).astype(BF)
        remap_ref[b * 512 : b * 512 + 512, :] = dot_back(back[b * 512 : b * 512 + 512, :], inject).astype(BF)
    for r in range(3):
        value = dot_rows(windows[(r + 1) * 64 : (r + 1) * 64 + 2048, :], deltas[...])
        put_half(core, keep_ref, send_ref, slice(r * 768, r * 768 + 768), value)
    tail = jnp.concatenate([dot_rows(rem_ref[...], back[...])[0:64], jnp.zeros((32, 256), F32)], 0)
    put_half(core, keep_ref, send_ref, slice(2304, 2400), tail)


def credit_rows_kernel(flag_ref, n_ref, s_ref, in_ref, out_ref, inner_out, outer_out, n_sum, s_sum):
    odd, east_odd = flag_ref[1] != 0, flag_ref[2] != 0
    for r in range(2):
        for src, dst, first in ((n_ref, n_sum, 16), (s_ref, s_sum, 18)):
            inner, outer = in_ref[first + r].astype(F32), out_ref[first + r].astype(F32)
            dst[r] = src[r].astype(F32)
            dst[r, 0:2] = dst[r, 0:2] + jnp.where(east_odd, inner, outer)
            dst[r, 62:64] = dst[r, 62:64] + jnp.where(east_odd, outer, inner)
        put_pair(odd, inner_out, outer_out, r, s_sum[r].astype(BF), n_sum[r].astype(BF))


def atmos_back_kernel(
    flag_ref, x_ref, s_ref, n_ref, in_ref, out_ref, act_ref, slope_ref, own_ref, ci_ref, co_ref, ri_ref, ro_ref, bi_ref, bo_ref,
    low_ref, p_ref, keep_ref, send_ref, windows, deltas, total, credit,
):
    core = flag_ref[1]
    odd, east_odd = core != 0, flag_ref[2] != 0
    atmos_windows(flag_ref, windows, x_ref, s_ref, n_ref, in_ref, out_ref)
    maps = packed_maps(p_ref)
    for r in range(16):
        value = own_ref[r].astype(F32) + bi_ref[16 + r].astype(F32) + bo_ref[16 + r].astype(F32) + low_ref[r].astype(F32)
        if r < 2:
            value += jnp.where(odd, ri_ref[r].astype(F32), ro_ref[r].astype(F32))
        if r >= 14:
            value += jnp.where(odd, ro_ref[r - 14].astype(F32), ri_ref[r - 14].astype(F32))
        total[...] = value
        inner, outer = ci_ref[r].astype(F32), co_ref[r].astype(F32)
        total[0:2, :] += jnp.where(east_odd, inner, outer)
        total[62:64, :] += jnp.where(east_odd, outer, inner)
        credit[r * 64 : r * 64 + 64, :] = total[...].astype(BF)
    for h in range(2):
        here = slice(h * 1024, h * 1024 + 1024)
        back = jnp.dot(credit[...], maps[h], preferred_element_type=F32)
        deltas[here, :] = (back * slope_ref[here, :].astype(F32)).astype(BF)
    for r in range(3):
        value = dot_rows(windows[r * 64 : r * 64 + 2048, :], deltas[...])
        put_half(core, keep_ref, send_ref, slice(r * 768, r * 768 + 768), value)
    lower = dot_rows(credit[...], act_ref[0:1024, :])
    upper = dot_rows(credit[...], act_ref[1024:2048, :])
    tail = jnp.concatenate([lower[0:64] + upper[64:128], jnp.zeros((32, 256), F32)], 0)
    put_half(core, keep_ref, send_ref, slice(2304, 2400), tail)


def exchange(x, mask):
    count = lax.axis_size("lon") * lax.axis_size("lat")
    return lax.ppermute(x, AXES, [(i, i ^ mask) for i in range(count)])


def reduce_streams(streams, orders):
    rank = lax.axis_index("lon") * lax.axis_size("lat") + lax.axis_index("lat")
    bit = lambda n: (rank >> n) & 1
    near = [(2, bit(1) ^ bit(2)), (8, bit(3) ^ bit(4)), (32, bit(5) ^ bit(6))]
    far = (6, 24, 96)
    count = range(len(streams))
    for level in range(3):
        steps = [near[orders[i][level]] for i in count]
        half = streams[0].shape[0] // 2
        keep = [lax.dynamic_slice_in_dim(streams[i], steps[i][1] * half, half) for i in count]
        send = [lax.dynamic_slice_in_dim(streams[i], (1 - steps[i][1]) * half, half).astype(BF) for i in count]
        streams = [keep[i] + exchange(send[i], steps[i][0]).astype(F32) for i in count]
    streams = [s.astype(BF) for s in streams]
    for level in range(3):
        got = [exchange(streams[i], far[orders[i][level]]) for i in count]
        streams = [(streams[i].astype(F32) + got[i].astype(F32)).astype(BF) for i in count]
    for level in (2, 1, 0):
        steps = [near[orders[i][level]] for i in count]
        got = [exchange(streams[i], steps[i][0]) for i in count]
        streams = [
            jnp.where(
                steps[i][1] == 0,
                jnp.concatenate([streams[i], got[i]]),
                jnp.concatenate([got[i], streams[i]]),
            )
            for i in count
        ]
    return streams


def lane_sign():
    lane = lax.broadcasted_iota(jnp.int32, (64, 128), 1)
    return jnp.where(lane < 64, jnp.float32(1.0), jnp.float32(-1.0))


def gather_kernel(
    flag_ref, slot_ref, w_ref, fn_ref, fs_ref, fi_ref, fo_ref, low_ref, own_ref, bi_ref, bo_ref, o_ref, m_ref, inj_ref,
    out_ref, mixed_ref, cols_ref, inner_ref, outer_ref, table, picked, cols,
):
    top = flag_ref[0]
    odd, east_odd = flag_ref[1] != 0, flag_ref[2] != 0

    @pl.when(top == 0)
    def _():
        for r in range(20):
            rows = own_ref[r] if r < 16 else (fn_ref[r - 16] if r < 18 else fs_ref[r - 18])
            table[r * NEAR : r * NEAR + 64, :] = rows.astype(F32)
            table[r * NEAR + 64 : r * NEAR + 66, :] = jnp.where(east_odd, fi_ref[r].astype(F32), fo_ref[r].astype(F32))
            table[r * NEAR + 66 : r * NEAR + 68, :] = jnp.where(east_odd, fo_ref[r].astype(F32), fi_ref[r].astype(F32))

    @pl.when(top != 0)
    def _():
        for r in range(32):
            base = r * BAND
            table[base : base + 64, :] = (low_ref[r] if r < 16 else own_ref[r - 16]).astype(F32)
            inner, outer = bi_ref[r].astype(F32), bo_ref[r].astype(F32)
            table[base + 64 : base + 128, :] = jnp.where(east_odd, inner, outer)
            table[base + 128 : base + 192, :] = jnp.where(east_odd, outer, inner)

    def step(q, carry):
        base = pl.multiple_of(q * 64, 64)
        for u in range(64):
            at = slot_ref[q, u]
            picked[pl.ds(base + u, 1), :] = table[pl.ds(at, 1), :]
        return carry

    lax.fori_loop(0, 128, step, 0)
    sign = lane_sign()
    wt = w_ref[...].T
    for row in range(32):
        acc = jnp.zeros((64, 128), F32)
        for k in range(4):
            q = row * 4 + k
            factor = jnp.maximum(wt[:, q : q + 1] * sign, 0.0)
            acc = acc + factor * picked[q * 64 : q * 64 + 64, :]
        acc = acc + pltpu.roll(acc, 64, 1)
        out_ref[row * 64 : row * 64 + 64, :] = acc.astype(BF)
    land = m_ref[...].astype(F32).T
    inject = jnp.concatenate([inj_ref[...], jnp.zeros_like(inj_ref[...])], 0)
    for b in range(4):
        injected = jnp.dot(out_ref[b * 512 : b * 512 + 512, :], inject, preferred_element_type=F32)
        for u in range(8):
            r = b * 8 + u
            value = land[:, r : r + 1] * (o_ref[r].astype(F32) + injected[u * 64 : u * 64 + 64])
            mixed_ref[r] = value.astype(BF)
            for c, i in enumerate((0, 1, 62, 63)):
                cols[c, r : r + 1, :] = value[i : i + 1]
    for r in range(2):
        put_pair(odd, inner_ref, outer_ref, r, mixed_ref[r], mixed_ref[30 + r])
    cols_ref[...] = cols[...].astype(BF)


def scatter_kernel(
    flag_ref, slot_ref, w_ref, g_ref, own_ref, n_ref, s_ref, side_in, side_out, low_ref, band_in, band_out, t0, t1, t2, t3, parts
):
    top = flag_ref[0]
    east_odd = flag_ref[2] != 0
    tables = (t0, t1, t2, t3)

    def clear(count):
        def one(i, carry):
            base = pl.multiple_of(i * 96, 96)
            for t in tables:
                t[pl.ds(base, 96), :] = jnp.zeros((96, 128), F32)
            return carry

        lax.fori_loop(0, count // 96, one, 0)

    @pl.when(top == 0)
    def _():
        clear(20 * NEAR)

    @pl.when(top != 0)
    def _():
        clear(32 * BAND)

    sign = lane_sign()
    wt = w_ref[...].T
    for row in range(32):
        g = g_ref[row * 64 : row * 64 + 64, :].astype(F32)
        for k in range(4):
            q = row * 4 + k
            parts[q * 64 : q * 64 + 64, :] = jnp.maximum(wt[:, q : q + 1] * sign, 0.0) * g

    def step(row, carry):
        base = pl.multiple_of(row * 256, 256)
        for u in range(64):
            for k in range(4):
                at = slot_ref[row * 4 + k, u]
                t = tables[k]
                t[pl.ds(at, 1), :] = t[pl.ds(at, 1), :] + parts[pl.ds(base + k * 64 + u, 1), :]
        return carry

    lax.fori_loop(0, 32, step, 0)

    def total(start, size):
        where = pl.ds(start, size)
        return ((t0[where, :] + t1[where, :]) + (t2[where, :] + t3[where, :])).astype(BF)

    @pl.when(top == 0)
    def _():
        for r in range(20):
            rows = total(r * NEAR, 64)
            if r < 16:
                own_ref[r] = rows
            elif r < 18:
                n_ref[r - 16] = rows
            else:
                s_ref[r - 18] = rows
            put_pair(east_odd, side_in, side_out, r, total(r * NEAR + 64, 2), total(r * NEAR + 66, 2))

    @pl.when(top != 0)
    def _():
        for r in range(2):
            n_ref[r] = jnp.zeros((64, 128), BF)
            s_ref[r] = jnp.zeros((64, 128), BF)
        side_in[...] = jnp.zeros_like(side_in)
        side_out[...] = jnp.zeros_like(side_out)
        for r in range(32):
            base = r * BAND
            if r < 16:
                low_ref[r] = total(base, 64)
            else:
                own_ref[r - 16] = total(base, 64)
            put_pair(east_odd, band_in, band_out, r, total(base + 64, 64), total(base + 128, 64))


def entry_slots(source_row, source_col, weight, is_top, row_count, col_count):
    nx = col_count * lax.axis_size("lon")
    row = source_row - lax.axis_index("lat") * row_count
    col = jnp.remainder(source_col - lax.axis_index("lon") * col_count + nx // 2, nx) - nx // 2
    half = row_count // 2
    inside = (row >= 0) & (row < row_count)
    wrapped = row & (row_count - 1)
    packed = wrapped & (half - 1)
    upper = wrapped >= half
    near_row = jnp.where(inside, packed, jnp.where(row < 0, packed + 4, packed + half))
    near_col = jnp.where((col >= 0) & (col < col_count), col, jnp.where(col < 0, col + col_count + 2, col + 2))
    band_row = jnp.where(row >= 0, packed + half, packed)
    band_col = jnp.where((col >= 0) & (col < col_count), col, jnp.where(col < 0, col + 2 * col_count, col + col_count))
    slot = jnp.where(is_top, band_row * BAND + band_col, near_row * NEAR + near_col)
    signed = jnp.where(upper, -weight, weight)
    order = lambda x: jnp.transpose(x, (0, 2, 1)).reshape(-1, col_count)
    return order(slot), order(signed)


def body(
    atmos_state,
    atmos_weights,
    flux_project,
    source_row,
    source_col,
    intersection_weight,
    ocean_state,
    flux_inject,
    ocean_mask,
    ocean_weights,
    out_cotangent,
):
    row_count, col_count, chans = atmos_state.shape
    flux_chans = flux_project.shape[1]
    cells = row_count * col_count
    half = cells // 2
    lats = lax.axis_size("lat")
    is_top = lax.axis_index("lat") == lats - 1
    core = lax.rem(lax.axis_index("lat"), 2)
    flags = jnp.stack([is_top.astype(jnp.int32), core, lax.rem(lax.axis_index("lon"), 2)])
    struct = lambda *shape: (shape, BF)
    block = lambda shape, at: pl.BlockSpec(shape, lambda i: (at[0], at[1], 0))
    row = (1, 64, 256)
    inner, outer = call(
        rows_kernel,
        "rows",
        (struct(2, 64, 256), struct(2, 64, 256)),
        (flags, atmos_state, atmos_state, out_cotangent, out_cotangent, ocean_mask),
        specs=[SMEM, block(row, (0, 0)), block(row, (31, 0)), block(row, (0, 0)), block(row, (31, 0)), VMEM],
        grid=(1,),
    )
    inner, outer = lat_pairs(inner, outer, True)
    slab = (32, 16, 256)
    inner, outer, south, north = call(
        edges_kernel,
        "edges",
        (struct(2, 34, 256), struct(2, 34, 256), struct(2, 64, 256), struct(2, 64, 256)),
        (flags, atmos_state, atmos_state, out_cotangent, out_cotangent, ocean_mask, inner, outer),
        [pltpu.VMEM((4, 34, 256), F32)],
        specs=[SMEM, block(slab, (0, 0)), block(slab, (0, 3)), block(slab, (0, 0)), block(slab, (0, 3))] + [VMEM] * 3,
        grid=(1,),
    )
    side_in, side_out = lon_pairs(inner, outer)
    project = flux_project.T
    atmos_w = atmos_weights.reshape(3, 3 * chans, chans)
    ocean_w = ocean_weights.reshape(3, 3 * chans, chans)
    act, slope, own, inner, outer, first, last = call(
        atmos_kernel,
        "atmos",
        (struct(cells, chans), struct(cells, chans), struct(16, 64, 128), struct(2, 64, 128), struct(2, 64, 128),
         struct(16, 2, 128), struct(16, 2, 128)),
        (flags, atmos_state, south, north, side_in, side_out, atmos_w, project),
        [pltpu.VMEM((34 * 64, 768), BF)],
        scalars=1,
    )
    low_tile = lax.ppermute(own, "lat", [(lats - 2, lats - 1)])
    two = jnp.concatenate([low_tile, own], 0)
    band_in, band_out = lon_pairs(two, two, lats - 1)
    inner, outer = lat_pairs(inner, outer, False)
    flux_south, flux_north, inner, outer = call(
        flux_edges_kernel,
        "flux_edges",
        (struct(2, 64, 128), struct(2, 64, 128), struct(20, 2, 128), struct(20, 2, 128)),
        (flags, first, last, inner, outer),
        scalars=1,
    )
    flux_in, flux_out = lon_pairs(inner, outer, 0, lats - 1)
    late = lax.optimization_barrier((own, source_row, source_col, intersection_weight, ocean_weights))
    slots, signed = entry_slots(*late[1:4], is_top, row_count, col_count)
    back_w = jnp.transpose(late[4], (0, 2, 1)).reshape(3, 3 * chans, chans)
    remapped, mixed, cols, inner, outer = call(
        gather_kernel,
        "gather_mix",
        (struct(cells, 128), struct(32, 64, 256), struct(4, 32, 256), struct(2, 64, 256), struct(2, 64, 256)),
        (flags, slots, signed, flux_north, flux_south, flux_in, flux_out, low_tile, own, band_in, band_out,
         ocean_state, ocean_mask, flux_inject),
        [pltpu.VMEM((32 * BAND, 128), F32), pltpu.VMEM((8192, 128), F32), pltpu.VMEM((4, 32, 256), F32)],
        scalars=2,
    )
    inner, outer = lat_pairs(inner, outer, True)
    inner, outer, first, last, mixed_south, mixed_north = call(
        mixed_edges_kernel,
        "mixed_edges",
        (struct(2, 36, 256), struct(2, 36, 256), struct(36, 256), struct(36, 256), struct(2, 64, 256), struct(2, 64, 256)),
        (flags, cols, inner, outer),
        [pltpu.VMEM((4, 36, 256), F32)],
        scalars=1,
    )
    mixed_in, mixed_out = lon_pairs(inner, outer)
    halves = ((GRAD_ROWS, 128), F32), ((GRAD_ROWS, 128), BF)
    ocean_out, remap_grad, ocean_keep, ocean_send = call(
        ocean_kernel,
        "ocean",
        (struct(32, 64, 256), struct(cells, 128)) + halves,
        (
            flags, mixed, mixed_south, mixed_north, first, last, mixed_in, mixed_out,
            out_cotangent, south, north, side_in, side_out, ocean_mask, remapped, ocean_w, back_w, flux_inject,
        ),
        [
            pltpu.VMEM((36 * 64, 768), BF),
            pltpu.VMEM((2, 48, 768), F32),
            pltpu.VMEM((64, 768), BF),
            pltpu.VMEM((64, 768), BF),
            pltpu.VMEM((cells, 256), BF),
            pltpu.VMEM((34 * 64, 768), BF),
            pltpu.VMEM((2, 40, 256), F32),
            pltpu.VMEM((cells, 256), BF),
        ],
        scalars=1,
    )
    own, to_north, to_south, inner, outer, low_tile, band_in, band_out = call(
        scatter_kernel,
        "scatter_rows",
        (struct(16, 64, 128), struct(2, 64, 128), struct(2, 64, 128), struct(20, 2, 128), struct(20, 2, 128),
         struct(16, 64, 128), struct(32, 64, 128), struct(32, 64, 128)),
        (flags, slots, signed, remap_grad),
        [pltpu.VMEM((32 * BAND, 128), F32)] * 4 + [pltpu.VMEM((8192, 128), F32)],
        scalars=2,
    )
    band_in, band_out = lon_pairs(band_in, band_out, lats - 1)
    credit_in, credit_out = lon_pairs(inner, outer, 0, lats - 1)
    inner, outer = call(
        credit_rows_kernel,
        "credit_rows",
        (struct(2, 64, 128),) * 2,
        (flags, to_north, to_south, credit_in, credit_out),
        [pltpu.VMEM((2, 64, 128), F32)] * 2,
        scalars=1,
    )
    low_tile = low_tile.astype(F32) + band_in[:16].astype(F32) + band_out[:16].astype(F32)
    rows_in, rows_out = lat_pairs(inner, outer, False)
    from_band = lax.ppermute(low_tile.astype(BF), "lat", [(lats - 1, lats - 2)])
    atmos_keep, atmos_send = call(
        atmos_back_kernel,
        "atmos_back",
        halves,
        (flags, atmos_state, south, north, side_in, side_out, act, slope, own, credit_in, credit_out, rows_in, rows_out,
         band_in, band_out, from_band, project),
        [pltpu.VMEM((34 * 64, 768), BF), pltpu.VMEM((cells, 256), BF), pltpu.VMEM((64, 128), F32), pltpu.VMEM((half, 128), BF)],
        scalars=1,
    )
    ocean_keep, ocean_send, atmos_keep, atmos_send = lax.optimization_barrier(
        (ocean_keep, ocean_send, atmos_keep, atmos_send)
    )
    ocean = ocean_keep + exchange(ocean_send, 1).astype(F32)
    atmos = atmos_keep + exchange(atmos_send, 1).astype(F32)
    cut = 1600
    rest = GRAD_ROWS - cut
    sums = reduce_streams(
        [ocean[:cut], jnp.concatenate([ocean[cut:], atmos[:rest]]), atmos[rest:]], ((0, 1, 2), (1, 2, 0), (2, 0, 1))
    )
    ocean = jnp.concatenate([sums[0], sums[1][:rest]])
    atmos = jnp.concatenate([sums[1][rest:], sums[2]])

    def joined(mine):
        other = exchange(mine, 1)
        pair = jnp.concatenate([jnp.where(core == 0, mine, other), jnp.where(core == 0, other, mine)], 1).astype(F32)
        return pair[: 9 * chans].reshape(9, chans, chans), pair[9 * chans : 9 * chans + flux_chans]

    grad_ocean, grad_inject = joined(ocean)
    grad_atmos, grad_project = joined(atmos)
    return (ocean_out, grad_atmos, grad_ocean, grad_project.T, grad_inject)


def solution(mesh):
    return jax.shard_map(
        body,
        mesh=mesh,
        in_specs=(
            P("lat", "lon", None),
            P(),
            P(),
            P("lat", "lon", None),
            P("lat", "lon", None),
            P("lat", "lon", None),
            P("lat", "lon", None),
            P(),
            P("lat", "lon"),
            P(),
            P("lat", "lon", None),
        ),
        out_specs=(P("lat", "lon", None), P(), P(), P(), P()),
        check_vma=False,
    )
```

```python
import jax
import jax.numpy as jnp
from jax import lax
from jax.experimental import pallas as pl
from jax.experimental.pallas import tpu as pltpu
from jax.sharding import PartitionSpec as P

BF = jnp.bfloat16
F32 = jnp.float32
VLIM = 56 << 20
AXES = ("lon", "lat")
NEAR = 72
BAND = 192


def lat_pairs(inner, outer, fold):
    lons, lats = lax.axis_size("lon"), lax.axis_size("lat")
    at = lambda i, j: i * lats + j
    inside = [(at(i, j), at(i, j ^ 1)) for i in range(lons) for j in range(lats)]
    across = [(at(i, j), at(i, j + 1 if j % 2 else j - 1)) for i in range(lons) for j in range(1, lats - 1)]
    if fold:
        across += [(at(i, lats - 1), at(lons - 1 - i, lats - 1)) for i in range(lons)]
    return lax.ppermute(inner, AXES, inside), lax.ppermute(outer, AXES, across)


def lon_pairs(inner, outer, first=0, last=None):
    lons, lats = lax.axis_size("lon"), lax.axis_size("lat")
    here = range(first, lats if last is None else last)
    inside = [(i * lats + j, (i ^ 1) * lats + j) for i in range(lons) for j in here]
    across = [(i * lats + j, ((i + 1 if i % 2 else i - 1) % lons) * lats + j) for i in range(lons) for j in here]
    return lax.ppermute(inner, AXES, inside), lax.ppermute(outer, AXES, across)


def sigmoid(value):
    return 1.0 / (1.0 + jnp.exp(-value))


def silu_slope(value, sigma):
    return sigma * (1.0 + value * (1.0 - sigma))


VMEM = pl.BlockSpec(memory_space=pltpu.VMEM)
SMEM = pl.BlockSpec(memory_space=pltpu.SMEM)
PARAMS = pltpu.CompilerParams(vmem_limit_bytes=VLIM)
GRAD_ROWS = 2400


def call(kernel, name, outs, ins, scratch=(), scalars=0, specs=None, grid=None):
    if specs is None:
        specs = [SMEM] * scalars + [VMEM] * (len(ins) - scalars)
    extra = {} if grid is None else {"grid": grid}
    return pl.pallas_call(
        kernel,
        name=name,
        out_shape=tuple(jax.ShapeDtypeStruct(shape, kind) for shape, kind in outs),
        in_specs=specs,
        out_specs=(VMEM,) * len(outs),
        scratch_shapes=list(scratch),
        compiler_params=PARAMS,
        **extra,
    )(*ins)


def turned_row(row):
    a = lax.broadcasted_iota(jnp.int32, (64, 64), 0)
    b = lax.broadcasted_iota(jnp.int32, (64, 64), 1)
    flip = jnp.where(a + b == 63, jnp.float32(1.0), jnp.float32(0.0)).astype(BF)
    return jnp.dot(flip, row, preferred_element_type=F32)


def build_windows(dst, rows, row_of, west_of, east_of, turned=False):
    first, last = (512, 0) if turned else (0, 512)
    at = lax.broadcasted_iota(jnp.int32, (64, 256), 0)
    for r in range(rows):
        value = row_of(r)
        wide = value.astype(F32)
        left = jnp.where(at == 0, west_of(r).astype(F32), pltpu.roll(wide, 1, 0))
        right = jnp.where(at == 63, east_of(r).astype(F32), pltpu.roll(wide, 63, 0))
        here = slice(r * 64, r * 64 + 64)
        dst[here, first : first + 256] = left.astype(BF)
        dst[here, 256:512] = value
        dst[here, last : last + 256] = right.astype(BF)


def conv_rows(windows, w, start, count, turned=False):
    acc = jnp.zeros((count, 256), F32)
    for r in range(3):
        taps = w[2 - r if turned else r]
        acc += jnp.dot(windows[start + r * 64 : start + r * 64 + count, :], taps, preferred_element_type=F32)
    return acc


def dot_back(a, b):
    return lax.dot_general(a, b, (((1,), (1,)), ((), ())), preferred_element_type=F32)


def turned_lanes(x):
    return jnp.concatenate([x[:, 512:768], x[:, 256:512], x[:, 0:256]], 1)


def put_half(core, keep_ref, send_ref, here, value):
    low, high = value[:, 0:128], value[:, 128:256]
    keep_ref[here, :] = jnp.where(core == 0, low, high)
    send_ref[here, :] = jnp.where(core == 0, high, low).astype(BF)


def dot_rows(a, b):
    return lax.dot_general(a, b, (((0,), (0,)), ((), ())), preferred_element_type=F32)


def put_pair(odd, inner_ref, outer_ref, r, low, high):
    inner_ref[r] = jnp.where(odd, low, high)
    outer_ref[r] = jnp.where(odd, high, low)


def rows_kernel(flag_ref, a0_ref, a1_ref, c0_ref, c1_ref, m_ref, inner_ref, outer_ref):
    odd = flag_ref[1] != 0
    land = m_ref[...].astype(F32).T
    put_pair(odd, inner_ref, outer_ref, 0, a0_ref[0], a1_ref[0])
    low = (c0_ref[0].astype(F32) * land[:, 0:1]).astype(BF)
    high = (c1_ref[0].astype(F32) * land[:, 31:32]).astype(BF)
    put_pair(odd, inner_ref, outer_ref, 1, low, high)


def edges_kernel(
    flag_ref, a0_ref, a1_ref, c0_ref, c1_ref, m_ref, inner_ref, outer_ref, inner_out, outer_out, s_ref, n_ref, cols
):
    top, odd = flag_ref[0] != 0, flag_ref[1] != 0
    land = m_ref[...].astype(F32).T
    for r in range(2):
        s_ref[r] = jnp.where(odd, inner_ref[r], outer_ref[r])
    north = jnp.where(odd, outer_ref[0], inner_ref[0]).astype(F32)
    north = jnp.where(top, jnp.zeros_like(north), north)
    cn = jnp.where(odd, outer_ref[1], inner_ref[1])
    cn = jnp.where(top, turned_row(cn), cn.astype(F32))
    n_ref[0], n_ref[1] = north.astype(BF), cn.astype(BF)
    for r in range(32):
        here = slice(r + 1, r + 2)
        cols[0, here, :] = a0_ref[r, 0:1].astype(F32)
        cols[1, here, :] = c0_ref[r, 0:1].astype(F32) * land[0:1, r : r + 1]
        cols[2, here, :] = a1_ref[r, 15:16].astype(F32)
        cols[3, here, :] = c1_ref[r, 15:16].astype(F32) * land[63:64, r : r + 1]
    for k, (row, i) in enumerate(((s_ref[0], 0), (s_ref[1], 0), (s_ref[0], 63), (s_ref[1], 63))):
        cols[k, 0:1, :] = row[i : i + 1].astype(F32)
    for k, (row, i) in enumerate(((north, 0), (cn, 0), (north, 63), (cn, 63))):
        cols[k, 33:34, :] = row[i : i + 1]
    put_pair(flag_ref[2] != 0, inner_out, outer_out, slice(0, 2), cols[0:2].astype(BF), cols[2:4].astype(BF))


def mixed_edges_kernel(
    flag_ref, cols_in, inner_ref, outer_ref, inner_out, outer_out, first_ref, last_ref, south_ref, north_ref, cols
):
    top, odd = flag_ref[0] != 0, flag_ref[1] != 0
    for r in range(2):
        south_ref[r] = jnp.where(odd, inner_ref[r], outer_ref[r])
        s = south_ref[r].astype(F32)
        n = jnp.where(odd, outer_ref[r], inner_ref[r]).astype(F32)
        n = jnp.where(top, turned_row(outer_ref[1 - r]), n)
        north_ref[r] = n.astype(BF)
        for k, i in enumerate((0, 1, 62, 63)):
            cols[k, r : r + 1, :] = s[i : i + 1]
            cols[k, 34 + r : 35 + r, :] = n[i : i + 1]
    for k in range(4):
        cols[k, 2:34, :] = cols_in[k].astype(F32)
    first_ref[...] = cols[0].astype(BF)
    last_ref[...] = cols[3].astype(BF)
    put_pair(flag_ref[2] != 0, inner_out, outer_out, slice(0, 2), cols[0:2].astype(BF), cols[2:4].astype(BF))


def flux_edges_kernel(flag_ref, first_ref, last_ref, inner_ref, outer_ref, south_ref, north_ref, inner_out, outer_out):
    odd, east_odd = flag_ref[1] != 0, flag_ref[2] != 0
    for r in range(20):
        if r < 16:
            first, last = first_ref[r], last_ref[r]
        else:
            a, b = (inner_ref, outer_ref) if r >= 18 else (outer_ref, inner_ref)
            row = jnp.where(odd, a[r % 2], b[r % 2])
            (north_ref if r < 18 else south_ref)[r % 2] = row
            first, last = row[0:2], row[62:64]
        put_pair(east_odd, inner_out, outer_out, r, first, last)


def atmos_windows(flag_ref, windows, x_ref, s_ref, n_ref, in_ref, out_ref):
    odd = flag_ref[2] != 0
    west = jnp.where(odd, in_ref[0].astype(F32), out_ref[0].astype(F32))
    east = jnp.where(odd, out_ref[0].astype(F32), in_ref[0].astype(F32))
    build_windows(
        windows,
        34,
        lambda r: s_ref[0] if r == 0 else (n_ref[0] if r == 33 else x_ref[r - 1]),
        lambda r: west[r : r + 1, :],
        lambda r: east[r : r + 1, :],
    )


def packed_maps(p_ref):
    p = p_ref[...]
    zeros = jnp.zeros_like(p)
    return jnp.concatenate([p, zeros], 0), jnp.concatenate([zeros, p], 0)


def atmos_kernel(
    flag_ref, x_ref, s_ref, n_ref, in_ref, out_ref, w_ref, p_ref,
    act_ref, slope_ref, own_ref, inner_out, outer_out, first_ref, last_ref, windows,
):
    atmos_windows(flag_ref, windows, x_ref, s_ref, n_ref, in_ref, out_ref)
    maps = packed_maps(p_ref)
    for b in range(2):
        packed = jnp.zeros((512, 128), F32)
        for h in range(2):
            start = h * 1024 + b * 512
            pre = conv_rows(windows, w_ref, start, 512)
            sigma = sigmoid(pre)
            act = (pre * sigma).astype(BF)
            act_ref[start : start + 512, :] = act
            slope_ref[start : start + 512, :] = silu_slope(pre, sigma).astype(BF)
            packed += dot_back(act, maps[h])
        for u in range(8):
            r = b * 8 + u
            row = packed[u * 64 : u * 64 + 64].astype(BF)
            own_ref[r] = row
            first_ref[r] = row[0:2]
            last_ref[r] = row[62:64]
    for r in range(2):
        put_pair(flag_ref[1] != 0, inner_out, outer_out, r, own_ref[r], own_ref[14 + r])


def ocean_kernel(
    flag_ref, x_ref, s_ref, n_ref, first_ref, last_ref, in_ref, beyond_ref, c_ref, cs_ref, cn_ref, ci_ref, co_ref, m_ref,
    w_ref, wt_ref, inj_ref, out_ref, remap_ref, deltas, back,
    windows, sides, north, turned_north, dwin, dsides,
):
    top, odd = flag_ref[0] != 0, flag_ref[2] != 0
    west = [jnp.where(odd, in_ref[k].astype(F32), beyond_ref[k].astype(F32)) for k in range(2)]
    east = [jnp.where(odd, beyond_ref[k].astype(F32), in_ref[k].astype(F32)) for k in range(2)]
    cot_west = jnp.where(odd, ci_ref[1].astype(F32), co_ref[1].astype(F32))
    cot_east = jnp.where(odd, co_ref[1].astype(F32), ci_ref[1].astype(F32))
    land = m_ref[...].astype(F32).T
    build_windows(
        windows,
        36,
        lambda r: s_ref[r] if r < 2 else (n_ref[r - 34] if r >= 34 else x_ref[r - 2]),
        lambda r: west[1][r : r + 1, :],
        lambda r: east[0][r : r + 1, :],
    )
    sides[...] = jnp.zeros_like(sides)
    for side, columns in ((0, (west[0], west[1], first_ref[...])), (1, (last_ref[...], east[0], east[1]))):
        for q in range(3):
            sides[side, 0:36, q * 256 : q * 256 + 256] = columns[q].astype(F32)

    def side_rows(start, count):
        return jnp.concatenate([sides[0, start : start + count, :], sides[1, start : start + count, :]], 0).astype(BF)

    pre = jnp.zeros((80, 256), F32)
    lines = [jnp.concatenate([windows[(33 + r) * 64 : (34 + r) * 64, :], side_rows(33 + r, 8)], 0) for r in range(3)]
    for r in range(3):
        pre += jnp.dot(jnp.where(top, turned_lanes(lines[2 - r]), lines[r]), w_ref[r], preferred_element_type=F32)
    slope = silu_slope(pre, sigmoid(pre))
    d_north = (cn_ref[1].astype(F32) * slope[0:64]).astype(BF)
    side_pre = jnp.zeros((80, 256), F32)
    for r in range(3):
        side_pre += jnp.dot(side_rows(r, 40), w_ref[r], preferred_element_type=F32)
    side_slope = silu_slope(side_pre, sigmoid(side_pre))
    at = lax.broadcasted_iota(jnp.int32, (40, 256), 0)
    for side, cot in ((0, cot_west), (1, cot_east)):
        corner = slope[64 + side * 8 : 65 + side * 8]
        here = jnp.where(at == 33, corner, side_slope[side * 40 : side * 40 + 40])
        dsides[side] = jnp.zeros((40, 256), F32)
        dsides[side, 0:34, :] = cot * here[0:34]
    pre = conv_rows(windows, w_ref, 0, 64)
    d_south = (cs_ref[1].astype(F32) * silu_slope(pre, sigmoid(pre))).astype(BF)
    for b in range(4):
        pre = conv_rows(windows, w_ref, 64 + b * 512, 512)
        sigma = sigmoid(pre)
        act = pre * sigma
        slope = silu_slope(pre, sigma)
        for u in range(8):
            r = b * 8 + u
            here = slice(u * 64, u * 64 + 64)
            wet = land[:, r : r + 1]
            out_ref[r] = (wet * act[here]).astype(BF)
            deltas[r * 64 : r * 64 + 64, :] = (c_ref[r].astype(F32) * wet * slope[here]).astype(BF)
    dry = jnp.zeros((64, 256), BF)
    build_windows(
        dwin,
        34,
        lambda r: d_south if r == 0 else (dry if r == 33 else deltas[r * 64 - 64 : r * 64, :]),
        lambda r: dsides[0, r : r + 1, :] if r < 33 else dry[0:1],
        lambda r: dsides[1, r : r + 1, :] if r < 33 else dry[0:1],
        turned=True,
    )
    for dst, turned in ((north, False), (turned_north, True)):
        build_windows(
            dst, 1, lambda r: d_north, lambda r: dsides[0, 33:34, :], lambda r: dsides[1, 33:34, :], turned=turned
        )
    beyond = jnp.dot(
        jnp.where(top, north[...], turned_north[...]), wt_ref[jnp.where(top, 2, 0)], preferred_element_type=F32
    )
    inject = jnp.concatenate([inj_ref[...], inj_ref[...]], 0)
    for b in range(4):
        total = conv_rows(dwin, wt_ref, b * 512, 512, turned=True)
        for u in range(8):
            r = b * 8 + u
            value = total[u * 64 : u * 64 + 64]
            if r == 31:
                value = value + beyond
            back[r * 64 : r * 64 + 64, :] = (land[:, r : r + 1] * value).astype(BF)
        remap_ref[b * 512 : b * 512 + 512, :] = dot_back(back[b * 512 : b * 512 + 512, :], inject).astype(BF)


def ocean_grads_kernel(
    flag_ref, x_ref, s_ref, n_ref, in_ref, beyond_ref, deltas, back, rem_ref, keep_ref, send_ref, windows
):
    core, odd = flag_ref[1], flag_ref[2] != 0
    west = jnp.where(odd, in_ref[1].astype(F32), beyond_ref[1].astype(F32))
    east = jnp.where(odd, beyond_ref[0].astype(F32), in_ref[0].astype(F32))
    build_windows(
        windows,
        34,
        lambda r: s_ref[1] if r == 0 else (n_ref[0] if r == 33 else x_ref[r - 1]),
        lambda r: west[r + 1 : r + 2, :],
        lambda r: east[r + 1 : r + 2, :],
    )
    for r in range(3):
        value = dot_rows(windows[r * 64 : r * 64 + 2048, :], deltas[...])
        put_half(core, keep_ref, send_ref, slice(r * 768, r * 768 + 768), value)
    tail = jnp.concatenate([dot_rows(rem_ref[...], back[...])[0:64], jnp.zeros((32, 256), F32)], 0)
    put_half(core, keep_ref, send_ref, slice(2304, 2400), tail)


def credit_rows_kernel(flag_ref, n_ref, s_ref, in_ref, out_ref, inner_out, outer_out, n_sum, s_sum):
    odd, east_odd = flag_ref[1] != 0, flag_ref[2] != 0
    for r in range(2):
        for src, dst, first in ((n_ref, n_sum, 16), (s_ref, s_sum, 18)):
            inner, outer = in_ref[first + r].astype(F32), out_ref[first + r].astype(F32)
            dst[r] = src[r].astype(F32)
            dst[r, 0:2] = dst[r, 0:2] + jnp.where(east_odd, inner, outer)
            dst[r, 62:64] = dst[r, 62:64] + jnp.where(east_odd, outer, inner)
        put_pair(odd, inner_out, outer_out, r, s_sum[r].astype(BF), n_sum[r].astype(BF))


def atmos_back_kernel(
    flag_ref, x_ref, s_ref, n_ref, in_ref, out_ref, act_ref, slope_ref, own_ref, ci_ref, co_ref, ri_ref, ro_ref, bi_ref, bo_ref,
    low_ref, p_ref, keep_ref, send_ref, windows, deltas, total, credit,
):
    core = flag_ref[1]
    odd, east_odd = core != 0, flag_ref[2] != 0
    atmos_windows(flag_ref, windows, x_ref, s_ref, n_ref, in_ref, out_ref)
    maps = packed_maps(p_ref)
    for r in range(16):
        value = own_ref[r].astype(F32) + bi_ref[16 + r].astype(F32) + bo_ref[16 + r].astype(F32) + low_ref[r].astype(F32)
        if r < 2:
            value += jnp.where(odd, ri_ref[r].astype(F32), ro_ref[r].astype(F32))
        if r >= 14:
            value += jnp.where(odd, ro_ref[r - 14].astype(F32), ri_ref[r - 14].astype(F32))
        total[...] = value
        inner, outer = ci_ref[r].astype(F32), co_ref[r].astype(F32)
        total[0:2, :] += jnp.where(east_odd, inner, outer)
        total[62:64, :] += jnp.where(east_odd, outer, inner)
        credit[r * 64 : r * 64 + 64, :] = total[...].astype(BF)
    for h in range(2):
        here = slice(h * 1024, h * 1024 + 1024)
        back = jnp.dot(credit[...], maps[h], preferred_element_type=F32)
        deltas[here, :] = (back * slope_ref[here, :].astype(F32)).astype(BF)
    for r in range(3):
        value = dot_rows(windows[r * 64 : r * 64 + 2048, :], deltas[...])
        put_half(core, keep_ref, send_ref, slice(r * 768, r * 768 + 768), value)
    lower = dot_rows(credit[...], act_ref[0:1024, :])
    upper = dot_rows(credit[...], act_ref[1024:2048, :])
    tail = jnp.concatenate([lower[0:64] + upper[64:128], jnp.zeros((32, 256), F32)], 0)
    put_half(core, keep_ref, send_ref, slice(2304, 2400), tail)


def exchange(x, mask):
    count = lax.axis_size("lon") * lax.axis_size("lat")
    return lax.ppermute(x, AXES, [(i, i ^ mask) for i in range(count)])


def reduce_streams(streams, orders):
    rank = lax.axis_index("lon") * lax.axis_size("lat") + lax.axis_index("lat")
    bit = lambda n: (rank >> n) & 1
    near = [(2, bit(1) ^ bit(2)), (8, bit(3) ^ bit(4)), (32, bit(5) ^ bit(6))]
    far = (6, 24, 96)
    count = range(len(streams))
    for level in range(3):
        steps = [near[orders[i][level]] for i in count]
        half = streams[0].shape[0] // 2
        keep = [lax.dynamic_slice_in_dim(streams[i], steps[i][1] * half, half) for i in count]
        send = [lax.dynamic_slice_in_dim(streams[i], (1 - steps[i][1]) * half, half).astype(BF) for i in count]
        streams = [keep[i] + exchange(send[i], steps[i][0]).astype(F32) for i in count]
    streams = [s.astype(BF) for s in streams]
    for level in range(3):
        got = [exchange(streams[i], far[orders[i][level]]) for i in count]
        streams = [(streams[i].astype(F32) + got[i].astype(F32)).astype(BF) for i in count]
    for level in (2, 1, 0):
        steps = [near[orders[i][level]] for i in count]
        got = [exchange(streams[i], steps[i][0]) for i in count]
        streams = [
            jnp.where(
                steps[i][1] == 0,
                jnp.concatenate([streams[i], got[i]]),
                jnp.concatenate([got[i], streams[i]]),
            )
            for i in count
        ]
    return streams


def lane_sign():
    lane = lax.broadcasted_iota(jnp.int32, (64, 128), 1)
    return jnp.where(lane < 64, jnp.float32(1.0), jnp.float32(-1.0))


def gather_kernel(
    flag_ref, slot_ref, w_ref, fn_ref, fs_ref, fi_ref, fo_ref, low_ref, own_ref, bi_ref, bo_ref, o_ref, m_ref, inj_ref,
    out_ref, mixed_ref, cols_ref, inner_ref, outer_ref, table, picked, cols,
):
    top = flag_ref[0]
    odd, east_odd = flag_ref[1] != 0, flag_ref[2] != 0

    @pl.when(top == 0)
    def _():
        for r in range(20):
            rows = own_ref[r] if r < 16 else (fn_ref[r - 16] if r < 18 else fs_ref[r - 18])
            table[r * NEAR : r * NEAR + 64, :] = rows.astype(F32)
            table[r * NEAR + 64 : r * NEAR + 66, :] = jnp.where(east_odd, fi_ref[r].astype(F32), fo_ref[r].astype(F32))
            table[r * NEAR + 66 : r * NEAR + 68, :] = jnp.where(east_odd, fo_ref[r].astype(F32), fi_ref[r].astype(F32))

    @pl.when(top != 0)
    def _():
        for r in range(32):
            base = r * BAND
            table[base : base + 64, :] = (low_ref[r] if r < 16 else own_ref[r - 16]).astype(F32)
            inner, outer = bi_ref[r].astype(F32), bo_ref[r].astype(F32)
            table[base + 64 : base + 128, :] = jnp.where(east_odd, inner, outer)
            table[base + 128 : base + 192, :] = jnp.where(east_odd, outer, inner)

    def step(q, carry):
        base = pl.multiple_of(q * 64, 64)
        for u in range(64):
            at = slot_ref[q, u]
            picked[pl.ds(base + u, 1), :] = table[pl.ds(at, 1), :]
        return carry

    lax.fori_loop(0, 128, step, 0)
    sign = lane_sign()
    wt = w_ref[...].T
    for row in range(32):
        acc = jnp.zeros((64, 128), F32)
        for k in range(4):
            q = row * 4 + k
            factor = jnp.maximum(wt[:, q : q + 1] * sign, 0.0)
            acc = acc + factor * picked[q * 64 : q * 64 + 64, :]
        acc = acc + pltpu.roll(acc, 64, 1)
        out_ref[row * 64 : row * 64 + 64, :] = acc.astype(BF)
    land = m_ref[...].astype(F32).T
    inject = jnp.concatenate([inj_ref[...], jnp.zeros_like(inj_ref[...])], 0)
    for b in range(4):
        injected = jnp.dot(out_ref[b * 512 : b * 512 + 512, :], inject, preferred_element_type=F32)
        for u in range(8):
            r = b * 8 + u
            value = land[:, r : r + 1] * (o_ref[r].astype(F32) + injected[u * 64 : u * 64 + 64])
            mixed_ref[r] = value.astype(BF)
            for c, i in enumerate((0, 1, 62, 63)):
                cols[c, r : r + 1, :] = value[i : i + 1]
    for r in range(2):
        put_pair(odd, inner_ref, outer_ref, r, mixed_ref[r], mixed_ref[30 + r])
    cols_ref[...] = cols[...].astype(BF)


def scatter_kernel(
    flag_ref, slot_ref, w_ref, g_ref, own_ref, n_ref, s_ref, side_in, side_out, low_ref, band_in, band_out, t0, t1, t2, t3, parts
):
    top = flag_ref[0]
    east_odd = flag_ref[2] != 0
    tables = (t0, t1, t2, t3)

    def clear(count):
        def one(i, carry):
            base = pl.multiple_of(i * 96, 96)
            for t in tables:
                t[pl.ds(base, 96), :] = jnp.zeros((96, 128), F32)
            return carry

        lax.fori_loop(0, count // 96, one, 0)

    @pl.when(top == 0)
    def _():
        clear(20 * NEAR)

    @pl.when(top != 0)
    def _():
        clear(32 * BAND)

    sign = lane_sign()
    wt = w_ref[...].T
    for row in range(32):
        g = g_ref[row * 64 : row * 64 + 64, :].astype(F32)
        for k in range(4):
            q = row * 4 + k
            parts[q * 64 : q * 64 + 64, :] = jnp.maximum(wt[:, q : q + 1] * sign, 0.0) * g

    def step(row, carry):
        base = pl.multiple_of(row * 256, 256)
        for u in range(64):
            for k in range(4):
                at = slot_ref[row * 4 + k, u]
                t = tables[k]
                t[pl.ds(at, 1), :] = t[pl.ds(at, 1), :] + parts[pl.ds(base + k * 64 + u, 1), :]
        return carry

    lax.fori_loop(0, 32, step, 0)

    def total(start, size):
        where = pl.ds(start, size)
        return ((t0[where, :] + t1[where, :]) + (t2[where, :] + t3[where, :])).astype(BF)

    @pl.when(top == 0)
    def _():
        for r in range(20):
            rows = total(r * NEAR, 64)
            if r < 16:
                own_ref[r] = rows
            elif r < 18:
                n_ref[r - 16] = rows
            else:
                s_ref[r - 18] = rows
            put_pair(east_odd, side_in, side_out, r, total(r * NEAR + 64, 2), total(r * NEAR + 66, 2))

    @pl.when(top != 0)
    def _():
        for r in range(2):
            n_ref[r] = jnp.zeros((64, 128), BF)
            s_ref[r] = jnp.zeros((64, 128), BF)
        side_in[...] = jnp.zeros_like(side_in)
        side_out[...] = jnp.zeros_like(side_out)
        for r in range(32):
            base = r * BAND
            if r < 16:
                low_ref[r] = total(base, 64)
            else:
                own_ref[r - 16] = total(base, 64)
            put_pair(east_odd, band_in, band_out, r, total(base + 64, 64), total(base + 128, 64))


def entry_slots(source_row, source_col, weight, is_top, row_count, col_count):
    nx = col_count * lax.axis_size("lon")
    row = source_row - lax.axis_index("lat") * row_count
    col = jnp.remainder(source_col - lax.axis_index("lon") * col_count + nx // 2, nx) - nx // 2
    half = row_count // 2
    inside = (row >= 0) & (row < row_count)
    wrapped = row & (row_count - 1)
    packed = wrapped & (half - 1)
    upper = wrapped >= half
    near_row = jnp.where(inside, packed, jnp.where(row < 0, packed + 4, packed + half))
    near_col = jnp.where((col >= 0) & (col < col_count), col, jnp.where(col < 0, col + col_count + 2, col + 2))
    band_row = jnp.where(row >= 0, packed + half, packed)
    band_col = jnp.where((col >= 0) & (col < col_count), col, jnp.where(col < 0, col + 2 * col_count, col + col_count))
    slot = jnp.where(is_top, band_row * BAND + band_col, near_row * NEAR + near_col)
    signed = jnp.where(upper, -weight, weight)
    order = lambda x: jnp.transpose(x, (0, 2, 1)).reshape(-1, col_count)
    return order(slot), order(signed)


def body(
    atmos_state,
    atmos_weights,
    flux_project,
    source_row,
    source_col,
    intersection_weight,
    ocean_state,
    flux_inject,
    ocean_mask,
    ocean_weights,
    out_cotangent,
):
    row_count, col_count, chans = atmos_state.shape
    flux_chans = flux_project.shape[1]
    cells = row_count * col_count
    half = cells // 2
    lats = lax.axis_size("lat")
    is_top = lax.axis_index("lat") == lats - 1
    core = lax.rem(lax.axis_index("lat"), 2)
    flags = jnp.stack([is_top.astype(jnp.int32), core, lax.rem(lax.axis_index("lon"), 2)])
    struct = lambda *shape: (shape, BF)
    block = lambda shape, at: pl.BlockSpec(shape, lambda i: (at[0], at[1], 0))
    row = (1, 64, 256)
    inner, outer = call(
        rows_kernel,
        "rows",
        (struct(2, 64, 256), struct(2, 64, 256)),
        (flags, atmos_state, atmos_state, out_cotangent, out_cotangent, ocean_mask),
        specs=[SMEM, block(row, (0, 0)), block(row, (31, 0)), block(row, (0, 0)), block(row, (31, 0)), VMEM],
        grid=(1,),
    )
    inner, outer = lat_pairs(inner, outer, True)
    slab = (32, 16, 256)
    inner, outer, south, north = call(
        edges_kernel,
        "edges",
        (struct(2, 34, 256), struct(2, 34, 256), struct(2, 64, 256), struct(2, 64, 256)),
        (flags, atmos_state, atmos_state, out_cotangent, out_cotangent, ocean_mask, inner, outer),
        [pltpu.VMEM((4, 34, 256), F32)],
        specs=[SMEM, block(slab, (0, 0)), block(slab, (0, 3)), block(slab, (0, 0)), block(slab, (0, 3))] + [VMEM] * 3,
        grid=(1,),
    )
    side_in, side_out = lon_pairs(inner, outer)
    project = flux_project.T
    atmos_w = atmos_weights.reshape(3, 3 * chans, chans)
    ocean_w = ocean_weights.reshape(3, 3 * chans, chans)
    act, slope, own, inner, outer, first, last = call(
        atmos_kernel,
        "atmos",
        (struct(cells, chans), struct(cells, chans), struct(16, 64, 128), struct(2, 64, 128), struct(2, 64, 128),
         struct(16, 2, 128), struct(16, 2, 128)),
        (flags, atmos_state, south, north, side_in, side_out, atmos_w, project),
        [pltpu.VMEM((34 * 64, 768), BF)],
        scalars=1,
    )
    low_tile = lax.ppermute(own, "lat", [(lats - 2, lats - 1)])
    inner, outer = lat_pairs(inner, outer, False)
    two, inner, outer = lax.optimization_barrier((jnp.concatenate([low_tile, own], 0), inner, outer))
    band_in, band_out = lon_pairs(two, two, lats - 1)
    flux_south, flux_north, inner, outer = call(
        flux_edges_kernel,
        "flux_edges",
        (struct(2, 64, 128), struct(2, 64, 128), struct(20, 2, 128), struct(20, 2, 128)),
        (flags, first, last, inner, outer),
        scalars=1,
    )
    flux_in, flux_out = lon_pairs(inner, outer, 0, lats - 1)
    late = lax.optimization_barrier((own, source_row, source_col, intersection_weight, ocean_weights))
    slots, signed = entry_slots(*late[1:4], is_top, row_count, col_count)
    back_w = jnp.transpose(late[4], (0, 2, 1)).reshape(3, 3 * chans, chans)
    remapped, mixed, cols, inner, outer = call(
        gather_kernel,
        "gather_mix",
        (struct(cells, 128), struct(32, 64, 256), struct(4, 32, 256), struct(2, 64, 256), struct(2, 64, 256)),
        (flags, slots, signed, flux_north, flux_south, flux_in, flux_out, low_tile, own, band_in, band_out,
         ocean_state, ocean_mask, flux_inject),
        [pltpu.VMEM((32 * BAND, 128), F32), pltpu.VMEM((8192, 128), F32), pltpu.VMEM((4, 32, 256), F32)],
        scalars=2,
    )
    inner, outer = lat_pairs(inner, outer, True)
    inner, outer, first, last, mixed_south, mixed_north = call(
        mixed_edges_kernel,
        "mixed_edges",
        (struct(2, 36, 256), struct(2, 36, 256), struct(36, 256), struct(36, 256), struct(2, 64, 256), struct(2, 64, 256)),
        (flags, cols, inner, outer),
        [pltpu.VMEM((4, 36, 256), F32)],
        scalars=1,
    )
    mixed_in, mixed_out = lon_pairs(inner, outer)
    halves = ((GRAD_ROWS, 128), F32), ((GRAD_ROWS, 128), BF)
    ocean_out, remap_grad, deltas, back = call(
        ocean_kernel,
        "ocean",
        (struct(32, 64, 256), struct(cells, 128), struct(cells, 256), struct(cells, 256)),
        (
            flags, mixed, mixed_south, mixed_north, first, last, mixed_in, mixed_out,
            out_cotangent, south, north, side_in, side_out, ocean_mask, ocean_w, back_w, flux_inject,
        ),
        [
            pltpu.VMEM((36 * 64, 768), BF),
            pltpu.VMEM((2, 48, 768), F32),
            pltpu.VMEM((64, 768), BF),
            pltpu.VMEM((64, 768), BF),
            pltpu.VMEM((34 * 64, 768), BF),
            pltpu.VMEM((2, 40, 256), F32),
        ],
        scalars=1,
    )
    own, to_north, to_south, inner, outer, low_tile, band_in, band_out = call(
        scatter_kernel,
        "scatter_rows",
        (struct(16, 64, 128), struct(2, 64, 128), struct(2, 64, 128), struct(20, 2, 128), struct(20, 2, 128),
         struct(16, 64, 128), struct(32, 64, 128), struct(32, 64, 128)),
        (flags, slots, signed, remap_grad),
        [pltpu.VMEM((32 * BAND, 128), F32)] * 4 + [pltpu.VMEM((8192, 128), F32)],
        scalars=2,
    )
    deltas, back, inner, outer, band_in, band_out = lax.optimization_barrier((deltas, back, inner, outer, band_in, band_out))
    ocean_keep, ocean_send = call(
        ocean_grads_kernel,
        "ocean_grads",
        halves,
        (flags, mixed, mixed_south, mixed_north, mixed_in, mixed_out, deltas, back, remapped),
        [pltpu.VMEM((34 * 64, 768), BF)],
        scalars=1,
    )
    band_in, band_out = lon_pairs(band_in, band_out, lats - 1)
    credit_in, credit_out = lon_pairs(inner, outer, 0, lats - 1)
    inner, outer = call(
        credit_rows_kernel,
        "credit_rows",
        (struct(2, 64, 128),) * 2,
        (flags, to_north, to_south, credit_in, credit_out),
        [pltpu.VMEM((2, 64, 128), F32)] * 2,
        scalars=1,
    )
    rows_in, rows_out = lat_pairs(inner, outer, False)
    band_in, band_out, rows_in, rows_out, ocean_keep, ocean_send = lax.optimization_barrier(
        (band_in, band_out, rows_in, rows_out, ocean_keep, ocean_send)
    )
    low_tile = low_tile.astype(F32) + band_in[:16].astype(F32) + band_out[:16].astype(F32)
    from_band = lax.ppermute(low_tile.astype(BF), "lat", [(lats - 1, lats - 2)])
    atmos_keep, atmos_send = call(
        atmos_back_kernel,
        "atmos_back",
        halves,
        (flags, atmos_state, south, north, side_in, side_out, act, slope, own, credit_in, credit_out, rows_in, rows_out,
         band_in, band_out, from_band, project),
        [pltpu.VMEM((34 * 64, 768), BF), pltpu.VMEM((cells, 256), BF), pltpu.VMEM((64, 128), F32), pltpu.VMEM((half, 128), BF)],
        scalars=1,
    )
    ocean_keep, ocean_send, atmos_keep, atmos_send = lax.optimization_barrier(
        (ocean_keep, ocean_send, atmos_keep, atmos_send)
    )
    ocean = ocean_keep + exchange(ocean_send, 1).astype(F32)
    atmos = atmos_keep + exchange(atmos_send, 1).astype(F32)
    cut = 1600
    rest = GRAD_ROWS - cut
    sums = reduce_streams(
        [ocean[:cut], jnp.concatenate([ocean[cut:], atmos[:rest]]), atmos[rest:]], ((0, 1, 2), (1, 2, 0), (2, 0, 1))
    )
    ocean = jnp.concatenate([sums[0], sums[1][:rest]])
    atmos = jnp.concatenate([sums[1][rest:], sums[2]])

    def joined(mine):
        other = exchange(mine, 1)
        pair = jnp.concatenate([jnp.where(core == 0, mine, other), jnp.where(core == 0, other, mine)], 1).astype(F32)
        return pair[: 9 * chans].reshape(9, chans, chans), pair[9 * chans : 9 * chans + flux_chans]

    grad_ocean, grad_inject = joined(ocean)
    grad_atmos, grad_project = joined(atmos)
    return (ocean_out, grad_atmos, grad_ocean, grad_project.T, grad_inject)


def solution(mesh):
    return jax.shard_map(
        body,
        mesh=mesh,
        in_specs=(
            P("lat", "lon", None),
            P(),
            P(),
            P("lat", "lon", None),
            P("lat", "lon", None),
            P("lat", "lon", None),
            P("lat", "lon", None),
            P(),
            P("lat", "lon"),
            P(),
            P("lat", "lon", None),
        ),
        out_specs=(P("lat", "lon", None), P(), P(), P(), P()),
        check_vma=False,
    )
```

```python
import jax
import jax.numpy as jnp
from jax import lax
from jax.experimental import pallas as pl
from jax.experimental.pallas import tpu as pltpu
from jax.sharding import PartitionSpec as P

BF = jnp.bfloat16
F32 = jnp.float32
VLIM = 56 << 20
AXES = ("lon", "lat")
NEAR = 72
BAND = 192


def lat_pairs(inner, outer, fold):
    lons, lats = lax.axis_size("lon"), lax.axis_size("lat")
    at = lambda i, j: i * lats + j
    inside = [(at(i, j), at(i, j ^ 1)) for i in range(lons) for j in range(lats)]
    across = [(at(i, j), at(i, j + 1 if j % 2 else j - 1)) for i in range(lons) for j in range(1, lats - 1)]
    if fold:
        across += [(at(i, lats - 1), at(lons - 1 - i, lats - 1)) for i in range(lons)]
    return lax.ppermute(inner, AXES, inside), lax.ppermute(outer, AXES, across)


def lon_pairs(inner, outer, first=0, last=None):
    lons, lats = lax.axis_size("lon"), lax.axis_size("lat")
    here = range(first, lats if last is None else last)
    inside = [(i * lats + j, (i ^ 1) * lats + j) for i in range(lons) for j in here]
    across = [(i * lats + j, ((i + 1 if i % 2 else i - 1) % lons) * lats + j) for i in range(lons) for j in here]
    return lax.ppermute(inner, AXES, inside), lax.ppermute(outer, AXES, across)


def sigmoid(value):
    return 1.0 / (1.0 + jnp.exp(-value))


def silu_slope(value, sigma):
    return sigma * (1.0 + value * (1.0 - sigma))


VMEM = pl.BlockSpec(memory_space=pltpu.VMEM)
SMEM = pl.BlockSpec(memory_space=pltpu.SMEM)
PARAMS = pltpu.CompilerParams(vmem_limit_bytes=VLIM)
GRAD_ROWS = 2400


def call(kernel, name, outs, ins, scratch=(), scalars=0, specs=None, grid=None):
    if specs is None:
        specs = [SMEM] * scalars + [VMEM] * (len(ins) - scalars)
    extra = {} if grid is None else {"grid": grid}
    return pl.pallas_call(
        kernel,
        name=name,
        out_shape=tuple(jax.ShapeDtypeStruct(shape, kind) for shape, kind in outs),
        in_specs=specs,
        out_specs=(VMEM,) * len(outs),
        scratch_shapes=list(scratch),
        compiler_params=PARAMS,
        **extra,
    )(*ins)


def turned_row(row):
    a = lax.broadcasted_iota(jnp.int32, (64, 64), 0)
    b = lax.broadcasted_iota(jnp.int32, (64, 64), 1)
    flip = jnp.where(a + b == 63, jnp.float32(1.0), jnp.float32(0.0)).astype(BF)
    return jnp.dot(flip, row, preferred_element_type=F32)


def build_windows(dst, rows, row_of, west_of, east_of, turned=False):
    first, last = (512, 0) if turned else (0, 512)
    at = lax.broadcasted_iota(jnp.int32, (64, 256), 0)
    for r in range(rows):
        value = row_of(r)
        wide = value.astype(F32)
        left = jnp.where(at == 0, west_of(r).astype(F32), pltpu.roll(wide, 1, 0))
        right = jnp.where(at == 63, east_of(r).astype(F32), pltpu.roll(wide, 63, 0))
        here = slice(r * 64, r * 64 + 64)
        dst[here, first : first + 256] = left.astype(BF)
        dst[here, 256:512] = value
        dst[here, last : last + 256] = right.astype(BF)


def conv_rows(windows, w, start, count, turned=False):
    acc = jnp.zeros((count, 256), F32)
    for r in range(3):
        taps = w[2 - r if turned else r]
        acc += jnp.dot(windows[start + r * 64 : start + r * 64 + count, :], taps, preferred_element_type=F32)
    return acc


def dot_back(a, b):
    return lax.dot_general(a, b, (((1,), (1,)), ((), ())), preferred_element_type=F32)


def turned_lanes(x):
    return jnp.concatenate([x[:, 512:768], x[:, 256:512], x[:, 0:256]], 1)


def put_half(core, keep_ref, send_ref, here, value):
    low, high = value[:, 0:128], value[:, 128:256]
    keep_ref[here, :] = jnp.where(core == 0, low, high)
    send_ref[here, :] = jnp.where(core == 0, high, low).astype(BF)


def dot_rows(a, b):
    return lax.dot_general(a, b, (((0,), (0,)), ((), ())), preferred_element_type=F32)


def put_pair(odd, inner_ref, outer_ref, r, low, high):
    inner_ref[r] = jnp.where(odd, low, high)
    outer_ref[r] = jnp.where(odd, high, low)


def rows_kernel(flag_ref, a0_ref, a1_ref, c0_ref, c1_ref, m_ref, inner_ref, outer_ref):
    odd = flag_ref[1] != 0
    land = m_ref[...].astype(F32).T
    put_pair(odd, inner_ref, outer_ref, 0, a0_ref[0], a1_ref[0])
    low = (c0_ref[0].astype(F32) * land[:, 0:1]).astype(BF)
    high = (c1_ref[0].astype(F32) * land[:, 31:32]).astype(BF)
    put_pair(odd, inner_ref, outer_ref, 1, low, high)


def edges_kernel(
    flag_ref, a0_ref, a1_ref, c0_ref, c1_ref, m_ref, inner_ref, outer_ref, inner_out, outer_out, s_ref, n_ref, cols
):
    top, odd = flag_ref[0] != 0, flag_ref[1] != 0
    land = m_ref[...].astype(F32).T
    for r in range(2):
        s_ref[r] = jnp.where(odd, inner_ref[r], outer_ref[r])
    north = jnp.where(odd, outer_ref[0], inner_ref[0]).astype(F32)
    north = jnp.where(top, jnp.zeros_like(north), north)
    cn = jnp.where(odd, outer_ref[1], inner_ref[1])
    cn = jnp.where(top, turned_row(cn), cn.astype(F32))
    n_ref[0], n_ref[1] = north.astype(BF), cn.astype(BF)
    for r in range(32):
        here = slice(r + 1, r + 2)
        cols[0, here, :] = a0_ref[r, 0:1].astype(F32)
        cols[1, here, :] = c0_ref[r, 0:1].astype(F32) * land[0:1, r : r + 1]
        cols[2, here, :] = a1_ref[r, 15:16].astype(F32)
        cols[3, here, :] = c1_ref[r, 15:16].astype(F32) * land[63:64, r : r + 1]
    for k, (row, i) in enumerate(((s_ref[0], 0), (s_ref[1], 0), (s_ref[0], 63), (s_ref[1], 63))):
        cols[k, 0:1, :] = row[i : i + 1].astype(F32)
    for k, (row, i) in enumerate(((north, 0), (cn, 0), (north, 63), (cn, 63))):
        cols[k, 33:34, :] = row[i : i + 1]
    put_pair(flag_ref[2] != 0, inner_out, outer_out, slice(0, 2), cols[0:2].astype(BF), cols[2:4].astype(BF))


def mixed_edges_kernel(
    flag_ref, cols_in, inner_ref, outer_ref, inner_out, outer_out, first_ref, last_ref, south_ref, north_ref, cols
):
    top, odd = flag_ref[0] != 0, flag_ref[1] != 0
    for r in range(2):
        south_ref[r] = jnp.where(odd, inner_ref[r], outer_ref[r])
        s = south_ref[r].astype(F32)
        n = jnp.where(odd, outer_ref[r], inner_ref[r]).astype(F32)
        n = jnp.where(top, turned_row(outer_ref[1 - r]), n)
        north_ref[r] = n.astype(BF)
        for k, i in enumerate((0, 1, 62, 63)):
            cols[k, r : r + 1, :] = s[i : i + 1]
            cols[k, 34 + r : 35 + r, :] = n[i : i + 1]
    for k in range(4):
        cols[k, 2:34, :] = cols_in[k].astype(F32)
    first_ref[...] = cols[0].astype(BF)
    last_ref[...] = cols[3].astype(BF)
    put_pair(flag_ref[2] != 0, inner_out, outer_out, slice(0, 2), cols[0:2].astype(BF), cols[2:4].astype(BF))


def flux_edges_kernel(flag_ref, first_ref, last_ref, inner_ref, outer_ref, south_ref, north_ref, inner_out, outer_out):
    odd, east_odd = flag_ref[1] != 0, flag_ref[2] != 0
    for r in range(20):
        if r < 16:
            first, last = first_ref[r], last_ref[r]
        else:
            a, b = (inner_ref, outer_ref) if r >= 18 else (outer_ref, inner_ref)
            row = jnp.where(odd, a[r % 2], b[r % 2])
            (north_ref if r < 18 else south_ref)[r % 2] = row
            first, last = row[0:2], row[62:64]
        put_pair(east_odd, inner_out, outer_out, r, first, last)


def atmos_windows(flag_ref, windows, x_ref, s_ref, n_ref, in_ref, out_ref):
    odd = flag_ref[2] != 0
    west = jnp.where(odd, in_ref[0].astype(F32), out_ref[0].astype(F32))
    east = jnp.where(odd, out_ref[0].astype(F32), in_ref[0].astype(F32))
    build_windows(
        windows,
        34,
        lambda r: s_ref[0] if r == 0 else (n_ref[0] if r == 33 else x_ref[r - 1]),
        lambda r: west[r : r + 1, :],
        lambda r: east[r : r + 1, :],
    )


def packed_maps(p_ref):
    p = p_ref[...]
    zeros = jnp.zeros_like(p)
    return jnp.concatenate([p, zeros], 0), jnp.concatenate([zeros, p], 0)


def atmos_kernel(
    flag_ref, x_ref, s_ref, n_ref, in_ref, out_ref, w_ref, p_ref,
    act_ref, slope_ref, own_ref, inner_out, outer_out, first_ref, last_ref, windows,
):
    atmos_windows(flag_ref, windows, x_ref, s_ref, n_ref, in_ref, out_ref)
    maps = packed_maps(p_ref)
    for b in range(2):
        packed = jnp.zeros((512, 128), F32)
        for h in range(2):
            start = h * 1024 + b * 512
            pre = conv_rows(windows, w_ref, start, 512)
            sigma = sigmoid(pre)
            act = (pre * sigma).astype(BF)
            act_ref[start : start + 512, :] = act
            slope_ref[start : start + 512, :] = silu_slope(pre, sigma).astype(BF)
            packed += dot_back(act, maps[h])
        for u in range(8):
            r = b * 8 + u
            row = packed[u * 64 : u * 64 + 64].astype(BF)
            own_ref[r] = row
            first_ref[r] = row[0:2]
            last_ref[r] = row[62:64]
    for r in range(2):
        put_pair(flag_ref[1] != 0, inner_out, outer_out, r, own_ref[r], own_ref[14 + r])


def ocean_kernel(
    flag_ref, x_ref, s_ref, n_ref, first_ref, last_ref, in_ref, beyond_ref, c_ref, cs_ref, cn_ref, ci_ref, co_ref, m_ref,
    w_ref, wt_ref, inj_ref, out_ref, remap_ref, deltas, back,
    windows, sides, north, turned_north, dwin, dsides,
):
    top, odd = flag_ref[0] != 0, flag_ref[2] != 0
    west = [jnp.where(odd, in_ref[k].astype(F32), beyond_ref[k].astype(F32)) for k in range(2)]
    east = [jnp.where(odd, beyond_ref[k].astype(F32), in_ref[k].astype(F32)) for k in range(2)]
    cot_west = jnp.where(odd, ci_ref[1].astype(F32), co_ref[1].astype(F32))
    cot_east = jnp.where(odd, co_ref[1].astype(F32), ci_ref[1].astype(F32))
    land = m_ref[...].astype(F32).T
    build_windows(
        windows,
        36,
        lambda r: s_ref[r] if r < 2 else (n_ref[r - 34] if r >= 34 else x_ref[r - 2]),
        lambda r: west[1][r : r + 1, :],
        lambda r: east[0][r : r + 1, :],
    )
    sides[...] = jnp.zeros_like(sides)
    for side, columns in ((0, (west[0], west[1], first_ref[...])), (1, (last_ref[...], east[0], east[1]))):
        for q in range(3):
            sides[side, 0:36, q * 256 : q * 256 + 256] = columns[q].astype(F32)

    def side_rows(start, count):
        return jnp.concatenate([sides[0, start : start + count, :], sides[1, start : start + count, :]], 0).astype(BF)

    pre = jnp.zeros((80, 256), F32)
    lines = [jnp.concatenate([windows[(33 + r) * 64 : (34 + r) * 64, :], side_rows(33 + r, 8)], 0) for r in range(3)]
    for r in range(3):
        pre += jnp.dot(jnp.where(top, turned_lanes(lines[2 - r]), lines[r]), w_ref[r], preferred_element_type=F32)
    slope = silu_slope(pre, sigmoid(pre))
    d_north = (cn_ref[1].astype(F32) * slope[0:64]).astype(BF)
    side_pre = jnp.zeros((80, 256), F32)
    for r in range(3):
        side_pre += jnp.dot(side_rows(r, 40), w_ref[r], preferred_element_type=F32)
    side_slope = silu_slope(side_pre, sigmoid(side_pre))
    at = lax.broadcasted_iota(jnp.int32, (40, 256), 0)
    for side, cot in ((0, cot_west), (1, cot_east)):
        corner = slope[64 + side * 8 : 65 + side * 8]
        here = jnp.where(at == 33, corner, side_slope[side * 40 : side * 40 + 40])
        dsides[side] = jnp.zeros((40, 256), F32)
        dsides[side, 0:34, :] = cot * here[0:34]
    pre = conv_rows(windows, w_ref, 0, 64)
    d_south = (cs_ref[1].astype(F32) * silu_slope(pre, sigmoid(pre))).astype(BF)
    for b in range(4):
        pre = conv_rows(windows, w_ref, 64 + b * 512, 512)
        sigma = sigmoid(pre)
        act = pre * sigma
        slope = silu_slope(pre, sigma)
        for u in range(8):
            r = b * 8 + u
            here = slice(u * 64, u * 64 + 64)
            wet = land[:, r : r + 1]
            out_ref[r] = (wet * act[here]).astype(BF)
            deltas[r * 64 : r * 64 + 64, :] = (c_ref[r].astype(F32) * wet * slope[here]).astype(BF)
    dry = jnp.zeros((64, 256), BF)
    build_windows(
        dwin,
        34,
        lambda r: d_south if r == 0 else (dry if r == 33 else deltas[r * 64 - 64 : r * 64, :]),
        lambda r: dsides[0, r : r + 1, :] if r < 33 else dry[0:1],
        lambda r: dsides[1, r : r + 1, :] if r < 33 else dry[0:1],
        turned=True,
    )
    for dst, turned in ((north, False), (turned_north, True)):
        build_windows(
            dst, 1, lambda r: d_north, lambda r: dsides[0, 33:34, :], lambda r: dsides[1, 33:34, :], turned=turned
        )
    beyond = jnp.dot(
        jnp.where(top, north[...], turned_north[...]), wt_ref[jnp.where(top, 2, 0)], preferred_element_type=F32
    )
    inject = jnp.concatenate([inj_ref[...], inj_ref[...]], 0)
    for b in range(4):
        total = conv_rows(dwin, wt_ref, b * 512, 512, turned=True)
        for u in range(8):
            r = b * 8 + u
            value = total[u * 64 : u * 64 + 64]
            if r == 31:
                value = value + beyond
            back[r * 64 : r * 64 + 64, :] = (land[:, r : r + 1] * value).astype(BF)
        remap_ref[b * 512 : b * 512 + 512, :] = dot_back(back[b * 512 : b * 512 + 512, :], inject).astype(BF)


def ocean_grads_kernel(
    flag_ref, x_ref, s_ref, n_ref, in_ref, beyond_ref, deltas, back, rem_ref, keep_ref, send_ref, windows
):
    core, odd = flag_ref[1], flag_ref[2] != 0
    west = jnp.where(odd, in_ref[1].astype(F32), beyond_ref[1].astype(F32))
    east = jnp.where(odd, beyond_ref[0].astype(F32), in_ref[0].astype(F32))
    build_windows(
        windows,
        34,
        lambda r: s_ref[1] if r == 0 else (n_ref[0] if r == 33 else x_ref[r - 1]),
        lambda r: west[r + 1 : r + 2, :],
        lambda r: east[r + 1 : r + 2, :],
    )
    for r in range(3):
        value = dot_rows(windows[r * 64 : r * 64 + 2048, :], deltas[...])
        put_half(core, keep_ref, send_ref, slice(r * 768, r * 768 + 768), value)
    tail = jnp.concatenate([dot_rows(rem_ref[...], back[...])[0:64], jnp.zeros((32, 256), F32)], 0)
    put_half(core, keep_ref, send_ref, slice(2304, 2400), tail)


def credit_rows_kernel(flag_ref, n_ref, s_ref, in_ref, out_ref, inner_out, outer_out, n_sum, s_sum):
    odd, east_odd = flag_ref[1] != 0, flag_ref[2] != 0
    for r in range(2):
        for src, dst, first in ((n_ref, n_sum, 16), (s_ref, s_sum, 18)):
            inner, outer = in_ref[first + r].astype(F32), out_ref[first + r].astype(F32)
            dst[r] = src[r].astype(F32)
            dst[r, 0:2] = dst[r, 0:2] + jnp.where(east_odd, inner, outer)
            dst[r, 62:64] = dst[r, 62:64] + jnp.where(east_odd, outer, inner)
        put_pair(odd, inner_out, outer_out, r, s_sum[r].astype(BF), n_sum[r].astype(BF))


def atmos_back_kernel(
    flag_ref, x_ref, s_ref, n_ref, in_ref, out_ref, act_ref, slope_ref, own_ref, ci_ref, co_ref, ri_ref, ro_ref, bi_ref, bo_ref,
    low_ref, p_ref, keep_ref, send_ref, windows, deltas, total, credit,
):
    core = flag_ref[1]
    odd, east_odd = core != 0, flag_ref[2] != 0
    atmos_windows(flag_ref, windows, x_ref, s_ref, n_ref, in_ref, out_ref)
    maps = packed_maps(p_ref)
    for r in range(16):
        value = own_ref[r].astype(F32) + bi_ref[16 + r].astype(F32) + bo_ref[16 + r].astype(F32) + low_ref[r].astype(F32)
        if r < 2:
            value += jnp.where(odd, ri_ref[r].astype(F32), ro_ref[r].astype(F32))
        if r >= 14:
            value += jnp.where(odd, ro_ref[r - 14].astype(F32), ri_ref[r - 14].astype(F32))
        total[...] = value
        inner, outer = ci_ref[r].astype(F32), co_ref[r].astype(F32)
        total[0:2, :] += jnp.where(east_odd, inner, outer)
        total[62:64, :] += jnp.where(east_odd, outer, inner)
        credit[r * 64 : r * 64 + 64, :] = total[...].astype(BF)
    for h in range(2):
        here = slice(h * 1024, h * 1024 + 1024)
        back = jnp.dot(credit[...], maps[h], preferred_element_type=F32)
        deltas[here, :] = (back * slope_ref[here, :].astype(F32)).astype(BF)
    for r in range(3):
        value = dot_rows(windows[r * 64 : r * 64 + 2048, :], deltas[...])
        put_half(core, keep_ref, send_ref, slice(r * 768, r * 768 + 768), value)
    lower = dot_rows(credit[...], act_ref[0:1024, :])
    upper = dot_rows(credit[...], act_ref[1024:2048, :])
    tail = jnp.concatenate([lower[0:64] + upper[64:128], jnp.zeros((32, 256), F32)], 0)
    put_half(core, keep_ref, send_ref, slice(2304, 2400), tail)


def exchange(x, mask):
    count = lax.axis_size("lon") * lax.axis_size("lat")
    return lax.ppermute(x, AXES, [(i, i ^ mask) for i in range(count)])


def reduce_streams(streams, orders):
    rank = lax.axis_index("lon") * lax.axis_size("lat") + lax.axis_index("lat")
    bit = lambda n: (rank >> n) & 1
    near = [(2, bit(1) ^ bit(2)), (8, bit(3) ^ bit(4)), (32, bit(5) ^ bit(6))]
    far = (6, 24, 96)
    count = range(len(streams))
    for level in range(3):
        steps = [near[orders[i][level]] for i in count]
        half = streams[0].shape[0] // 2
        keep = [lax.dynamic_slice_in_dim(streams[i], steps[i][1] * half, half) for i in count]
        send = [lax.dynamic_slice_in_dim(streams[i], (1 - steps[i][1]) * half, half).astype(BF) for i in count]
        streams = [keep[i] + exchange(send[i], steps[i][0]).astype(F32) for i in count]
    streams = [s.astype(BF) for s in streams]
    for level in range(3):
        got = [exchange(streams[i], far[orders[i][level]]) for i in count]
        streams = [(streams[i].astype(F32) + got[i].astype(F32)).astype(BF) for i in count]
    for level in (2, 1, 0):
        steps = [near[orders[i][level]] for i in count]
        got = [exchange(streams[i], steps[i][0]) for i in count]
        streams = [
            jnp.where(
                steps[i][1] == 0,
                jnp.concatenate([streams[i], got[i]]),
                jnp.concatenate([got[i], streams[i]]),
            )
            for i in count
        ]
    return streams


def join_kernel(flag_ref, mine_ref, other_ref, main_ref, tail_ref):
    first = flag_ref[1] == 0
    for r in range(25):
        here = slice(r * 96, r * 96 + 96)
        mine, other = mine_ref[here, :], other_ref[here, :]
        low = jnp.where(first, mine, other).astype(F32)
        high = jnp.where(first, other, mine).astype(F32)
        if r < 24:
            main_ref[here, 0:128] = low
            main_ref[here, 128:256] = high
        else:
            tail_ref[:, 0:128] = low[0:64]
            tail_ref[:, 128:256] = high[0:64]


def lane_sign():
    lane = lax.broadcasted_iota(jnp.int32, (64, 128), 1)
    return jnp.where(lane < 64, jnp.float32(1.0), jnp.float32(-1.0))


def gather_kernel(
    flag_ref, slot_ref, w_ref, fn_ref, fs_ref, fi_ref, fo_ref, low_ref, own_ref, bi_ref, bo_ref, o_ref, m_ref, inj_ref,
    out_ref, mixed_ref, cols_ref, inner_ref, outer_ref, table, picked, cols,
):
    top = flag_ref[0]
    odd, east_odd = flag_ref[1] != 0, flag_ref[2] != 0

    @pl.when(top == 0)
    def _():
        for r in range(20):
            rows = own_ref[r] if r < 16 else (fn_ref[r - 16] if r < 18 else fs_ref[r - 18])
            table[r * NEAR : r * NEAR + 64, :] = rows.astype(F32)
            table[r * NEAR + 64 : r * NEAR + 66, :] = jnp.where(east_odd, fi_ref[r].astype(F32), fo_ref[r].astype(F32))
            table[r * NEAR + 66 : r * NEAR + 68, :] = jnp.where(east_odd, fo_ref[r].astype(F32), fi_ref[r].astype(F32))

    @pl.when(top != 0)
    def _():
        for r in range(32):
            base = r * BAND
            table[base : base + 64, :] = (low_ref[r] if r < 16 else own_ref[r - 16]).astype(F32)
            inner, outer = bi_ref[r].astype(F32), bo_ref[r].astype(F32)
            table[base + 64 : base + 128, :] = jnp.where(east_odd, inner, outer)
            table[base + 128 : base + 192, :] = jnp.where(east_odd, outer, inner)

    def step(q, carry):
        base = pl.multiple_of(q * 64, 64)
        for u in range(64):
            at = slot_ref[q, u]
            picked[pl.ds(base + u, 1), :] = table[pl.ds(at, 1), :]
        return carry

    lax.fori_loop(0, 128, step, 0)
    sign = lane_sign()
    wt = w_ref[...].T
    for row in range(32):
        acc = jnp.zeros((64, 128), F32)
        for k in range(4):
            q = row * 4 + k
            factor = jnp.maximum(wt[:, q : q + 1] * sign, 0.0)
            acc = acc + factor * picked[q * 64 : q * 64 + 64, :]
        acc = acc + pltpu.roll(acc, 64, 1)
        out_ref[row * 64 : row * 64 + 64, :] = acc.astype(BF)
    land = m_ref[...].astype(F32).T
    inject = jnp.concatenate([inj_ref[...], jnp.zeros_like(inj_ref[...])], 0)
    for b in range(4):
        injected = jnp.dot(out_ref[b * 512 : b * 512 + 512, :], inject, preferred_element_type=F32)
        for u in range(8):
            r = b * 8 + u
            value = land[:, r : r + 1] * (o_ref[r].astype(F32) + injected[u * 64 : u * 64 + 64])
            mixed_ref[r] = value.astype(BF)
            for c, i in enumerate((0, 1, 62, 63)):
                cols[c, r : r + 1, :] = value[i : i + 1]
    for r in range(2):
        put_pair(odd, inner_ref, outer_ref, r, mixed_ref[r], mixed_ref[30 + r])
    cols_ref[...] = cols[...].astype(BF)


def scatter_kernel(
    flag_ref, slot_ref, w_ref, g_ref, own_ref, n_ref, s_ref, side_in, side_out, low_ref, band_in, band_out, *scratch
):
    top = flag_ref[0]
    east_odd = flag_ref[2] != 0
    tables, parts = scratch[:8], scratch[8]

    def clear(count):
        def one(i, carry):
            base = pl.multiple_of(i * 96, 96)
            for t in tables:
                t[pl.ds(base, 96), :] = jnp.zeros((96, 128), F32)
            return carry

        lax.fori_loop(0, count // 96, one, 0)

    @pl.when(top == 0)
    def _():
        clear(20 * NEAR)

    @pl.when(top != 0)
    def _():
        clear(32 * BAND)

    sign = lane_sign()
    wt = w_ref[...].T
    for row in range(32):
        g = g_ref[row * 64 : row * 64 + 64, :].astype(F32)
        for k in range(4):
            q = row * 4 + k
            parts[q * 64 : q * 64 + 64, :] = jnp.maximum(wt[:, q : q + 1] * sign, 0.0) * g

    def step(row, carry):
        base = pl.multiple_of(row * 256, 256)
        for u in range(64):
            for k in range(4):
                at = slot_ref[row * 4 + k, u]
                t = tables[k + u % 2 * 4]
                t[pl.ds(at, 1), :] = t[pl.ds(at, 1), :] + parts[pl.ds(base + k * 64 + u, 1), :]
        return carry

    lax.fori_loop(0, 32, step, 0)

    def total(start, size):
        where = pl.ds(start, size)
        pairs = [tables[k][where, :] + tables[k + 4][where, :] for k in range(4)]
        return ((pairs[0] + pairs[1]) + (pairs[2] + pairs[3])).astype(BF)

    @pl.when(top == 0)
    def _():
        for r in range(20):
            rows = total(r * NEAR, 64)
            if r < 16:
                own_ref[r] = rows
            elif r < 18:
                n_ref[r - 16] = rows
            else:
                s_ref[r - 18] = rows
            put_pair(east_odd, side_in, side_out, r, total(r * NEAR + 64, 2), total(r * NEAR + 66, 2))

    @pl.when(top != 0)
    def _():
        for r in range(2):
            n_ref[r] = jnp.zeros((64, 128), BF)
            s_ref[r] = jnp.zeros((64, 128), BF)
        side_in[...] = jnp.zeros_like(side_in)
        side_out[...] = jnp.zeros_like(side_out)
        for r in range(32):
            base = r * BAND
            if r < 16:
                low_ref[r] = total(base, 64)
            else:
                own_ref[r - 16] = total(base, 64)
            put_pair(east_odd, band_in, band_out, r, total(base + 64, 64), total(base + 128, 64))


def entry_slots(source_row, source_col, weight, is_top, row_count, col_count):
    nx = col_count * lax.axis_size("lon")
    row = source_row - lax.axis_index("lat") * row_count
    col = jnp.remainder(source_col - lax.axis_index("lon") * col_count + nx // 2, nx) - nx // 2
    half = row_count // 2
    inside = (row >= 0) & (row < row_count)
    wrapped = row & (row_count - 1)
    packed = wrapped & (half - 1)
    upper = wrapped >= half
    near_row = jnp.where(inside, packed, jnp.where(row < 0, packed + 4, packed + half))
    near_col = jnp.where((col >= 0) & (col < col_count), col, jnp.where(col < 0, col + col_count + 2, col + 2))
    band_row = jnp.where(row >= 0, packed + half, packed)
    band_col = jnp.where((col >= 0) & (col < col_count), col, jnp.where(col < 0, col + 2 * col_count, col + col_count))
    slot = jnp.where(is_top, band_row * BAND + band_col, near_row * NEAR + near_col)
    signed = jnp.where(upper, -weight, weight)
    order = lambda x: jnp.transpose(x, (0, 2, 1)).reshape(-1, col_count)
    return order(slot), order(signed)


def body(
    atmos_state,
    atmos_weights,
    flux_project,
    source_row,
    source_col,
    intersection_weight,
    ocean_state,
    flux_inject,
    ocean_mask,
    ocean_weights,
    out_cotangent,
):
    row_count, col_count, chans = atmos_state.shape
    flux_chans = flux_project.shape[1]
    cells = row_count * col_count
    half = cells // 2
    lats = lax.axis_size("lat")
    is_top = lax.axis_index("lat") == lats - 1
    core = lax.rem(lax.axis_index("lat"), 2)
    flags = jnp.stack([is_top.astype(jnp.int32), core, lax.rem(lax.axis_index("lon"), 2)])
    struct = lambda *shape: (shape, BF)
    block = lambda shape, at: pl.BlockSpec(shape, lambda i: (at[0], at[1], 0))
    row = (1, 64, 256)
    inner, outer = call(
        rows_kernel,
        "rows",
        (struct(2, 64, 256), struct(2, 64, 256)),
        (flags, atmos_state, atmos_state, out_cotangent, out_cotangent, ocean_mask),
        specs=[SMEM, block(row, (0, 0)), block(row, (31, 0)), block(row, (0, 0)), block(row, (31, 0)), VMEM],
        grid=(1,),
    )
    inner, outer = lat_pairs(inner, outer, True)
    slab = (32, 16, 256)
    inner, outer, south, north = call(
        edges_kernel,
        "edges",
        (struct(2, 34, 256), struct(2, 34, 256), struct(2, 64, 256), struct(2, 64, 256)),
        (flags, atmos_state, atmos_state, out_cotangent, out_cotangent, ocean_mask, inner, outer),
        [pltpu.VMEM((4, 34, 256), F32)],
        specs=[SMEM, block(slab, (0, 0)), block(slab, (0, 3)), block(slab, (0, 0)), block(slab, (0, 3))] + [VMEM] * 3,
        grid=(1,),
    )
    side_in, side_out = lon_pairs(inner, outer)
    project = flux_project.T
    atmos_w = atmos_weights.reshape(3, 3 * chans, chans)
    ocean_w = ocean_weights.reshape(3, 3 * chans, chans)
    act, slope, own, inner, outer, first, last = call(
        atmos_kernel,
        "atmos",
        (struct(cells, chans), struct(cells, chans), struct(16, 64, 128), struct(2, 64, 128), struct(2, 64, 128),
         struct(16, 2, 128), struct(16, 2, 128)),
        (flags, atmos_state, south, north, side_in, side_out, atmos_w, project),
        [pltpu.VMEM((34 * 64, 768), BF)],
        scalars=1,
    )
    low_tile = lax.ppermute(own, "lat", [(lats - 2, lats - 1)])
    inner, outer = lat_pairs(inner, outer, False)
    two, inner, outer = lax.optimization_barrier((jnp.concatenate([low_tile, own], 0), inner, outer))
    band_in, band_out = lon_pairs(two, two, lats - 1)
    flux_south, flux_north, inner, outer = call(
        flux_edges_kernel,
        "flux_edges",
        (struct(2, 64, 128), struct(2, 64, 128), struct(20, 2, 128), struct(20, 2, 128)),
        (flags, first, last, inner, outer),
        scalars=1,
    )
    flux_in, flux_out = lon_pairs(inner, outer, 0, lats - 1)
    late = lax.optimization_barrier((own, source_row, source_col, intersection_weight, ocean_weights))
    slots, signed = entry_slots(*late[1:4], is_top, row_count, col_count)
    back_w = jnp.transpose(late[4], (0, 2, 1)).reshape(3, 3 * chans, chans)
    remapped, mixed, cols, inner, outer = call(
        gather_kernel,
        "gather_mix",
        (struct(cells, 128), struct(32, 64, 256), struct(4, 32, 256), struct(2, 64, 256), struct(2, 64, 256)),
        (flags, slots, signed, flux_north, flux_south, flux_in, flux_out, low_tile, own, band_in, band_out,
         ocean_state, ocean_mask, flux_inject),
        [pltpu.VMEM((32 * BAND, 128), F32), pltpu.VMEM((8192, 128), F32), pltpu.VMEM((4, 32, 256), F32)],
        scalars=2,
    )
    inner, outer = lat_pairs(inner, outer, True)
    inner, outer, first, last, mixed_south, mixed_north = call(
        mixed_edges_kernel,
        "mixed_edges",
        (struct(2, 36, 256), struct(2, 36, 256), struct(36, 256), struct(36, 256), struct(2, 64, 256), struct(2, 64, 256)),
        (flags, cols, inner, outer),
        [pltpu.VMEM((4, 36, 256), F32)],
        scalars=1,
    )
    mixed_in, mixed_out = lon_pairs(inner, outer)
    halves = ((GRAD_ROWS, 128), F32), ((GRAD_ROWS, 128), BF)
    ocean_out, remap_grad, deltas, back = call(
        ocean_kernel,
        "ocean",
        (struct(32, 64, 256), struct(cells, 128), struct(cells, 256), struct(cells, 256)),
        (
            flags, mixed, mixed_south, mixed_north, first, last, mixed_in, mixed_out,
            out_cotangent, south, north, side_in, side_out, ocean_mask, ocean_w, back_w, flux_inject,
        ),
        [
            pltpu.VMEM((36 * 64, 768), BF),
            pltpu.VMEM((2, 48, 768), F32),
            pltpu.VMEM((64, 768), BF),
            pltpu.VMEM((64, 768), BF),
            pltpu.VMEM((34 * 64, 768), BF),
            pltpu.VMEM((2, 40, 256), F32),
        ],
        scalars=1,
    )
    own, to_north, to_south, inner, outer, low_tile, band_in, band_out = call(
        scatter_kernel,
        "scatter_rows",
        (struct(16, 64, 128), struct(2, 64, 128), struct(2, 64, 128), struct(20, 2, 128), struct(20, 2, 128),
         struct(16, 64, 128), struct(32, 64, 128), struct(32, 64, 128)),
        (flags, slots, signed, remap_grad),
        [pltpu.VMEM((32 * BAND, 128), F32)] * 8 + [pltpu.VMEM((8192, 128), F32)],
        scalars=2,
    )
    deltas, back, inner, outer, band_in, band_out = lax.optimization_barrier((deltas, back, inner, outer, band_in, band_out))
    ocean_keep, ocean_send = call(
        ocean_grads_kernel,
        "ocean_grads",
        halves,
        (flags, mixed, mixed_south, mixed_north, mixed_in, mixed_out, deltas, back, remapped),
        [pltpu.VMEM((34 * 64, 768), BF)],
        scalars=1,
    )
    band_in, band_out = lon_pairs(band_in, band_out, lats - 1)
    credit_in, credit_out = lon_pairs(inner, outer, 0, lats - 1)
    credit_in, credit_out, ocean_keep, ocean_send = lax.optimization_barrier(
        (credit_in, credit_out, ocean_keep, ocean_send)
    )
    inner, outer = call(
        credit_rows_kernel,
        "credit_rows",
        (struct(2, 64, 128),) * 2,
        (flags, to_north, to_south, credit_in, credit_out),
        [pltpu.VMEM((2, 64, 128), F32)] * 2,
        scalars=1,
    )
    rows_in, rows_out = lat_pairs(inner, outer, False)
    band_in, band_out, rows_in, rows_out = lax.optimization_barrier((band_in, band_out, rows_in, rows_out))
    low_tile = low_tile.astype(F32) + band_in[:16].astype(F32) + band_out[:16].astype(F32)
    from_band = lax.ppermute(low_tile.astype(BF), "lat", [(lats - 1, lats - 2)])
    atmos_keep, atmos_send = call(
        atmos_back_kernel,
        "atmos_back",
        halves,
        (flags, atmos_state, south, north, side_in, side_out, act, slope, own, credit_in, credit_out, rows_in, rows_out,
         band_in, band_out, from_band, project),
        [pltpu.VMEM((34 * 64, 768), BF), pltpu.VMEM((cells, 256), BF), pltpu.VMEM((64, 128), F32), pltpu.VMEM((half, 128), BF)],
        scalars=1,
    )
    ocean = ocean_keep + exchange(ocean_send, 1).astype(F32)
    ocean, atmos = lax.optimization_barrier((ocean, atmos_keep + exchange(atmos_send, 1).astype(F32)))
    cut = 1600
    rest = GRAD_ROWS - cut
    sums = reduce_streams(
        [ocean[:cut], jnp.concatenate([ocean[cut:], atmos[:rest]]), atmos[rest:]], ((0, 1, 2), (1, 2, 0), (2, 0, 1))
    )
    ocean = jnp.concatenate([sums[0], sums[1][:rest]])
    atmos = jnp.concatenate([sums[1][rest:], sums[2]])

    def joined(mine):
        main, tail = call(
            join_kernel,
            "join",
            (((9 * chans, chans), F32), ((flux_chans, chans), F32)),
            (flags, mine, exchange(mine, 1)),
            scalars=1,
        )
        return main.reshape(9, chans, chans), tail

    grad_ocean, grad_inject = joined(ocean)
    grad_atmos, grad_project = joined(atmos)
    return (ocean_out, grad_atmos, grad_ocean, grad_project.T, grad_inject)


def solution(mesh):
    return jax.shard_map(
        body,
        mesh=mesh,
        in_specs=(
            P("lat", "lon", None),
            P(),
            P(),
            P("lat", "lon", None),
            P("lat", "lon", None),
            P("lat", "lon", None),
            P("lat", "lon", None),
            P(),
            P("lat", "lon"),
            P(),
            P("lat", "lon", None),
        ),
        out_specs=(P("lat", "lon", None), P(), P(), P(), P()),
        check_vma=False,
    )
```

```python
import jax
import jax.numpy as jnp
from jax import lax
from jax.experimental import pallas as pl
from jax.experimental.pallas import tpu as pltpu
from jax.sharding import PartitionSpec as P

BF = jnp.bfloat16
F32 = jnp.float32
MIB = 1 << 20
LIMITS = {"atmos": 20, "gather_mix": 20, "ocean": 28, "scatter_rows": 36, "ocean_grads": 18, "atmos_back": 18}
AXES = ("lon", "lat")
NEAR = 72
BAND = 192


def lat_pairs(inner, outer, fold):
    lons, lats = lax.axis_size("lon"), lax.axis_size("lat")
    at = lambda i, j: i * lats + j
    inside = [(at(i, j), at(i, j ^ 1)) for i in range(lons) for j in range(lats)]
    across = [(at(i, j), at(i, j + 1 if j % 2 else j - 1)) for i in range(lons) for j in range(1, lats - 1)]
    if fold:
        across += [(at(i, lats - 1), at(lons - 1 - i, lats - 1)) for i in range(lons)]
    return lax.ppermute(inner, AXES, inside), lax.ppermute(outer, AXES, across)


def lon_pairs(inner, outer, first=0, last=None):
    lons, lats = lax.axis_size("lon"), lax.axis_size("lat")
    here = range(first, lats if last is None else last)
    inside = [(i * lats + j, (i ^ 1) * lats + j) for i in range(lons) for j in here]
    across = [(i * lats + j, ((i + 1 if i % 2 else i - 1) % lons) * lats + j) for i in range(lons) for j in here]
    return lax.ppermute(inner, AXES, inside), lax.ppermute(outer, AXES, across)


def sigmoid(value):
    return 1.0 / (1.0 + jnp.exp(-value))


def silu_slope(value, sigma):
    return sigma * (1.0 + value * (1.0 - sigma))


VMEM = pl.BlockSpec(memory_space=pltpu.VMEM)
SMEM = pl.BlockSpec(memory_space=pltpu.SMEM)
GRAD_ROWS = 2400


def call(kernel, name, outs, ins, scratch=(), scalars=0, specs=None, grid=None):
    if specs is None:
        specs = [SMEM] * scalars + [VMEM] * (len(ins) - scalars)
    extra = {} if grid is None else {"grid": grid}
    return pl.pallas_call(
        kernel,
        name=name,
        out_shape=tuple(jax.ShapeDtypeStruct(shape, kind) for shape, kind in outs),
        in_specs=specs,
        out_specs=(VMEM,) * len(outs),
        scratch_shapes=list(scratch),
        compiler_params=pltpu.CompilerParams(vmem_limit_bytes=LIMITS.get(name, 8) * MIB),
        **extra,
    )(*ins)


def turned_row(row):
    a = lax.broadcasted_iota(jnp.int32, (64, 64), 0)
    b = lax.broadcasted_iota(jnp.int32, (64, 64), 1)
    flip = jnp.where(a + b == 63, jnp.float32(1.0), jnp.float32(0.0)).astype(BF)
    return jnp.dot(flip, row, preferred_element_type=F32)


def build_windows(dst, rows, row_of, west_of, east_of, turned=False):
    first, last = (512, 0) if turned else (0, 512)
    at = lax.broadcasted_iota(jnp.int32, (64, 256), 0)
    for r in range(rows):
        value = row_of(r)
        wide = value.astype(F32)
        left = jnp.where(at == 0, west_of(r).astype(F32), pltpu.roll(wide, 1, 0))
        right = jnp.where(at == 63, east_of(r).astype(F32), pltpu.roll(wide, 63, 0))
        here = slice(r * 64, r * 64 + 64)
        dst[here, first : first + 256] = left.astype(BF)
        dst[here, 256:512] = value
        dst[here, last : last + 256] = right.astype(BF)


def conv_rows(windows, w, start, count, turned=False):
    acc = jnp.zeros((count, 256), F32)
    for r in range(3):
        taps = w[2 - r if turned else r]
        acc += jnp.dot(windows[start + r * 64 : start + r * 64 + count, :], taps, preferred_element_type=F32)
    return acc


def dot_back(a, b):
    return lax.dot_general(a, b, (((1,), (1,)), ((), ())), preferred_element_type=F32)


def turned_lanes(x):
    return jnp.concatenate([x[:, 512:768], x[:, 256:512], x[:, 0:256]], 1)


def put_half(core, keep_ref, send_ref, here, value):
    low, high = value[:, 0:128], value[:, 128:256]
    keep_ref[here, :] = jnp.where(core == 0, low, high)
    send_ref[here, :] = jnp.where(core == 0, high, low).astype(BF)


def dot_rows(a, b):
    return lax.dot_general(a, b, (((0,), (0,)), ((), ())), preferred_element_type=F32)


def put_pair(odd, inner_ref, outer_ref, r, low, high):
    inner_ref[r] = jnp.where(odd, low, high)
    outer_ref[r] = jnp.where(odd, high, low)


def rows_kernel(flag_ref, a0_ref, a1_ref, c0_ref, c1_ref, m_ref, inner_ref, outer_ref):
    odd = flag_ref[1] != 0
    land = m_ref[...].astype(F32).T
    put_pair(odd, inner_ref, outer_ref, 0, a0_ref[0], a1_ref[0])
    low = (c0_ref[0].astype(F32) * land[:, 0:1]).astype(BF)
    high = (c1_ref[0].astype(F32) * land[:, 31:32]).astype(BF)
    put_pair(odd, inner_ref, outer_ref, 1, low, high)


def edges_kernel(
    flag_ref, a0_ref, a1_ref, c0_ref, c1_ref, m_ref, inner_ref, outer_ref, inner_out, outer_out, s_ref, n_ref, cols
):
    top, odd = flag_ref[0] != 0, flag_ref[1] != 0
    land = m_ref[...].astype(F32).T
    for r in range(2):
        s_ref[r] = jnp.where(odd, inner_ref[r], outer_ref[r])
    north = jnp.where(odd, outer_ref[0], inner_ref[0]).astype(F32)
    north = jnp.where(top, jnp.zeros_like(north), north)
    cn = jnp.where(odd, outer_ref[1], inner_ref[1])
    cn = jnp.where(top, turned_row(cn), cn.astype(F32))
    n_ref[0], n_ref[1] = north.astype(BF), cn.astype(BF)
    for r in range(32):
        here = slice(r + 1, r + 2)
        cols[0, here, :] = a0_ref[r, 0:1].astype(F32)
        cols[1, here, :] = c0_ref[r, 0:1].astype(F32) * land[0:1, r : r + 1]
        cols[2, here, :] = a1_ref[r, 15:16].astype(F32)
        cols[3, here, :] = c1_ref[r, 15:16].astype(F32) * land[63:64, r : r + 1]
    for k, (row, i) in enumerate(((s_ref[0], 0), (s_ref[1], 0), (s_ref[0], 63), (s_ref[1], 63))):
        cols[k, 0:1, :] = row[i : i + 1].astype(F32)
    for k, (row, i) in enumerate(((north, 0), (cn, 0), (north, 63), (cn, 63))):
        cols[k, 33:34, :] = row[i : i + 1]
    put_pair(flag_ref[2] != 0, inner_out, outer_out, slice(0, 2), cols[0:2].astype(BF), cols[2:4].astype(BF))


def mixed_edges_kernel(
    flag_ref, cols_in, inner_ref, outer_ref, inner_out, outer_out, first_ref, last_ref, south_ref, north_ref, cols
):
    top, odd = flag_ref[0] != 0, flag_ref[1] != 0
    for r in range(2):
        south_ref[r] = jnp.where(odd, inner_ref[r], outer_ref[r])
        s = south_ref[r].astype(F32)
        n = jnp.where(odd, outer_ref[r], inner_ref[r]).astype(F32)
        n = jnp.where(top, turned_row(outer_ref[1 - r]), n)
        north_ref[r] = n.astype(BF)
        for k, i in enumerate((0, 1, 62, 63)):
            cols[k, r : r + 1, :] = s[i : i + 1]
            cols[k, 34 + r : 35 + r, :] = n[i : i + 1]
    for k in range(4):
        cols[k, 2:34, :] = cols_in[k].astype(F32)
    first_ref[...] = cols[0].astype(BF)
    last_ref[...] = cols[3].astype(BF)
    put_pair(flag_ref[2] != 0, inner_out, outer_out, slice(0, 2), cols[0:2].astype(BF), cols[2:4].astype(BF))


def flux_edges_kernel(flag_ref, first_ref, last_ref, inner_ref, outer_ref, south_ref, north_ref, inner_out, outer_out):
    odd, east_odd = flag_ref[1] != 0, flag_ref[2] != 0
    for r in range(20):
        if r < 16:
            first, last = first_ref[r], last_ref[r]
        else:
            a, b = (inner_ref, outer_ref) if r >= 18 else (outer_ref, inner_ref)
            row = jnp.where(odd, a[r % 2], b[r % 2])
            (north_ref if r < 18 else south_ref)[r % 2] = row
            first, last = row[0:2], row[62:64]
        put_pair(east_odd, inner_out, outer_out, r, first, last)


def atmos_windows(flag_ref, windows, x_ref, s_ref, n_ref, in_ref, out_ref):
    odd = flag_ref[2] != 0
    west = jnp.where(odd, in_ref[0].astype(F32), out_ref[0].astype(F32))
    east = jnp.where(odd, out_ref[0].astype(F32), in_ref[0].astype(F32))
    build_windows(
        windows,
        34,
        lambda r: s_ref[0] if r == 0 else (n_ref[0] if r == 33 else x_ref[r - 1]),
        lambda r: west[r : r + 1, :],
        lambda r: east[r : r + 1, :],
    )


def packed_maps(p_ref):
    p = p_ref[...]
    zeros = jnp.zeros_like(p)
    return jnp.concatenate([p, zeros], 0), jnp.concatenate([zeros, p], 0)


def atmos_kernel(
    flag_ref, x_ref, s_ref, n_ref, in_ref, out_ref, w_ref, p_ref,
    act_ref, slope_ref, own_ref, inner_out, outer_out, first_ref, last_ref, windows,
):
    atmos_windows(flag_ref, windows, x_ref, s_ref, n_ref, in_ref, out_ref)
    maps = packed_maps(p_ref)
    for b in range(2):
        packed = jnp.zeros((512, 128), F32)
        for h in range(2):
            start = h * 1024 + b * 512
            pre = conv_rows(windows, w_ref, start, 512)
            sigma = sigmoid(pre)
            act = (pre * sigma).astype(BF)
            act_ref[start : start + 512, :] = act
            slope_ref[start : start + 512, :] = silu_slope(pre, sigma).astype(BF)
            packed += dot_back(act, maps[h])
        for u in range(8):
            r = b * 8 + u
            row = packed[u * 64 : u * 64 + 64].astype(BF)
            own_ref[r] = row
            first_ref[r] = row[0:2]
            last_ref[r] = row[62:64]
    for r in range(2):
        put_pair(flag_ref[1] != 0, inner_out, outer_out, r, own_ref[r], own_ref[14 + r])


def ocean_kernel(
    flag_ref, x_ref, s_ref, n_ref, first_ref, last_ref, in_ref, beyond_ref, c_ref, cs_ref, cn_ref, ci_ref, co_ref, m_ref,
    w_ref, wt_ref, inj_ref, out_ref, remap_ref, deltas, back,
    windows, sides, north, turned_north, dwin, dsides,
):
    top, odd = flag_ref[0] != 0, flag_ref[2] != 0
    west = [jnp.where(odd, in_ref[k].astype(F32), beyond_ref[k].astype(F32)) for k in range(2)]
    east = [jnp.where(odd, beyond_ref[k].astype(F32), in_ref[k].astype(F32)) for k in range(2)]
    cot_west = jnp.where(odd, ci_ref[1].astype(F32), co_ref[1].astype(F32))
    cot_east = jnp.where(odd, co_ref[1].astype(F32), ci_ref[1].astype(F32))
    land = m_ref[...].astype(F32).T
    build_windows(
        windows,
        36,
        lambda r: s_ref[r] if r < 2 else (n_ref[r - 34] if r >= 34 else x_ref[r - 2]),
        lambda r: west[1][r : r + 1, :],
        lambda r: east[0][r : r + 1, :],
    )
    sides[...] = jnp.zeros_like(sides)
    for side, columns in ((0, (west[0], west[1], first_ref[...])), (1, (last_ref[...], east[0], east[1]))):
        for q in range(3):
            sides[side, 0:36, q * 256 : q * 256 + 256] = columns[q].astype(F32)

    def side_rows(start, count):
        return jnp.concatenate([sides[0, start : start + count, :], sides[1, start : start + count, :]], 0).astype(BF)

    pre = jnp.zeros((80, 256), F32)
    lines = [jnp.concatenate([windows[(33 + r) * 64 : (34 + r) * 64, :], side_rows(33 + r, 8)], 0) for r in range(3)]
    for r in range(3):
        pre += jnp.dot(jnp.where(top, turned_lanes(lines[2 - r]), lines[r]), w_ref[r], preferred_element_type=F32)
    slope = silu_slope(pre, sigmoid(pre))
    d_north = (cn_ref[1].astype(F32) * slope[0:64]).astype(BF)
    side_pre = jnp.zeros((80, 256), F32)
    for r in range(3):
        side_pre += jnp.dot(side_rows(r, 40), w_ref[r], preferred_element_type=F32)
    side_slope = silu_slope(side_pre, sigmoid(side_pre))
    at = lax.broadcasted_iota(jnp.int32, (40, 256), 0)
    for side, cot in ((0, cot_west), (1, cot_east)):
        corner = slope[64 + side * 8 : 65 + side * 8]
        here = jnp.where(at == 33, corner, side_slope[side * 40 : side * 40 + 40])
        dsides[side] = jnp.zeros((40, 256), F32)
        dsides[side, 0:34, :] = cot * here[0:34]
    pre = conv_rows(windows, w_ref, 0, 64)
    d_south = (cs_ref[1].astype(F32) * silu_slope(pre, sigmoid(pre))).astype(BF)
    for b in range(4):
        pre = conv_rows(windows, w_ref, 64 + b * 512, 512)
        sigma = sigmoid(pre)
        act = pre * sigma
        slope = silu_slope(pre, sigma)
        for u in range(8):
            r = b * 8 + u
            here = slice(u * 64, u * 64 + 64)
            wet = land[:, r : r + 1]
            out_ref[r] = (wet * act[here]).astype(BF)
            deltas[r * 64 : r * 64 + 64, :] = (c_ref[r].astype(F32) * wet * slope[here]).astype(BF)
    dry = jnp.zeros((64, 256), BF)
    build_windows(
        dwin,
        34,
        lambda r: d_south if r == 0 else (dry if r == 33 else deltas[r * 64 - 64 : r * 64, :]),
        lambda r: dsides[0, r : r + 1, :] if r < 33 else dry[0:1],
        lambda r: dsides[1, r : r + 1, :] if r < 33 else dry[0:1],
        turned=True,
    )
    for dst, turned in ((north, False), (turned_north, True)):
        build_windows(
            dst, 1, lambda r: d_north, lambda r: dsides[0, 33:34, :], lambda r: dsides[1, 33:34, :], turned=turned
        )
    beyond = jnp.dot(
        jnp.where(top, north[...], turned_north[...]), wt_ref[jnp.where(top, 2, 0)], preferred_element_type=F32
    )
    inject = jnp.concatenate([inj_ref[...], inj_ref[...]], 0)
    for b in range(4):
        total = conv_rows(dwin, wt_ref, b * 512, 512, turned=True)
        for u in range(8):
            r = b * 8 + u
            value = total[u * 64 : u * 64 + 64]
            if r == 31:
                value = value + beyond
            back[r * 64 : r * 64 + 64, :] = (land[:, r : r + 1] * value).astype(BF)
        remap_ref[b * 512 : b * 512 + 512, :] = dot_back(back[b * 512 : b * 512 + 512, :], inject).astype(BF)


def ocean_grads_kernel(
    flag_ref, x_ref, s_ref, n_ref, in_ref, beyond_ref, deltas, back, rem_ref, keep_ref, send_ref, windows
):
    core, odd = flag_ref[1], flag_ref[2] != 0
    west = jnp.where(odd, in_ref[1].astype(F32), beyond_ref[1].astype(F32))
    east = jnp.where(odd, beyond_ref[0].astype(F32), in_ref[0].astype(F32))
    build_windows(
        windows,
        34,
        lambda r: s_ref[1] if r == 0 else (n_ref[0] if r == 33 else x_ref[r - 1]),
        lambda r: west[r + 1 : r + 2, :],
        lambda r: east[r + 1 : r + 2, :],
    )
    for r in range(3):
        value = dot_rows(windows[r * 64 : r * 64 + 2048, :], deltas[...])
        put_half(core, keep_ref, send_ref, slice(r * 768, r * 768 + 768), value)
    tail = jnp.concatenate([dot_rows(rem_ref[...], back[...])[0:64], jnp.zeros((32, 256), F32)], 0)
    put_half(core, keep_ref, send_ref, slice(2304, 2400), tail)


def credit_rows_kernel(flag_ref, n_ref, s_ref, in_ref, out_ref, inner_out, outer_out, n_sum, s_sum):
    odd, east_odd = flag_ref[1] != 0, flag_ref[2] != 0
    for r in range(2):
        for src, dst, first in ((n_ref, n_sum, 16), (s_ref, s_sum, 18)):
            inner, outer = in_ref[first + r].astype(F32), out_ref[first + r].astype(F32)
            dst[r] = src[r].astype(F32)
            dst[r, 0:2] = dst[r, 0:2] + jnp.where(east_odd, inner, outer)
            dst[r, 62:64] = dst[r, 62:64] + jnp.where(east_odd, outer, inner)
        put_pair(odd, inner_out, outer_out, r, s_sum[r].astype(BF), n_sum[r].astype(BF))


def atmos_back_kernel(
    flag_ref, x_ref, s_ref, n_ref, in_ref, out_ref, act_ref, slope_ref, own_ref, ci_ref, co_ref, ri_ref, ro_ref, bi_ref, bo_ref,
    low_ref, p_ref, keep_ref, send_ref, windows, deltas, total, credit,
):
    core = flag_ref[1]
    odd, east_odd = core != 0, flag_ref[2] != 0
    atmos_windows(flag_ref, windows, x_ref, s_ref, n_ref, in_ref, out_ref)
    maps = packed_maps(p_ref)
    for r in range(16):
        value = own_ref[r].astype(F32) + bi_ref[16 + r].astype(F32) + bo_ref[16 + r].astype(F32) + low_ref[r].astype(F32)
        if r < 2:
            value += jnp.where(odd, ri_ref[r].astype(F32), ro_ref[r].astype(F32))
        if r >= 14:
            value += jnp.where(odd, ro_ref[r - 14].astype(F32), ri_ref[r - 14].astype(F32))
        total[...] = value
        inner, outer = ci_ref[r].astype(F32), co_ref[r].astype(F32)
        total[0:2, :] += jnp.where(east_odd, inner, outer)
        total[62:64, :] += jnp.where(east_odd, outer, inner)
        credit[r * 64 : r * 64 + 64, :] = total[...].astype(BF)
    for h in range(2):
        here = slice(h * 1024, h * 1024 + 1024)
        back = jnp.dot(credit[...], maps[h], preferred_element_type=F32)
        deltas[here, :] = (back * slope_ref[here, :].astype(F32)).astype(BF)
    for r in range(3):
        value = dot_rows(windows[r * 64 : r * 64 + 2048, :], deltas[...])
        put_half(core, keep_ref, send_ref, slice(r * 768, r * 768 + 768), value)
    lower = dot_rows(credit[...], act_ref[0:1024, :])
    upper = dot_rows(credit[...], act_ref[1024:2048, :])
    tail = jnp.concatenate([lower[0:64] + upper[64:128], jnp.zeros((32, 256), F32)], 0)
    put_half(core, keep_ref, send_ref, slice(2304, 2400), tail)


def exchange(x, mask):
    count = lax.axis_size("lon") * lax.axis_size("lat")
    return lax.ppermute(x, AXES, [(i, i ^ mask) for i in range(count)])


def reduce_streams(streams, orders):
    rank = lax.axis_index("lon") * lax.axis_size("lat") + lax.axis_index("lat")
    bit = lambda n: (rank >> n) & 1
    near = [(2, bit(1) ^ bit(2)), (8, bit(3) ^ bit(4)), (32, bit(5) ^ bit(6))]
    far = (6, 24, 96)
    count = range(len(streams))
    for level in range(3):
        steps = [near[orders[i][level]] for i in count]
        half = streams[0].shape[0] // 2
        keep = [lax.dynamic_slice_in_dim(streams[i], steps[i][1] * half, half) for i in count]
        send = [lax.dynamic_slice_in_dim(streams[i], (1 - steps[i][1]) * half, half).astype(BF) for i in count]
        streams = [keep[i] + exchange(send[i], steps[i][0]).astype(F32) for i in count]
    streams = [s.astype(BF) for s in streams]
    for level in range(3):
        got = [exchange(streams[i], far[orders[i][level]]) for i in count]
        streams = [(streams[i].astype(F32) + got[i].astype(F32)).astype(BF) for i in count]
    for level in (2, 1, 0):
        steps = [near[orders[i][level]] for i in count]
        got = [exchange(streams[i], steps[i][0]) for i in count]
        streams = [
            jnp.where(
                steps[i][1] == 0,
                jnp.concatenate([streams[i], got[i]]),
                jnp.concatenate([got[i], streams[i]]),
            )
            for i in count
        ]
    return streams


def lane_sign():
    lane = lax.broadcasted_iota(jnp.int32, (64, 128), 1)
    return jnp.where(lane < 64, jnp.float32(1.0), jnp.float32(-1.0))


def gather_kernel(
    flag_ref, slot_ref, w_ref, fn_ref, fs_ref, fi_ref, fo_ref, low_ref, own_ref, bi_ref, bo_ref, o_ref, m_ref, inj_ref,
    out_ref, mixed_ref, cols_ref, inner_ref, outer_ref, table, picked, cols,
):
    top = flag_ref[0]
    odd, east_odd = flag_ref[1] != 0, flag_ref[2] != 0

    @pl.when(top == 0)
    def _():
        for r in range(20):
            rows = own_ref[r] if r < 16 else (fn_ref[r - 16] if r < 18 else fs_ref[r - 18])
            table[r * NEAR : r * NEAR + 64, :] = rows.astype(F32)
            table[r * NEAR + 64 : r * NEAR + 66, :] = jnp.where(east_odd, fi_ref[r].astype(F32), fo_ref[r].astype(F32))
            table[r * NEAR + 66 : r * NEAR + 68, :] = jnp.where(east_odd, fo_ref[r].astype(F32), fi_ref[r].astype(F32))

    @pl.when(top != 0)
    def _():
        for r in range(32):
            base = r * BAND
            table[base : base + 64, :] = (low_ref[r] if r < 16 else own_ref[r - 16]).astype(F32)
            inner, outer = bi_ref[r].astype(F32), bo_ref[r].astype(F32)
            table[base + 64 : base + 128, :] = jnp.where(east_odd, inner, outer)
            table[base + 128 : base + 192, :] = jnp.where(east_odd, outer, inner)

    def step(q, carry):
        base = pl.multiple_of(q * 64, 64)
        for u in range(64):
            at = slot_ref[q, u]
            picked[pl.ds(base + u, 1), :] = table[pl.ds(at, 1), :]
        return carry

    lax.fori_loop(0, 128, step, 0)
    sign = lane_sign()
    wt = w_ref[...].T
    for row in range(32):
        acc = jnp.zeros((64, 128), F32)
        for k in range(4):
            q = row * 4 + k
            factor = jnp.maximum(wt[:, q : q + 1] * sign, 0.0)
            acc = acc + factor * picked[q * 64 : q * 64 + 64, :]
        acc = acc + pltpu.roll(acc, 64, 1)
        out_ref[row * 64 : row * 64 + 64, :] = acc.astype(BF)
    land = m_ref[...].astype(F32).T
    inject = jnp.concatenate([inj_ref[...], jnp.zeros_like(inj_ref[...])], 0)
    for b in range(4):
        injected = jnp.dot(out_ref[b * 512 : b * 512 + 512, :], inject, preferred_element_type=F32)
        for u in range(8):
            r = b * 8 + u
            value = land[:, r : r + 1] * (o_ref[r].astype(F32) + injected[u * 64 : u * 64 + 64])
            mixed_ref[r] = value.astype(BF)
            for c, i in enumerate((0, 1, 62, 63)):
                cols[c, r : r + 1, :] = value[i : i + 1]
    for r in range(2):
        put_pair(odd, inner_ref, outer_ref, r, mixed_ref[r], mixed_ref[30 + r])
    cols_ref[...] = cols[...].astype(BF)


def scatter_kernel(
    flag_ref, slot_ref, w_ref, g_ref, own_ref, n_ref, s_ref, side_in, side_out, low_ref, band_in, band_out, *scratch
):
    top = flag_ref[0]
    east_odd = flag_ref[2] != 0
    tables, parts = scratch[:8], scratch[8]

    def clear(count):
        def one(i, carry):
            base = pl.multiple_of(i * 96, 96)
            for t in tables:
                t[pl.ds(base, 96), :] = jnp.zeros((96, 128), F32)
            return carry

        lax.fori_loop(0, count // 96, one, 0)

    @pl.when(top == 0)
    def _():
        clear(20 * NEAR)

    @pl.when(top != 0)
    def _():
        clear(32 * BAND)

    sign = lane_sign()
    wt = w_ref[...].T
    for row in range(32):
        g = g_ref[row * 64 : row * 64 + 64, :].astype(F32)
        for k in range(4):
            q = row * 4 + k
            parts[q * 64 : q * 64 + 64, :] = jnp.maximum(wt[:, q : q + 1] * sign, 0.0) * g

    def step(row, carry):
        base = pl.multiple_of(row * 256, 256)
        for u in range(64):
            for k in range(4):
                at = slot_ref[row * 4 + k, u]
                t = tables[k + u % 2 * 4]
                t[pl.ds(at, 1), :] = t[pl.ds(at, 1), :] + parts[pl.ds(base + k * 64 + u, 1), :]
        return carry

    lax.fori_loop(0, 32, step, 0)

    def total(start, size):
        where = pl.ds(start, size)
        pairs = [tables[k][where, :] + tables[k + 4][where, :] for k in range(4)]
        return ((pairs[0] + pairs[1]) + (pairs[2] + pairs[3])).astype(BF)

    @pl.when(top == 0)
    def _():
        for r in range(20):
            rows = total(r * NEAR, 64)
            if r < 16:
                own_ref[r] = rows
            elif r < 18:
                n_ref[r - 16] = rows
            else:
                s_ref[r - 18] = rows
            put_pair(east_odd, side_in, side_out, r, total(r * NEAR + 64, 2), total(r * NEAR + 66, 2))

    @pl.when(top != 0)
    def _():
        for r in range(2):
            n_ref[r] = jnp.zeros((64, 128), BF)
            s_ref[r] = jnp.zeros((64, 128), BF)
        side_in[...] = jnp.zeros_like(side_in)
        side_out[...] = jnp.zeros_like(side_out)
        for r in range(32):
            base = r * BAND
            if r < 16:
                low_ref[r] = total(base, 64)
            else:
                own_ref[r - 16] = total(base, 64)
            put_pair(east_odd, band_in, band_out, r, total(base + 64, 64), total(base + 128, 64))


def entry_slots(source_row, source_col, weight, is_top, row_count, col_count):
    nx = col_count * lax.axis_size("lon")
    row = source_row - lax.axis_index("lat") * row_count
    col = jnp.remainder(source_col - lax.axis_index("lon") * col_count + nx // 2, nx) - nx // 2
    half = row_count // 2
    inside = (row >= 0) & (row < row_count)
    wrapped = row & (row_count - 1)
    packed = wrapped & (half - 1)
    upper = wrapped >= half
    near_row = jnp.where(inside, packed, jnp.where(row < 0, packed + 4, packed + half))
    near_col = jnp.where((col >= 0) & (col < col_count), col, jnp.where(col < 0, col + col_count + 2, col + 2))
    band_row = jnp.where(row >= 0, packed + half, packed)
    band_col = jnp.where((col >= 0) & (col < col_count), col, jnp.where(col < 0, col + 2 * col_count, col + col_count))
    slot = jnp.where(is_top, band_row * BAND + band_col, near_row * NEAR + near_col)
    signed = jnp.where(upper, -weight, weight)
    order = lambda x: jnp.transpose(x, (0, 2, 1)).reshape(-1, col_count)
    return order(slot), order(signed)


def body(
    atmos_state,
    atmos_weights,
    flux_project,
    source_row,
    source_col,
    intersection_weight,
    ocean_state,
    flux_inject,
    ocean_mask,
    ocean_weights,
    out_cotangent,
):
    row_count, col_count, chans = atmos_state.shape
    flux_chans = flux_project.shape[1]
    cells = row_count * col_count
    half = cells // 2
    lats = lax.axis_size("lat")
    is_top = lax.axis_index("lat") == lats - 1
    core = lax.rem(lax.axis_index("lat"), 2)
    flags = jnp.stack([is_top.astype(jnp.int32), core, lax.rem(lax.axis_index("lon"), 2)])
    struct = lambda *shape: (shape, BF)
    block = lambda shape, at: pl.BlockSpec(shape, lambda i: (at[0], at[1], 0))
    row = (1, 64, 256)
    inner, outer = call(
        rows_kernel,
        "rows",
        (struct(2, 64, 256), struct(2, 64, 256)),
        (flags, atmos_state, atmos_state, out_cotangent, out_cotangent, ocean_mask),
        specs=[SMEM, block(row, (0, 0)), block(row, (31, 0)), block(row, (0, 0)), block(row, (31, 0)), VMEM],
        grid=(1,),
    )
    inner, outer = lat_pairs(inner, outer, True)
    slab = (32, 16, 256)
    inner, outer, south, north = call(
        edges_kernel,
        "edges",
        (struct(2, 34, 256), struct(2, 34, 256), struct(2, 64, 256), struct(2, 64, 256)),
        (flags, atmos_state, atmos_state, out_cotangent, out_cotangent, ocean_mask, inner, outer),
        [pltpu.VMEM((4, 34, 256), F32)],
        specs=[SMEM, block(slab, (0, 0)), block(slab, (0, 3)), block(slab, (0, 0)), block(slab, (0, 3))] + [VMEM] * 3,
        grid=(1,),
    )
    side_in, side_out = lon_pairs(inner, outer)
    project = flux_project.T
    atmos_w = atmos_weights.reshape(3, 3 * chans, chans)
    ocean_w = ocean_weights.reshape(3, 3 * chans, chans)
    act, slope, own, inner, outer, first, last = call(
        atmos_kernel,
        "atmos",
        (struct(cells, chans), struct(cells, chans), struct(16, 64, 128), struct(2, 64, 128), struct(2, 64, 128),
         struct(16, 2, 128), struct(16, 2, 128)),
        (flags, atmos_state, south, north, side_in, side_out, atmos_w, project),
        [pltpu.VMEM((34 * 64, 768), BF)],
        scalars=1,
    )
    low_tile = lax.ppermute(own, "lat", [(lats - 2, lats - 1)])
    inner, outer = lat_pairs(inner, outer, False)
    two, inner, outer = lax.optimization_barrier((jnp.concatenate([low_tile, own], 0), inner, outer))
    band_in, band_out = lon_pairs(two, two, lats - 1)
    flux_south, flux_north, inner, outer = call(
        flux_edges_kernel,
        "flux_edges",
        (struct(2, 64, 128), struct(2, 64, 128), struct(20, 2, 128), struct(20, 2, 128)),
        (flags, first, last, inner, outer),
        scalars=1,
    )
    flux_in, flux_out = lon_pairs(inner, outer, 0, lats - 1)
    late = lax.optimization_barrier((own, source_row, source_col, intersection_weight, ocean_weights))
    slots, signed = entry_slots(*late[1:4], is_top, row_count, col_count)
    back_w = jnp.transpose(late[4], (0, 2, 1)).reshape(3, 3 * chans, chans)
    remapped, mixed, cols, inner, outer = call(
        gather_kernel,
        "gather_mix",
        (struct(cells, 128), struct(32, 64, 256), struct(4, 32, 256), struct(2, 64, 256), struct(2, 64, 256)),
        (flags, slots, signed, flux_north, flux_south, flux_in, flux_out, low_tile, own, band_in, band_out,
         ocean_state, ocean_mask, flux_inject),
        [pltpu.VMEM((32 * BAND, 128), F32), pltpu.VMEM((8192, 128), F32), pltpu.VMEM((4, 32, 256), F32)],
        scalars=2,
    )
    inner, outer = lat_pairs(inner, outer, True)
    inner, outer, first, last, mixed_south, mixed_north = call(
        mixed_edges_kernel,
        "mixed_edges",
        (struct(2, 36, 256), struct(2, 36, 256), struct(36, 256), struct(36, 256), struct(2, 64, 256), struct(2, 64, 256)),
        (flags, cols, inner, outer),
        [pltpu.VMEM((4, 36, 256), F32)],
        scalars=1,
    )
    mixed_in, mixed_out = lon_pairs(inner, outer)
    halves = ((GRAD_ROWS, 128), F32), ((GRAD_ROWS, 128), BF)
    ocean_out, remap_grad, deltas, back = call(
        ocean_kernel,
        "ocean",
        (struct(32, 64, 256), struct(cells, 128), struct(cells, 256), struct(cells, 256)),
        (
            flags, mixed, mixed_south, mixed_north, first, last, mixed_in, mixed_out,
            out_cotangent, south, north, side_in, side_out, ocean_mask, ocean_w, back_w, flux_inject,
        ),
        [
            pltpu.VMEM((36 * 64, 768), BF),
            pltpu.VMEM((2, 48, 768), F32),
            pltpu.VMEM((64, 768), BF),
            pltpu.VMEM((64, 768), BF),
            pltpu.VMEM((34 * 64, 768), BF),
            pltpu.VMEM((2, 40, 256), F32),
        ],
        scalars=1,
    )
    own, to_north, to_south, inner, outer, low_tile, band_in, band_out = call(
        scatter_kernel,
        "scatter_rows",
        (struct(16, 64, 128), struct(2, 64, 128), struct(2, 64, 128), struct(20, 2, 128), struct(20, 2, 128),
         struct(16, 64, 128), struct(32, 64, 128), struct(32, 64, 128)),
        (flags, slots, signed, remap_grad),
        [pltpu.VMEM((32 * BAND, 128), F32)] * 8 + [pltpu.VMEM((8192, 128), F32)],
        scalars=2,
    )
    deltas, back, inner, outer, band_in, band_out = lax.optimization_barrier((deltas, back, inner, outer, band_in, band_out))
    ocean_keep, ocean_send = call(
        ocean_grads_kernel,
        "ocean_grads",
        halves,
        (flags, mixed, mixed_south, mixed_north, mixed_in, mixed_out, deltas, back, remapped),
        [pltpu.VMEM((34 * 64, 768), BF)],
        scalars=1,
    )
    band_in, band_out = lon_pairs(band_in, band_out, lats - 1)
    credit_in, credit_out = lon_pairs(inner, outer, 0, lats - 1)
    credit_in, credit_out, ocean_keep, ocean_send = lax.optimization_barrier(
        (credit_in, credit_out, ocean_keep, ocean_send)
    )
    inner, outer = call(
        credit_rows_kernel,
        "credit_rows",
        (struct(2, 64, 128),) * 2,
        (flags, to_north, to_south, credit_in, credit_out),
        [pltpu.VMEM((2, 64, 128), F32)] * 2,
        scalars=1,
    )
    rows_in, rows_out = lat_pairs(inner, outer, False)
    band_in, band_out, _ = lax.optimization_barrier((band_in, band_out, inner))
    low_tile = low_tile.astype(F32) + band_in[:16].astype(F32) + band_out[:16].astype(F32)
    from_band = lax.ppermute(low_tile.astype(BF), "lat", [(lats - 1, lats - 2)])
    atmos_keep, atmos_send = call(
        atmos_back_kernel,
        "atmos_back",
        halves,
        (flags, atmos_state, south, north, side_in, side_out, act, slope, own, credit_in, credit_out, rows_in, rows_out,
         band_in, band_out, from_band, project),
        [pltpu.VMEM((34 * 64, 768), BF), pltpu.VMEM((cells, 256), BF), pltpu.VMEM((64, 128), F32), pltpu.VMEM((half, 128), BF)],
        scalars=1,
    )
    ocean = ocean_keep + exchange(ocean_send, 1).astype(F32)
    ocean, atmos = lax.optimization_barrier((ocean, atmos_keep + exchange(atmos_send, 1).astype(F32)))
    cut = 1600
    rest = GRAD_ROWS - cut
    sums = reduce_streams(
        [ocean[:cut], jnp.concatenate([ocean[cut:], atmos[:rest]]), atmos[rest:]], ((0, 1, 2), (1, 2, 0), (2, 0, 1))
    )
    ocean = jnp.concatenate([sums[0], sums[1][:rest]])
    atmos = jnp.concatenate([sums[1][rest:], sums[2]])

    def joined(mine):
        other = exchange(mine, 1)
        pair = jnp.concatenate([jnp.where(core == 0, mine, other), jnp.where(core == 0, other, mine)], 1).astype(F32)
        return pair[: 9 * chans].reshape(9, chans, chans), pair[9 * chans : 9 * chans + flux_chans]

    grad_ocean, grad_inject = joined(ocean)
    grad_atmos, grad_project = joined(atmos)
    return (ocean_out, grad_atmos, grad_ocean, grad_project.T, grad_inject)


def solution(mesh):
    return jax.shard_map(
        body,
        mesh=mesh,
        in_specs=(
            P("lat", "lon", None),
            P(),
            P(),
            P("lat", "lon", None),
            P("lat", "lon", None),
            P("lat", "lon", None),
            P("lat", "lon", None),
            P(),
            P("lat", "lon"),
            P(),
            P("lat", "lon", None),
        ),
        out_specs=(P("lat", "lon", None), P(), P(), P(), P()),
        check_vma=False,
    )
```

```python
import jax
import jax.numpy as jnp
from jax import lax
from jax.experimental import pallas as pl
from jax.experimental.pallas import tpu as pltpu
from jax.sharding import PartitionSpec as P

BF = jnp.bfloat16
F32 = jnp.float32
MIB = 1 << 20
BIG = 1 << 19
LIMITS = {"atmos": 20, "gather_mix": 20, "ocean": 28, "scatter_rows": 36, "ocean_grads": 18, "atmos_back": 18}
AXES = ("lon", "lat")
NEAR = 72
BAND = 192


def lat_pairs(inner, outer, fold):
    lons, lats = lax.axis_size("lon"), lax.axis_size("lat")
    at = lambda i, j: i * lats + j
    inside = [(at(i, j), at(i, j ^ 1)) for i in range(lons) for j in range(lats)]
    across = [(at(i, j), at(i, j + 1 if j % 2 else j - 1)) for i in range(lons) for j in range(1, lats - 1)]
    if fold:
        across += [(at(i, lats - 1), at(lons - 1 - i, lats - 1)) for i in range(lons)]
    return lax.ppermute(inner, AXES, inside), lax.ppermute(outer, AXES, across)


def lon_pairs(inner, outer, first=0, last=None):
    lons, lats = lax.axis_size("lon"), lax.axis_size("lat")
    here = range(first, lats if last is None else last)
    inside = [(i * lats + j, (i ^ 1) * lats + j) for i in range(lons) for j in here]
    across = [(i * lats + j, ((i + 1 if i % 2 else i - 1) % lons) * lats + j) for i in range(lons) for j in here]
    return lax.ppermute(inner, AXES, inside), lax.ppermute(outer, AXES, across)


def sigmoid(value):
    return 1.0 / (1.0 + jnp.exp(-value))


def silu_slope(value, sigma):
    return sigma * (1.0 + value * (1.0 - sigma))


VMEM = pl.BlockSpec(memory_space=pltpu.VMEM)
SMEM = pl.BlockSpec(memory_space=pltpu.SMEM)
GRAD_ROWS = 2400


def call(kernel, name, outs, ins, scratch=(), scalars=0, specs=None, grid=None):
    if specs is None:
        specs = [SMEM] * scalars + [VMEM] * (len(ins) - scalars)
    ins = [pltpu.with_memory_space_constraint(x, pltpu.HBM) if x.size >= BIG else x for x in ins]
    extra = {} if grid is None else {"grid": grid}
    return pl.pallas_call(
        kernel,
        name=name,
        out_shape=tuple(pltpu.HBM(*out[:2]) if len(out) > 2 else jax.ShapeDtypeStruct(*out) for out in outs),
        in_specs=specs,
        out_specs=(VMEM,) * len(outs),
        scratch_shapes=list(scratch),
        compiler_params=pltpu.CompilerParams(vmem_limit_bytes=LIMITS.get(name, 8) * MIB),
        **extra,
    )(*ins)


def turned_row(row):
    a = lax.broadcasted_iota(jnp.int32, (64, 64), 0)
    b = lax.broadcasted_iota(jnp.int32, (64, 64), 1)
    flip = jnp.where(a + b == 63, jnp.float32(1.0), jnp.float32(0.0)).astype(BF)
    return jnp.dot(flip, row, preferred_element_type=F32)


def build_windows(dst, rows, row_of, west_of, east_of, turned=False):
    first, last = (512, 0) if turned else (0, 512)
    at = lax.broadcasted_iota(jnp.int32, (64, 256), 0)
    for r in range(rows):
        value = row_of(r)
        wide = value.astype(F32)
        left = jnp.where(at == 0, west_of(r).astype(F32), pltpu.roll(wide, 1, 0))
        right = jnp.where(at == 63, east_of(r).astype(F32), pltpu.roll(wide, 63, 0))
        here = slice(r * 64, r * 64 + 64)
        dst[here, first : first + 256] = left.astype(BF)
        dst[here, 256:512] = value
        dst[here, last : last + 256] = right.astype(BF)


def conv_rows(windows, w, start, count, turned=False):
    acc = jnp.zeros((count, 256), F32)
    for r in range(3):
        taps = w[2 - r if turned else r]
        acc += jnp.dot(windows[start + r * 64 : start + r * 64 + count, :], taps, preferred_element_type=F32)
    return acc


def dot_back(a, b):
    return lax.dot_general(a, b, (((1,), (1,)), ((), ())), preferred_element_type=F32)


def turned_lanes(x):
    return jnp.concatenate([x[:, 512:768], x[:, 256:512], x[:, 0:256]], 1)


def put_half(core, keep_ref, send_ref, here, value):
    low, high = value[:, 0:128], value[:, 128:256]
    keep_ref[here, :] = jnp.where(core == 0, low, high)
    send_ref[here, :] = jnp.where(core == 0, high, low).astype(BF)


def dot_rows(a, b):
    return lax.dot_general(a, b, (((0,), (0,)), ((), ())), preferred_element_type=F32)


def put_pair(odd, inner_ref, outer_ref, r, low, high):
    inner_ref[r] = jnp.where(odd, low, high)
    outer_ref[r] = jnp.where(odd, high, low)


def rows_kernel(flag_ref, a0_ref, a1_ref, c0_ref, c1_ref, m_ref, inner_ref, outer_ref):
    odd = flag_ref[1] != 0
    land = m_ref[...].astype(F32).T
    put_pair(odd, inner_ref, outer_ref, 0, a0_ref[0], a1_ref[0])
    low = (c0_ref[0].astype(F32) * land[:, 0:1]).astype(BF)
    high = (c1_ref[0].astype(F32) * land[:, 31:32]).astype(BF)
    put_pair(odd, inner_ref, outer_ref, 1, low, high)


def edges_kernel(
    flag_ref, a0_ref, a1_ref, c0_ref, c1_ref, m_ref, inner_ref, outer_ref, inner_out, outer_out, s_ref, n_ref, cols
):
    top, odd = flag_ref[0] != 0, flag_ref[1] != 0
    land = m_ref[...].astype(F32).T
    for r in range(2):
        s_ref[r] = jnp.where(odd, inner_ref[r], outer_ref[r])
    north = jnp.where(odd, outer_ref[0], inner_ref[0]).astype(F32)
    north = jnp.where(top, jnp.zeros_like(north), north)
    cn = jnp.where(odd, outer_ref[1], inner_ref[1])
    cn = jnp.where(top, turned_row(cn), cn.astype(F32))
    n_ref[0], n_ref[1] = north.astype(BF), cn.astype(BF)
    for r in range(32):
        here = slice(r + 1, r + 2)
        cols[0, here, :] = a0_ref[r, 0:1].astype(F32)
        cols[1, here, :] = c0_ref[r, 0:1].astype(F32) * land[0:1, r : r + 1]
        cols[2, here, :] = a1_ref[r, 15:16].astype(F32)
        cols[3, here, :] = c1_ref[r, 15:16].astype(F32) * land[63:64, r : r + 1]
    for k, (row, i) in enumerate(((s_ref[0], 0), (s_ref[1], 0), (s_ref[0], 63), (s_ref[1], 63))):
        cols[k, 0:1, :] = row[i : i + 1].astype(F32)
    for k, (row, i) in enumerate(((north, 0), (cn, 0), (north, 63), (cn, 63))):
        cols[k, 33:34, :] = row[i : i + 1]
    put_pair(flag_ref[2] != 0, inner_out, outer_out, slice(0, 2), cols[0:2].astype(BF), cols[2:4].astype(BF))


def mixed_edges_kernel(
    flag_ref, cols_in, inner_ref, outer_ref, inner_out, outer_out, first_ref, last_ref, south_ref, north_ref, cols
):
    top, odd = flag_ref[0] != 0, flag_ref[1] != 0
    for r in range(2):
        south_ref[r] = jnp.where(odd, inner_ref[r], outer_ref[r])
        s = south_ref[r].astype(F32)
        n = jnp.where(odd, outer_ref[r], inner_ref[r]).astype(F32)
        n = jnp.where(top, turned_row(outer_ref[1 - r]), n)
        north_ref[r] = n.astype(BF)
        for k, i in enumerate((0, 1, 62, 63)):
            cols[k, r : r + 1, :] = s[i : i + 1]
            cols[k, 34 + r : 35 + r, :] = n[i : i + 1]
    for k in range(4):
        cols[k, 2:34, :] = cols_in[k].astype(F32)
    first_ref[...] = cols[0].astype(BF)
    last_ref[...] = cols[3].astype(BF)
    put_pair(flag_ref[2] != 0, inner_out, outer_out, slice(0, 2), cols[0:2].astype(BF), cols[2:4].astype(BF))


def flux_edges_kernel(flag_ref, first_ref, last_ref, inner_ref, outer_ref, south_ref, north_ref, inner_out, outer_out):
    odd, east_odd = flag_ref[1] != 0, flag_ref[2] != 0
    for r in range(20):
        if r < 16:
            first, last = first_ref[r], last_ref[r]
        else:
            a, b = (inner_ref, outer_ref) if r >= 18 else (outer_ref, inner_ref)
            row = jnp.where(odd, a[r % 2], b[r % 2])
            (north_ref if r < 18 else south_ref)[r % 2] = row
            first, last = row[0:2], row[62:64]
        put_pair(east_odd, inner_out, outer_out, r, first, last)


def atmos_windows(flag_ref, windows, x_ref, s_ref, n_ref, in_ref, out_ref):
    odd = flag_ref[2] != 0
    west = jnp.where(odd, in_ref[0].astype(F32), out_ref[0].astype(F32))
    east = jnp.where(odd, out_ref[0].astype(F32), in_ref[0].astype(F32))
    build_windows(
        windows,
        34,
        lambda r: s_ref[0] if r == 0 else (n_ref[0] if r == 33 else x_ref[r - 1]),
        lambda r: west[r : r + 1, :],
        lambda r: east[r : r + 1, :],
    )


def packed_maps(p_ref):
    p = p_ref[...]
    zeros = jnp.zeros_like(p)
    return jnp.concatenate([p, zeros], 0), jnp.concatenate([zeros, p], 0)


def atmos_kernel(
    flag_ref, x_ref, s_ref, n_ref, in_ref, out_ref, w_ref, p_ref,
    act_ref, slope_ref, own_ref, inner_out, outer_out, first_ref, last_ref, windows,
):
    atmos_windows(flag_ref, windows, x_ref, s_ref, n_ref, in_ref, out_ref)
    maps = packed_maps(p_ref)
    for b in range(2):
        packed = jnp.zeros((512, 128), F32)
        for h in range(2):
            start = h * 1024 + b * 512
            pre = conv_rows(windows, w_ref, start, 512)
            sigma = sigmoid(pre)
            act = (pre * sigma).astype(BF)
            act_ref[start : start + 512, :] = act
            slope_ref[start : start + 512, :] = silu_slope(pre, sigma).astype(BF)
            packed += dot_back(act, maps[h])
        for u in range(8):
            r = b * 8 + u
            row = packed[u * 64 : u * 64 + 64].astype(BF)
            own_ref[r] = row
            first_ref[r] = row[0:2]
            last_ref[r] = row[62:64]
    for r in range(2):
        put_pair(flag_ref[1] != 0, inner_out, outer_out, r, own_ref[r], own_ref[14 + r])


def ocean_kernel(
    flag_ref, x_ref, s_ref, n_ref, first_ref, last_ref, in_ref, beyond_ref, c_ref, cs_ref, cn_ref, ci_ref, co_ref, m_ref,
    w_ref, wt_ref, inj_ref, out_ref, remap_ref, deltas, back,
    windows, sides, north, turned_north, dwin, dsides,
):
    top, odd = flag_ref[0] != 0, flag_ref[2] != 0
    west = [jnp.where(odd, in_ref[k].astype(F32), beyond_ref[k].astype(F32)) for k in range(2)]
    east = [jnp.where(odd, beyond_ref[k].astype(F32), in_ref[k].astype(F32)) for k in range(2)]
    cot_west = jnp.where(odd, ci_ref[1].astype(F32), co_ref[1].astype(F32))
    cot_east = jnp.where(odd, co_ref[1].astype(F32), ci_ref[1].astype(F32))
    land = m_ref[...].astype(F32).T
    build_windows(
        windows,
        36,
        lambda r: s_ref[r] if r < 2 else (n_ref[r - 34] if r >= 34 else x_ref[r - 2]),
        lambda r: west[1][r : r + 1, :],
        lambda r: east[0][r : r + 1, :],
    )
    sides[...] = jnp.zeros_like(sides)
    for side, columns in ((0, (west[0], west[1], first_ref[...])), (1, (last_ref[...], east[0], east[1]))):
        for q in range(3):
            sides[side, 0:36, q * 256 : q * 256 + 256] = columns[q].astype(F32)

    def side_rows(start, count):
        return jnp.concatenate([sides[0, start : start + count, :], sides[1, start : start + count, :]], 0).astype(BF)

    pre = jnp.zeros((80, 256), F32)
    lines = [jnp.concatenate([windows[(33 + r) * 64 : (34 + r) * 64, :], side_rows(33 + r, 8)], 0) for r in range(3)]
    for r in range(3):
        pre += jnp.dot(jnp.where(top, turned_lanes(lines[2 - r]), lines[r]), w_ref[r], preferred_element_type=F32)
    slope = silu_slope(pre, sigmoid(pre))
    d_north = (cn_ref[1].astype(F32) * slope[0:64]).astype(BF)
    side_pre = jnp.zeros((80, 256), F32)
    for r in range(3):
        side_pre += jnp.dot(side_rows(r, 40), w_ref[r], preferred_element_type=F32)
    side_slope = silu_slope(side_pre, sigmoid(side_pre))
    at = lax.broadcasted_iota(jnp.int32, (40, 256), 0)
    for side, cot in ((0, cot_west), (1, cot_east)):
        corner = slope[64 + side * 8 : 65 + side * 8]
        here = jnp.where(at == 33, corner, side_slope[side * 40 : side * 40 + 40])
        dsides[side] = jnp.zeros((40, 256), F32)
        dsides[side, 0:34, :] = cot * here[0:34]
    pre = conv_rows(windows, w_ref, 0, 64)
    d_south = (cs_ref[1].astype(F32) * silu_slope(pre, sigmoid(pre))).astype(BF)
    for b in range(4):
        pre = conv_rows(windows, w_ref, 64 + b * 512, 512)
        sigma = sigmoid(pre)
        act = pre * sigma
        slope = silu_slope(pre, sigma)
        for u in range(8):
            r = b * 8 + u
            here = slice(u * 64, u * 64 + 64)
            wet = land[:, r : r + 1]
            out_ref[r] = (wet * act[here]).astype(BF)
            deltas[r * 64 : r * 64 + 64, :] = (c_ref[r].astype(F32) * wet * slope[here]).astype(BF)
    dry = jnp.zeros((64, 256), BF)
    build_windows(
        dwin,
        34,
        lambda r: d_south if r == 0 else (dry if r == 33 else deltas[r * 64 - 64 : r * 64, :]),
        lambda r: dsides[0, r : r + 1, :] if r < 33 else dry[0:1],
        lambda r: dsides[1, r : r + 1, :] if r < 33 else dry[0:1],
        turned=True,
    )
    for dst, turned in ((north, False), (turned_north, True)):
        build_windows(
            dst, 1, lambda r: d_north, lambda r: dsides[0, 33:34, :], lambda r: dsides[1, 33:34, :], turned=turned
        )
    beyond = jnp.dot(
        jnp.where(top, north[...], turned_north[...]), wt_ref[jnp.where(top, 2, 0)], preferred_element_type=F32
    )
    inject = jnp.concatenate([inj_ref[...], inj_ref[...]], 0)
    for b in range(4):
        total = conv_rows(dwin, wt_ref, b * 512, 512, turned=True)
        for u in range(8):
            r = b * 8 + u
            value = total[u * 64 : u * 64 + 64]
            if r == 31:
                value = value + beyond
            back[r * 64 : r * 64 + 64, :] = (land[:, r : r + 1] * value).astype(BF)
        remap_ref[b * 512 : b * 512 + 512, :] = dot_back(back[b * 512 : b * 512 + 512, :], inject).astype(BF)


def ocean_grads_kernel(
    flag_ref, x_ref, s_ref, n_ref, in_ref, beyond_ref, deltas, back, rem_ref, keep_ref, send_ref, windows
):
    core, odd = flag_ref[1], flag_ref[2] != 0
    west = jnp.where(odd, in_ref[1].astype(F32), beyond_ref[1].astype(F32))
    east = jnp.where(odd, beyond_ref[0].astype(F32), in_ref[0].astype(F32))
    build_windows(
        windows,
        34,
        lambda r: s_ref[1] if r == 0 else (n_ref[0] if r == 33 else x_ref[r - 1]),
        lambda r: west[r + 1 : r + 2, :],
        lambda r: east[r + 1 : r + 2, :],
    )
    for r in range(3):
        value = dot_rows(windows[r * 64 : r * 64 + 2048, :], deltas[...])
        put_half(core, keep_ref, send_ref, slice(r * 768, r * 768 + 768), value)
    tail = jnp.concatenate([dot_rows(rem_ref[...], back[...])[0:64], jnp.zeros((32, 256), F32)], 0)
    put_half(core, keep_ref, send_ref, slice(2304, 2400), tail)


def credit_rows_kernel(flag_ref, n_ref, s_ref, in_ref, out_ref, inner_out, outer_out, n_sum, s_sum):
    odd, east_odd = flag_ref[1] != 0, flag_ref[2] != 0
    for r in range(2):
        for src, dst, first in ((n_ref, n_sum, 16), (s_ref, s_sum, 18)):
            inner, outer = in_ref[first + r].astype(F32), out_ref[first + r].astype(F32)
            dst[r] = src[r].astype(F32)
            dst[r, 0:2] = dst[r, 0:2] + jnp.where(east_odd, inner, outer)
            dst[r, 62:64] = dst[r, 62:64] + jnp.where(east_odd, outer, inner)
        put_pair(odd, inner_out, outer_out, r, s_sum[r].astype(BF), n_sum[r].astype(BF))


def atmos_back_kernel(
    flag_ref, x_ref, s_ref, n_ref, in_ref, out_ref, act_ref, slope_ref, own_ref, ci_ref, co_ref, ri_ref, ro_ref, bi_ref, bo_ref,
    low_ref, p_ref, keep_ref, send_ref, windows, deltas, total, credit,
):
    core = flag_ref[1]
    odd, east_odd = core != 0, flag_ref[2] != 0
    atmos_windows(flag_ref, windows, x_ref, s_ref, n_ref, in_ref, out_ref)
    maps = packed_maps(p_ref)
    for r in range(16):
        value = own_ref[r].astype(F32) + bi_ref[16 + r].astype(F32) + bo_ref[16 + r].astype(F32) + low_ref[r].astype(F32)
        if r < 2:
            value += jnp.where(odd, ri_ref[r].astype(F32), ro_ref[r].astype(F32))
        if r >= 14:
            value += jnp.where(odd, ro_ref[r - 14].astype(F32), ri_ref[r - 14].astype(F32))
        total[...] = value
        inner, outer = ci_ref[r].astype(F32), co_ref[r].astype(F32)
        total[0:2, :] += jnp.where(east_odd, inner, outer)
        total[62:64, :] += jnp.where(east_odd, outer, inner)
        credit[r * 64 : r * 64 + 64, :] = total[...].astype(BF)
    for h in range(2):
        here = slice(h * 1024, h * 1024 + 1024)
        back = jnp.dot(credit[...], maps[h], preferred_element_type=F32)
        deltas[here, :] = (back * slope_ref[here, :].astype(F32)).astype(BF)
    for r in range(3):
        value = dot_rows(windows[r * 64 : r * 64 + 2048, :], deltas[...])
        put_half(core, keep_ref, send_ref, slice(r * 768, r * 768 + 768), value)
    lower = dot_rows(credit[...], act_ref[0:1024, :])
    upper = dot_rows(credit[...], act_ref[1024:2048, :])
    tail = jnp.concatenate([lower[0:64] + upper[64:128], jnp.zeros((32, 256), F32)], 0)
    put_half(core, keep_ref, send_ref, slice(2304, 2400), tail)


def exchange(x, mask):
    count = lax.axis_size("lon") * lax.axis_size("lat")
    return lax.ppermute(x, AXES, [(i, i ^ mask) for i in range(count)])


def reduce_streams(streams, orders):
    rank = lax.axis_index("lon") * lax.axis_size("lat") + lax.axis_index("lat")
    bit = lambda n: (rank >> n) & 1
    near = [(2, bit(1) ^ bit(2)), (8, bit(3) ^ bit(4)), (32, bit(5) ^ bit(6))]
    far = (6, 24, 96)
    count = range(len(streams))
    for level in range(3):
        steps = [near[orders[i][level]] for i in count]
        half = streams[0].shape[0] // 2
        keep = [lax.dynamic_slice_in_dim(streams[i], steps[i][1] * half, half) for i in count]
        send = [lax.dynamic_slice_in_dim(streams[i], (1 - steps[i][1]) * half, half).astype(BF) for i in count]
        streams = [keep[i] + exchange(send[i], steps[i][0]).astype(F32) for i in count]
    streams = [s.astype(BF) for s in streams]
    for level in range(3):
        got = [exchange(streams[i], far[orders[i][level]]) for i in count]
        streams = [(streams[i].astype(F32) + got[i].astype(F32)).astype(BF) for i in count]
    for level in (2, 1, 0):
        steps = [near[orders[i][level]] for i in count]
        got = [exchange(streams[i], steps[i][0]) for i in count]
        streams = [
            jnp.where(
                steps[i][1] == 0,
                jnp.concatenate([streams[i], got[i]]),
                jnp.concatenate([got[i], streams[i]]),
            )
            for i in count
        ]
    return streams


def lane_sign():
    lane = lax.broadcasted_iota(jnp.int32, (64, 128), 1)
    return jnp.where(lane < 64, jnp.float32(1.0), jnp.float32(-1.0))


def gather_kernel(
    flag_ref, slot_ref, w_ref, fn_ref, fs_ref, fi_ref, fo_ref, low_ref, own_ref, bi_ref, bo_ref, o_ref, m_ref, inj_ref,
    out_ref, mixed_ref, cols_ref, inner_ref, outer_ref, table, picked, cols,
):
    top = flag_ref[0]
    odd, east_odd = flag_ref[1] != 0, flag_ref[2] != 0

    @pl.when(top == 0)
    def _():
        for r in range(20):
            rows = own_ref[r] if r < 16 else (fn_ref[r - 16] if r < 18 else fs_ref[r - 18])
            table[r * NEAR : r * NEAR + 64, :] = rows.astype(F32)
            table[r * NEAR + 64 : r * NEAR + 66, :] = jnp.where(east_odd, fi_ref[r].astype(F32), fo_ref[r].astype(F32))
            table[r * NEAR + 66 : r * NEAR + 68, :] = jnp.where(east_odd, fo_ref[r].astype(F32), fi_ref[r].astype(F32))

    @pl.when(top != 0)
    def _():
        for r in range(32):
            base = r * BAND
            table[base : base + 64, :] = (low_ref[r] if r < 16 else own_ref[r - 16]).astype(F32)
            inner, outer = bi_ref[r].astype(F32), bo_ref[r].astype(F32)
            table[base + 64 : base + 128, :] = jnp.where(east_odd, inner, outer)
            table[base + 128 : base + 192, :] = jnp.where(east_odd, outer, inner)

    def step(q, carry):
        base = pl.multiple_of(q * 64, 64)
        for u in range(64):
            at = slot_ref[q, u]
            picked[pl.ds(base + u, 1), :] = table[pl.ds(at, 1), :]
        return carry

    lax.fori_loop(0, 128, step, 0)
    sign = lane_sign()
    wt = w_ref[...].T
    for row in range(32):
        acc = jnp.zeros((64, 128), F32)
        for k in range(4):
            q = row * 4 + k
            factor = jnp.maximum(wt[:, q : q + 1] * sign, 0.0)
            acc = acc + factor * picked[q * 64 : q * 64 + 64, :]
        acc = acc + pltpu.roll(acc, 64, 1)
        out_ref[row * 64 : row * 64 + 64, :] = acc.astype(BF)
    land = m_ref[...].astype(F32).T
    inject = jnp.concatenate([inj_ref[...], jnp.zeros_like(inj_ref[...])], 0)
    for b in range(4):
        injected = jnp.dot(out_ref[b * 512 : b * 512 + 512, :], inject, preferred_element_type=F32)
        for u in range(8):
            r = b * 8 + u
            value = land[:, r : r + 1] * (o_ref[r].astype(F32) + injected[u * 64 : u * 64 + 64])
            mixed_ref[r] = value.astype(BF)
            for c, i in enumerate((0, 1, 62, 63)):
                cols[c, r : r + 1, :] = value[i : i + 1]
    for r in range(2):
        put_pair(odd, inner_ref, outer_ref, r, mixed_ref[r], mixed_ref[30 + r])
    cols_ref[...] = cols[...].astype(BF)


def scatter_kernel(
    flag_ref, slot_ref, w_ref, g_ref, own_ref, n_ref, s_ref, side_in, side_out, low_ref, band_in, band_out, *scratch
):
    top = flag_ref[0]
    east_odd = flag_ref[2] != 0
    tables, parts = scratch[:8], scratch[8]

    def clear(count):
        def one(i, carry):
            base = pl.multiple_of(i * 96, 96)
            for t in tables:
                t[pl.ds(base, 96), :] = jnp.zeros((96, 128), F32)
            return carry

        lax.fori_loop(0, count // 96, one, 0)

    @pl.when(top == 0)
    def _():
        clear(20 * NEAR)

    @pl.when(top != 0)
    def _():
        clear(32 * BAND)

    sign = lane_sign()
    wt = w_ref[...].T
    for row in range(32):
        g = g_ref[row * 64 : row * 64 + 64, :].astype(F32)
        for k in range(4):
            q = row * 4 + k
            parts[q * 64 : q * 64 + 64, :] = jnp.maximum(wt[:, q : q + 1] * sign, 0.0) * g

    def step(row, carry):
        base = pl.multiple_of(row * 256, 256)
        for u in range(64):
            for k in range(4):
                at = slot_ref[row * 4 + k, u]
                t = tables[k + u % 2 * 4]
                t[pl.ds(at, 1), :] = t[pl.ds(at, 1), :] + parts[pl.ds(base + k * 64 + u, 1), :]
        return carry

    lax.fori_loop(0, 32, step, 0)

    def total(start, size):
        where = pl.ds(start, size)
        pairs = [tables[k][where, :] + tables[k + 4][where, :] for k in range(4)]
        return ((pairs[0] + pairs[1]) + (pairs[2] + pairs[3])).astype(BF)

    @pl.when(top == 0)
    def _():
        for r in range(20):
            rows = total(r * NEAR, 64)
            if r < 16:
                own_ref[r] = rows
            elif r < 18:
                n_ref[r - 16] = rows
            else:
                s_ref[r - 18] = rows
            put_pair(east_odd, side_in, side_out, r, total(r * NEAR + 64, 2), total(r * NEAR + 66, 2))

    @pl.when(top != 0)
    def _():
        for r in range(2):
            n_ref[r] = jnp.zeros((64, 128), BF)
            s_ref[r] = jnp.zeros((64, 128), BF)
        side_in[...] = jnp.zeros_like(side_in)
        side_out[...] = jnp.zeros_like(side_out)
        for r in range(32):
            base = r * BAND
            if r < 16:
                low_ref[r] = total(base, 64)
            else:
                own_ref[r - 16] = total(base, 64)
            put_pair(east_odd, band_in, band_out, r, total(base + 64, 64), total(base + 128, 64))


def entry_slots(source_row, source_col, weight, is_top, row_count, col_count):
    nx = col_count * lax.axis_size("lon")
    row = source_row - lax.axis_index("lat") * row_count
    col = jnp.remainder(source_col - lax.axis_index("lon") * col_count + nx // 2, nx) - nx // 2
    half = row_count // 2
    inside = (row >= 0) & (row < row_count)
    wrapped = row & (row_count - 1)
    packed = wrapped & (half - 1)
    upper = wrapped >= half
    near_row = jnp.where(inside, packed, jnp.where(row < 0, packed + 4, packed + half))
    near_col = jnp.where((col >= 0) & (col < col_count), col, jnp.where(col < 0, col + col_count + 2, col + 2))
    band_row = jnp.where(row >= 0, packed + half, packed)
    band_col = jnp.where((col >= 0) & (col < col_count), col, jnp.where(col < 0, col + 2 * col_count, col + col_count))
    slot = jnp.where(is_top, band_row * BAND + band_col, near_row * NEAR + near_col)
    signed = jnp.where(upper, -weight, weight)
    order = lambda x: jnp.transpose(x, (0, 2, 1)).reshape(-1, col_count)
    return order(slot), order(signed)


def body(
    atmos_state,
    atmos_weights,
    flux_project,
    source_row,
    source_col,
    intersection_weight,
    ocean_state,
    flux_inject,
    ocean_mask,
    ocean_weights,
    out_cotangent,
):
    row_count, col_count, chans = atmos_state.shape
    flux_chans = flux_project.shape[1]
    cells = row_count * col_count
    half = cells // 2
    lats = lax.axis_size("lat")
    is_top = lax.axis_index("lat") == lats - 1
    core = lax.rem(lax.axis_index("lat"), 2)
    flags = jnp.stack([is_top.astype(jnp.int32), core, lax.rem(lax.axis_index("lon"), 2)])
    struct = lambda *shape: (shape, BF)
    stored = lambda *shape: (shape, BF, True)
    block = lambda shape, at: pl.BlockSpec(shape, lambda i: (at[0], at[1], 0))
    row = (1, 64, 256)
    inner, outer = call(
        rows_kernel,
        "rows",
        (struct(2, 64, 256), struct(2, 64, 256)),
        (flags, atmos_state, atmos_state, out_cotangent, out_cotangent, ocean_mask),
        specs=[SMEM, block(row, (0, 0)), block(row, (31, 0)), block(row, (0, 0)), block(row, (31, 0)), VMEM],
        grid=(1,),
    )
    inner, outer = lat_pairs(inner, outer, True)
    slab = (32, 16, 256)
    inner, outer, south, north = call(
        edges_kernel,
        "edges",
        (struct(2, 34, 256), struct(2, 34, 256), struct(2, 64, 256), struct(2, 64, 256)),
        (flags, atmos_state, atmos_state, out_cotangent, out_cotangent, ocean_mask, inner, outer),
        [pltpu.VMEM((4, 34, 256), F32)],
        specs=[SMEM, block(slab, (0, 0)), block(slab, (0, 3)), block(slab, (0, 0)), block(slab, (0, 3))] + [VMEM] * 3,
        grid=(1,),
    )
    side_in, side_out = lon_pairs(inner, outer)
    project = flux_project.T
    atmos_w = atmos_weights.reshape(3, 3 * chans, chans)
    ocean_w = ocean_weights.reshape(3, 3 * chans, chans)
    act, slope, own, inner, outer, first, last = call(
        atmos_kernel,
        "atmos",
        (stored(cells, chans), stored(cells, chans), struct(16, 64, 128), struct(2, 64, 128), struct(2, 64, 128),
         struct(16, 2, 128), struct(16, 2, 128)),
        (flags, atmos_state, south, north, side_in, side_out, atmos_w, project),
        [pltpu.VMEM((34 * 64, 768), BF)],
        scalars=1,
    )
    low_tile = lax.ppermute(own, "lat", [(lats - 2, lats - 1)])
    inner, outer = lat_pairs(inner, outer, False)
    two, inner, outer = lax.optimization_barrier((jnp.concatenate([low_tile, own], 0), inner, outer))
    band_in, band_out = lon_pairs(two, two, lats - 1)
    flux_south, flux_north, inner, outer = call(
        flux_edges_kernel,
        "flux_edges",
        (struct(2, 64, 128), struct(2, 64, 128), struct(20, 2, 128), struct(20, 2, 128)),
        (flags, first, last, inner, outer),
        scalars=1,
    )
    flux_in, flux_out = lon_pairs(inner, outer, 0, lats - 1)
    late = lax.optimization_barrier((own, source_row, source_col, intersection_weight, ocean_weights))
    slots, signed = entry_slots(*late[1:4], is_top, row_count, col_count)
    back_w = jnp.transpose(late[4], (0, 2, 1)).reshape(3, 3 * chans, chans)
    remapped, mixed, cols, inner, outer = call(
        gather_kernel,
        "gather_mix",
        (struct(cells, 128), stored(32, 64, 256), struct(4, 32, 256), struct(2, 64, 256), struct(2, 64, 256)),
        (flags, slots, signed, flux_north, flux_south, flux_in, flux_out, low_tile, own, band_in, band_out,
         ocean_state, ocean_mask, flux_inject),
        [pltpu.VMEM((32 * BAND, 128), F32), pltpu.VMEM((8192, 128), F32), pltpu.VMEM((4, 32, 256), F32)],
        scalars=2,
    )
    inner, outer = lat_pairs(inner, outer, True)
    inner, outer, first, last, mixed_south, mixed_north = call(
        mixed_edges_kernel,
        "mixed_edges",
        (struct(2, 36, 256), struct(2, 36, 256), struct(36, 256), struct(36, 256), struct(2, 64, 256), struct(2, 64, 256)),
        (flags, cols, inner, outer),
        [pltpu.VMEM((4, 36, 256), F32)],
        scalars=1,
    )
    mixed_in, mixed_out = lon_pairs(inner, outer)
    halves = ((GRAD_ROWS, 128), F32), ((GRAD_ROWS, 128), BF)
    ocean_out, remap_grad, deltas, back = call(
        ocean_kernel,
        "ocean",
        (struct(32, 64, 256), struct(cells, 128), stored(cells, 256), stored(cells, 256)),
        (
            flags, mixed, mixed_south, mixed_north, first, last, mixed_in, mixed_out,
            out_cotangent, south, north, side_in, side_out, ocean_mask, ocean_w, back_w, flux_inject,
        ),
        [
            pltpu.VMEM((36 * 64, 768), BF),
            pltpu.VMEM((2, 48, 768), F32),
            pltpu.VMEM((64, 768), BF),
            pltpu.VMEM((64, 768), BF),
            pltpu.VMEM((34 * 64, 768), BF),
            pltpu.VMEM((2, 40, 256), F32),
        ],
        scalars=1,
    )
    own, to_north, to_south, inner, outer, low_tile, band_in, band_out = call(
        scatter_kernel,
        "scatter_rows",
        (struct(16, 64, 128), struct(2, 64, 128), struct(2, 64, 128), struct(20, 2, 128), struct(20, 2, 128),
         struct(16, 64, 128), struct(32, 64, 128), struct(32, 64, 128)),
        (flags, slots, signed, remap_grad),
        [pltpu.VMEM((32 * BAND, 128), F32)] * 8 + [pltpu.VMEM((8192, 128), F32)],
        scalars=2,
    )
    deltas, back, inner, outer, band_in, band_out = lax.optimization_barrier((deltas, back, inner, outer, band_in, band_out))
    ocean_keep, ocean_send = call(
        ocean_grads_kernel,
        "ocean_grads",
        halves,
        (flags, mixed, mixed_south, mixed_north, mixed_in, mixed_out, deltas, back, remapped),
        [pltpu.VMEM((34 * 64, 768), BF)],
        scalars=1,
    )
    band_in, band_out = lon_pairs(band_in, band_out, lats - 1)
    credit_in, credit_out = lon_pairs(inner, outer, 0, lats - 1)
    credit_in, credit_out, ocean_keep, ocean_send = lax.optimization_barrier(
        (credit_in, credit_out, ocean_keep, ocean_send)
    )
    inner, outer = call(
        credit_rows_kernel,
        "credit_rows",
        (struct(2, 64, 128),) * 2,
        (flags, to_north, to_south, credit_in, credit_out),
        [pltpu.VMEM((2, 64, 128), F32)] * 2,
        scalars=1,
    )
    rows_in, rows_out = lat_pairs(inner, outer, False)
    band_in, band_out, _ = lax.optimization_barrier((band_in, band_out, inner))
    low_tile = low_tile.astype(F32) + band_in[:16].astype(F32) + band_out[:16].astype(F32)
    from_band = lax.ppermute(low_tile.astype(BF), "lat", [(lats - 1, lats - 2)])
    atmos_keep, atmos_send = call(
        atmos_back_kernel,
        "atmos_back",
        halves,
        (flags, atmos_state, south, north, side_in, side_out, act, slope, own, credit_in, credit_out, rows_in, rows_out,
         band_in, band_out, from_band, project),
        [pltpu.VMEM((34 * 64, 768), BF), pltpu.VMEM((cells, 256), BF), pltpu.VMEM((64, 128), F32), pltpu.VMEM((half, 128), BF)],
        scalars=1,
    )
    ocean = ocean_keep + exchange(ocean_send, 1).astype(F32)
    ocean, atmos = lax.optimization_barrier((ocean, atmos_keep + exchange(atmos_send, 1).astype(F32)))
    cut = 1600
    rest = GRAD_ROWS - cut
    sums = reduce_streams(
        [ocean[:cut], jnp.concatenate([ocean[cut:], atmos[:rest]]), atmos[rest:]], ((0, 1, 2), (1, 2, 0), (2, 0, 1))
    )
    ocean = jnp.concatenate([sums[0], sums[1][:rest]])
    atmos = jnp.concatenate([sums[1][rest:], sums[2]])

    def joined(mine):
        other = exchange(mine, 1)
        pair = jnp.concatenate([jnp.where(core == 0, mine, other), jnp.where(core == 0, other, mine)], 1).astype(F32)
        return pair[: 9 * chans].reshape(9, chans, chans), pair[9 * chans : 9 * chans + flux_chans]

    grad_ocean, grad_inject = joined(ocean)
    grad_atmos, grad_project = joined(atmos)
    return (ocean_out, grad_atmos, grad_ocean, grad_project.T, grad_inject)


def solution(mesh):
    return jax.shard_map(
        body,
        mesh=mesh,
        in_specs=(
            P("lat", "lon", None),
            P(),
            P(),
            P("lat", "lon", None),
            P("lat", "lon", None),
            P("lat", "lon", None),
            P("lat", "lon", None),
            P(),
            P("lat", "lon"),
            P(),
            P("lat", "lon", None),
        ),
        out_specs=(P("lat", "lon", None), P(), P(), P(), P()),
        check_vma=False,
    )
```

```python
import jax
import jax.numpy as jnp
from jax import lax
from jax.experimental import pallas as pl
from jax.experimental.pallas import tpu as pltpu
from jax.sharding import PartitionSpec as P

BF = jnp.bfloat16
F32 = jnp.float32
MIB = 1 << 20
BIG = 1 << 19
LIMITS = {"atmos": 20, "gather_mix": 20, "ocean": 28, "scatter_rows": 36, "ocean_grads": 18, "atmos_back": 18}
AXES = ("lon", "lat")
NEAR = 72
BAND = 192


def lat_pairs(inner, outer, fold):
    lons, lats = lax.axis_size("lon"), lax.axis_size("lat")
    at = lambda i, j: i * lats + j
    inside = [(at(i, j), at(i, j ^ 1)) for i in range(lons) for j in range(lats)]
    across = [(at(i, j), at(i, j + 1 if j % 2 else j - 1)) for i in range(lons) for j in range(1, lats - 1)]
    if fold:
        across += [(at(i, lats - 1), at(lons - 1 - i, lats - 1)) for i in range(lons)]
    return lax.ppermute(inner, AXES, inside), lax.ppermute(outer, AXES, across)


def lon_pairs(inner, outer, first=0, last=None):
    lons, lats = lax.axis_size("lon"), lax.axis_size("lat")
    here = range(first, lats if last is None else last)
    inside = [(i * lats + j, (i ^ 1) * lats + j) for i in range(lons) for j in here]
    across = [(i * lats + j, ((i + 1 if i % 2 else i - 1) % lons) * lats + j) for i in range(lons) for j in here]
    return lax.ppermute(inner, AXES, inside), lax.ppermute(outer, AXES, across)


def sigmoid(value):
    return 1.0 / (1.0 + jnp.exp(-value))


def silu_slope(value, sigma):
    return sigma * (1.0 + value * (1.0 - sigma))


VMEM = pl.BlockSpec(memory_space=pltpu.VMEM)
SMEM = pl.BlockSpec(memory_space=pltpu.SMEM)
GRAD_ROWS = 2400


def call(kernel, name, outs, ins, scratch=(), scalars=0, specs=None, grid=None):
    if specs is None:
        specs = [SMEM] * scalars + [VMEM] * (len(ins) - scalars)
    ins = [pltpu.with_memory_space_constraint(x, pltpu.HBM) if x.size >= BIG else x for x in ins]
    extra = {} if grid is None else {"grid": grid}
    return pl.pallas_call(
        kernel,
        name=name,
        out_shape=tuple(pltpu.HBM(*out[:2]) if len(out) > 2 else jax.ShapeDtypeStruct(*out) for out in outs),
        in_specs=specs,
        out_specs=(VMEM,) * len(outs),
        scratch_shapes=list(scratch),
        compiler_params=pltpu.CompilerParams(vmem_limit_bytes=LIMITS.get(name, 8) * MIB),
        **extra,
    )(*ins)


def turned_row(row):
    a = lax.broadcasted_iota(jnp.int32, (64, 64), 0)
    b = lax.broadcasted_iota(jnp.int32, (64, 64), 1)
    flip = jnp.where(a + b == 63, jnp.float32(1.0), jnp.float32(0.0)).astype(BF)
    return jnp.dot(flip, row, preferred_element_type=F32)


def build_windows(dst, rows, row_of, west_of, east_of, turned=False):
    first, last = (512, 0) if turned else (0, 512)
    at = lax.broadcasted_iota(jnp.int32, (64, 256), 0)
    for r in range(rows):
        value = row_of(r)
        wide = value.astype(F32)
        left = jnp.where(at == 0, west_of(r).astype(F32), pltpu.roll(wide, 1, 0))
        right = jnp.where(at == 63, east_of(r).astype(F32), pltpu.roll(wide, 63, 0))
        here = slice(r * 64, r * 64 + 64)
        dst[here, first : first + 256] = left.astype(BF)
        dst[here, 256:512] = value
        dst[here, last : last + 256] = right.astype(BF)


def conv_rows(windows, w, start, count, turned=False):
    acc = jnp.zeros((count, 256), F32)
    for r in range(3):
        taps = w[2 - r if turned else r]
        acc += jnp.dot(windows[start + r * 64 : start + r * 64 + count, :], taps, preferred_element_type=F32)
    return acc


def dot_back(a, b):
    return lax.dot_general(a, b, (((1,), (1,)), ((), ())), preferred_element_type=F32)


def turned_lanes(x):
    return jnp.concatenate([x[:, 512:768], x[:, 256:512], x[:, 0:256]], 1)


def put_half(core, keep_ref, send_ref, here, value):
    low, high = value[:, 0:128], value[:, 128:256]
    keep_ref[here, :] = jnp.where(core == 0, low, high)
    send_ref[here, :] = jnp.where(core == 0, high, low).astype(BF)


def dot_rows(a, b):
    return lax.dot_general(a, b, (((0,), (0,)), ((), ())), preferred_element_type=F32)


def put_pair(odd, inner_ref, outer_ref, r, low, high):
    inner_ref[r] = jnp.where(odd, low, high)
    outer_ref[r] = jnp.where(odd, high, low)


def rows_kernel(flag_ref, a0_ref, a1_ref, c0_ref, c1_ref, m_ref, inner_ref, outer_ref):
    odd = flag_ref[1] != 0
    land = m_ref[...].astype(F32).T
    put_pair(odd, inner_ref, outer_ref, 0, a0_ref[0], a1_ref[0])
    low = (c0_ref[0].astype(F32) * land[:, 0:1]).astype(BF)
    high = (c1_ref[0].astype(F32) * land[:, 31:32]).astype(BF)
    put_pair(odd, inner_ref, outer_ref, 1, low, high)


def edges_kernel(
    flag_ref, a0_ref, a1_ref, c0_ref, c1_ref, m_ref, inner_ref, outer_ref, inner_out, outer_out, s_ref, n_ref, cols
):
    top, odd = flag_ref[0] != 0, flag_ref[1] != 0
    land = m_ref[...].astype(F32).T
    for r in range(2):
        s_ref[r] = jnp.where(odd, inner_ref[r], outer_ref[r])
    north = jnp.where(odd, outer_ref[0], inner_ref[0]).astype(F32)
    north = jnp.where(top, jnp.zeros_like(north), north)
    cn = jnp.where(odd, outer_ref[1], inner_ref[1])
    cn = jnp.where(top, turned_row(cn), cn.astype(F32))
    n_ref[0], n_ref[1] = north.astype(BF), cn.astype(BF)
    for r in range(32):
        here = slice(r + 1, r + 2)
        cols[0, here, :] = a0_ref[r, 0:1].astype(F32)
        cols[1, here, :] = c0_ref[r, 0:1].astype(F32) * land[0:1, r : r + 1]
        cols[2, here, :] = a1_ref[r, 15:16].astype(F32)
        cols[3, here, :] = c1_ref[r, 15:16].astype(F32) * land[63:64, r : r + 1]
    for k, (row, i) in enumerate(((s_ref[0], 0), (s_ref[1], 0), (s_ref[0], 63), (s_ref[1], 63))):
        cols[k, 0:1, :] = row[i : i + 1].astype(F32)
    for k, (row, i) in enumerate(((north, 0), (cn, 0), (north, 63), (cn, 63))):
        cols[k, 33:34, :] = row[i : i + 1]
    put_pair(flag_ref[2] != 0, inner_out, outer_out, slice(0, 2), cols[0:2].astype(BF), cols[2:4].astype(BF))


def mixed_edges_kernel(
    flag_ref, cols_in, inner_ref, outer_ref, inner_out, outer_out, first_ref, last_ref, south_ref, north_ref, cols
):
    top, odd = flag_ref[0] != 0, flag_ref[1] != 0
    for r in range(2):
        south_ref[r] = jnp.where(odd, inner_ref[r], outer_ref[r])
        s = south_ref[r].astype(F32)
        n = jnp.where(odd, outer_ref[r], inner_ref[r]).astype(F32)
        n = jnp.where(top, turned_row(outer_ref[1 - r]), n)
        north_ref[r] = n.astype(BF)
        for k, i in enumerate((0, 1, 62, 63)):
            cols[k, r : r + 1, :] = s[i : i + 1]
            cols[k, 34 + r : 35 + r, :] = n[i : i + 1]
    for k in range(4):
        cols[k, 2:34, :] = cols_in[k].astype(F32)
    first_ref[...] = cols[0].astype(BF)
    last_ref[...] = cols[3].astype(BF)
    put_pair(flag_ref[2] != 0, inner_out, outer_out, slice(0, 2), cols[0:2].astype(BF), cols[2:4].astype(BF))


def flux_edges_kernel(flag_ref, first_ref, last_ref, inner_ref, outer_ref, south_ref, north_ref, inner_out, outer_out):
    odd, east_odd = flag_ref[1] != 0, flag_ref[2] != 0
    for r in range(20):
        if r < 16:
            first, last = first_ref[r], last_ref[r]
        else:
            a, b = (inner_ref, outer_ref) if r >= 18 else (outer_ref, inner_ref)
            row = jnp.where(odd, a[r % 2], b[r % 2])
            (north_ref if r < 18 else south_ref)[r % 2] = row
            first, last = row[0:2], row[62:64]
        put_pair(east_odd, inner_out, outer_out, r, first, last)


def atmos_windows(flag_ref, windows, x_ref, s_ref, n_ref, in_ref, out_ref):
    odd = flag_ref[2] != 0
    west = jnp.where(odd, in_ref[0].astype(F32), out_ref[0].astype(F32))
    east = jnp.where(odd, out_ref[0].astype(F32), in_ref[0].astype(F32))
    build_windows(
        windows,
        34,
        lambda r: s_ref[0] if r == 0 else (n_ref[0] if r == 33 else x_ref[r - 1]),
        lambda r: west[r : r + 1, :],
        lambda r: east[r : r + 1, :],
    )


def packed_maps(p_ref):
    p = p_ref[...]
    zeros = jnp.zeros_like(p)
    return jnp.concatenate([p, zeros], 0), jnp.concatenate([zeros, p], 0)


def atmos_kernel(
    flag_ref, x_ref, s_ref, n_ref, in_ref, out_ref, w_ref, p_ref,
    act_ref, slope_ref, own_ref, inner_out, outer_out, first_ref, last_ref, windows,
):
    atmos_windows(flag_ref, windows, x_ref, s_ref, n_ref, in_ref, out_ref)
    maps = packed_maps(p_ref)
    for b in range(2):
        packed = jnp.zeros((512, 128), F32)
        for h in range(2):
            start = h * 1024 + b * 512
            pre = conv_rows(windows, w_ref, start, 512)
            sigma = sigmoid(pre)
            act = (pre * sigma).astype(BF)
            act_ref[start : start + 512, :] = act
            slope_ref[start : start + 512, :] = silu_slope(pre, sigma).astype(BF)
            packed += dot_back(act, maps[h])
        for u in range(8):
            r = b * 8 + u
            row = packed[u * 64 : u * 64 + 64].astype(BF)
            own_ref[r] = row
            first_ref[r] = row[0:2]
            last_ref[r] = row[62:64]
    for r in range(2):
        put_pair(flag_ref[1] != 0, inner_out, outer_out, r, own_ref[r], own_ref[14 + r])


def ocean_kernel(
    flag_ref, x_ref, s_ref, n_ref, first_ref, last_ref, in_ref, beyond_ref, c_ref, cs_ref, cn_ref, ci_ref, co_ref, m_ref,
    w_ref, wt_ref, inj_ref, out_ref, remap_ref, deltas, back,
    windows, sides, north, turned_north, dwin, dsides,
):
    top, odd = flag_ref[0] != 0, flag_ref[2] != 0
    west = [jnp.where(odd, in_ref[k].astype(F32), beyond_ref[k].astype(F32)) for k in range(2)]
    east = [jnp.where(odd, beyond_ref[k].astype(F32), in_ref[k].astype(F32)) for k in range(2)]
    cot_west = jnp.where(odd, ci_ref[1].astype(F32), co_ref[1].astype(F32))
    cot_east = jnp.where(odd, co_ref[1].astype(F32), ci_ref[1].astype(F32))
    land = m_ref[...].astype(F32).T
    build_windows(
        windows,
        36,
        lambda r: s_ref[r] if r < 2 else (n_ref[r - 34] if r >= 34 else x_ref[r - 2]),
        lambda r: west[1][r : r + 1, :],
        lambda r: east[0][r : r + 1, :],
    )
    sides[...] = jnp.zeros_like(sides)
    for side, columns in ((0, (west[0], west[1], first_ref[...])), (1, (last_ref[...], east[0], east[1]))):
        for q in range(3):
            sides[side, 0:36, q * 256 : q * 256 + 256] = columns[q].astype(F32)

    def side_rows(start, count):
        return jnp.concatenate([sides[0, start : start + count, :], sides[1, start : start + count, :]], 0).astype(BF)

    pre = jnp.zeros((80, 256), F32)
    lines = [jnp.concatenate([windows[(33 + r) * 64 : (34 + r) * 64, :], side_rows(33 + r, 8)], 0) for r in range(3)]
    for r in range(3):
        pre += jnp.dot(jnp.where(top, turned_lanes(lines[2 - r]), lines[r]), w_ref[r], preferred_element_type=F32)
    slope = silu_slope(pre, sigmoid(pre))
    d_north = (cn_ref[1].astype(F32) * slope[0:64]).astype(BF)
    side_pre = jnp.zeros((80, 256), F32)
    for r in range(3):
        side_pre += jnp.dot(side_rows(r, 40), w_ref[r], preferred_element_type=F32)
    side_slope = silu_slope(side_pre, sigmoid(side_pre))
    at = lax.broadcasted_iota(jnp.int32, (40, 256), 0)
    for side, cot in ((0, cot_west), (1, cot_east)):
        corner = slope[64 + side * 8 : 65 + side * 8]
        here = jnp.where(at == 33, corner, side_slope[side * 40 : side * 40 + 40])
        dsides[side] = jnp.zeros((40, 256), F32)
        dsides[side, 0:34, :] = cot * here[0:34]
    pre = conv_rows(windows, w_ref, 0, 64)
    d_south = (cs_ref[1].astype(F32) * silu_slope(pre, sigmoid(pre))).astype(BF)
    for b in range(4):
        pre = conv_rows(windows, w_ref, 64 + b * 512, 512)
        sigma = sigmoid(pre)
        act = pre * sigma
        slope = silu_slope(pre, sigma)
        for u in range(8):
            r = b * 8 + u
            here = slice(u * 64, u * 64 + 64)
            wet = land[:, r : r + 1]
            out_ref[r] = (wet * act[here]).astype(BF)
            deltas[r * 64 : r * 64 + 64, :] = (c_ref[r].astype(F32) * wet * slope[here]).astype(BF)
    dry = jnp.zeros((64, 256), BF)
    build_windows(
        dwin,
        34,
        lambda r: d_south if r == 0 else (dry if r == 33 else deltas[r * 64 - 64 : r * 64, :]),
        lambda r: dsides[0, r : r + 1, :] if r < 33 else dry[0:1],
        lambda r: dsides[1, r : r + 1, :] if r < 33 else dry[0:1],
        turned=True,
    )
    for dst, turned in ((north, False), (turned_north, True)):
        build_windows(
            dst, 1, lambda r: d_north, lambda r: dsides[0, 33:34, :], lambda r: dsides[1, 33:34, :], turned=turned
        )
    beyond = jnp.dot(
        jnp.where(top, north[...], turned_north[...]), wt_ref[jnp.where(top, 2, 0)], preferred_element_type=F32
    )
    inject = jnp.concatenate([inj_ref[...], inj_ref[...]], 0)
    for b in range(4):
        total = conv_rows(dwin, wt_ref, b * 512, 512, turned=True)
        for u in range(8):
            r = b * 8 + u
            value = total[u * 64 : u * 64 + 64]
            if r == 31:
                value = value + beyond
            back[r * 64 : r * 64 + 64, :] = (land[:, r : r + 1] * value).astype(BF)
        remap_ref[b * 512 : b * 512 + 512, :] = dot_back(back[b * 512 : b * 512 + 512, :], inject).astype(BF)


def ocean_grads_kernel(
    flag_ref, x_ref, s_ref, n_ref, in_ref, beyond_ref, deltas, back, rem_ref, keep_ref, send_ref, windows
):
    core, odd = flag_ref[1], flag_ref[2] != 0
    west = jnp.where(odd, in_ref[1].astype(F32), beyond_ref[1].astype(F32))
    east = jnp.where(odd, beyond_ref[0].astype(F32), in_ref[0].astype(F32))
    build_windows(
        windows,
        34,
        lambda r: s_ref[1] if r == 0 else (n_ref[0] if r == 33 else x_ref[r - 1]),
        lambda r: west[r + 1 : r + 2, :],
        lambda r: east[r + 1 : r + 2, :],
    )
    for r in range(3):
        value = dot_rows(windows[r * 64 : r * 64 + 2048, :], deltas[...])
        put_half(core, keep_ref, send_ref, slice(r * 768, r * 768 + 768), value)
    tail = jnp.concatenate([dot_rows(rem_ref[...], back[...])[0:64], jnp.zeros((32, 256), F32)], 0)
    put_half(core, keep_ref, send_ref, slice(2304, 2400), tail)


def credit_rows_kernel(flag_ref, n_ref, s_ref, in_ref, out_ref, inner_out, outer_out, n_sum, s_sum):
    odd, east_odd = flag_ref[1] != 0, flag_ref[2] != 0
    for r in range(2):
        for src, dst, first in ((n_ref, n_sum, 16), (s_ref, s_sum, 18)):
            inner, outer = in_ref[first + r].astype(F32), out_ref[first + r].astype(F32)
            dst[r] = src[r].astype(F32)
            dst[r, 0:2] = dst[r, 0:2] + jnp.where(east_odd, inner, outer)
            dst[r, 62:64] = dst[r, 62:64] + jnp.where(east_odd, outer, inner)
        put_pair(odd, inner_out, outer_out, r, s_sum[r].astype(BF), n_sum[r].astype(BF))


def atmos_back_kernel(
    flag_ref, x_ref, s_ref, n_ref, in_ref, out_ref, act_ref, slope_ref, own_ref, ci_ref, co_ref, ri_ref, ro_ref, bi_ref, bo_ref,
    low_ref, p_ref, keep_ref, send_ref, windows, deltas, total, credit,
):
    core = flag_ref[1]
    odd, east_odd = core != 0, flag_ref[2] != 0
    atmos_windows(flag_ref, windows, x_ref, s_ref, n_ref, in_ref, out_ref)
    maps = packed_maps(p_ref)
    for r in range(16):
        value = own_ref[r].astype(F32) + bi_ref[16 + r].astype(F32) + bo_ref[16 + r].astype(F32) + low_ref[r].astype(F32)
        if r < 2:
            value += jnp.where(odd, ri_ref[r].astype(F32), ro_ref[r].astype(F32))
        if r >= 14:
            value += jnp.where(odd, ro_ref[r - 14].astype(F32), ri_ref[r - 14].astype(F32))
        total[...] = value
        inner, outer = ci_ref[r].astype(F32), co_ref[r].astype(F32)
        total[0:2, :] += jnp.where(east_odd, inner, outer)
        total[62:64, :] += jnp.where(east_odd, outer, inner)
        credit[r * 64 : r * 64 + 64, :] = total[...].astype(BF)
    for h in range(2):
        here = slice(h * 1024, h * 1024 + 1024)
        back = jnp.dot(credit[...], maps[h], preferred_element_type=F32)
        deltas[here, :] = (back * slope_ref[here, :].astype(F32)).astype(BF)
    for r in range(3):
        value = dot_rows(windows[r * 64 : r * 64 + 2048, :], deltas[...])
        put_half(core, keep_ref, send_ref, slice(r * 768, r * 768 + 768), value)
    lower = dot_rows(credit[...], act_ref[0:1024, :])
    upper = dot_rows(credit[...], act_ref[1024:2048, :])
    tail = jnp.concatenate([lower[0:64] + upper[64:128], jnp.zeros((32, 256), F32)], 0)
    put_half(core, keep_ref, send_ref, slice(2304, 2400), tail)


def exchange(x, mask):
    count = lax.axis_size("lon") * lax.axis_size("lat")
    return lax.ppermute(x, AXES, [(i, i ^ mask) for i in range(count)])


def reduce_streams(streams, orders):
    rank = lax.axis_index("lon") * lax.axis_size("lat") + lax.axis_index("lat")
    bit = lambda n: (rank >> n) & 1
    near = [(2, bit(1) ^ bit(2)), (8, bit(3) ^ bit(4)), (32, bit(5) ^ bit(6))]
    far = (6, 24, 96)
    count = range(len(streams))
    for level in range(3):
        steps = [near[orders[i][level]] for i in count]
        half = streams[0].shape[0] // 2
        keep = [lax.dynamic_slice_in_dim(streams[i], steps[i][1] * half, half) for i in count]
        send = [lax.dynamic_slice_in_dim(streams[i], (1 - steps[i][1]) * half, half).astype(BF) for i in count]
        streams = [keep[i] + exchange(send[i], steps[i][0]).astype(F32) for i in count]
    streams = [s.astype(BF) for s in streams]
    for level in range(3):
        got = [exchange(streams[i], far[orders[i][level]]) for i in count]
        streams = [(streams[i].astype(F32) + got[i].astype(F32)).astype(BF) for i in count]
    for level in (2, 1, 0):
        steps = [near[orders[i][level]] for i in count]
        got = [exchange(streams[i], steps[i][0]) for i in count]
        streams = [
            jnp.where(
                steps[i][1] == 0,
                jnp.concatenate([streams[i], got[i]]),
                jnp.concatenate([got[i], streams[i]]),
            )
            for i in count
        ]
    return streams


def lane_sign():
    lane = lax.broadcasted_iota(jnp.int32, (64, 128), 1)
    return jnp.where(lane < 64, jnp.float32(1.0), jnp.float32(-1.0))


def gather_kernel(
    flag_ref, slot_ref, w_ref, fn_ref, fs_ref, fi_ref, fo_ref, low_ref, own_ref, bi_ref, bo_ref, o_ref, m_ref, inj_ref,
    out_ref, mixed_ref, cols_ref, inner_ref, outer_ref, table, picked, cols,
):
    top = flag_ref[0]
    odd, east_odd = flag_ref[1] != 0, flag_ref[2] != 0

    @pl.when(top == 0)
    def _():
        for r in range(20):
            rows = own_ref[r] if r < 16 else (fn_ref[r - 16] if r < 18 else fs_ref[r - 18])
            table[r * NEAR : r * NEAR + 64, :] = rows.astype(F32)
            table[r * NEAR + 64 : r * NEAR + 66, :] = jnp.where(east_odd, fi_ref[r].astype(F32), fo_ref[r].astype(F32))
            table[r * NEAR + 66 : r * NEAR + 68, :] = jnp.where(east_odd, fo_ref[r].astype(F32), fi_ref[r].astype(F32))

    @pl.when(top != 0)
    def _():
        for r in range(32):
            base = r * BAND
            table[base : base + 64, :] = (low_ref[r] if r < 16 else own_ref[r - 16]).astype(F32)
            inner, outer = bi_ref[r].astype(F32), bo_ref[r].astype(F32)
            table[base + 64 : base + 128, :] = jnp.where(east_odd, inner, outer)
            table[base + 128 : base + 192, :] = jnp.where(east_odd, outer, inner)

    def step(q, carry):
        base = pl.multiple_of(q * 64, 64)
        for u in range(64):
            at = slot_ref[q, u]
            picked[pl.ds(base + u, 1), :] = table[pl.ds(at, 1), :]
        return carry

    lax.fori_loop(0, 128, step, 0)
    sign = lane_sign()
    wt = w_ref[...].T
    for row in range(32):
        acc = jnp.zeros((64, 128), F32)
        for k in range(4):
            q = row * 4 + k
            factor = jnp.maximum(wt[:, q : q + 1] * sign, 0.0)
            acc = acc + factor * picked[q * 64 : q * 64 + 64, :]
        acc = acc + pltpu.roll(acc, 64, 1)
        out_ref[row * 64 : row * 64 + 64, :] = acc.astype(BF)
    land = m_ref[...].astype(F32).T
    inject = jnp.concatenate([inj_ref[...], jnp.zeros_like(inj_ref[...])], 0)
    for b in range(4):
        injected = jnp.dot(out_ref[b * 512 : b * 512 + 512, :], inject, preferred_element_type=F32)
        for u in range(8):
            r = b * 8 + u
            value = land[:, r : r + 1] * (o_ref[r].astype(F32) + injected[u * 64 : u * 64 + 64])
            mixed_ref[r] = value.astype(BF)
            for c, i in enumerate((0, 1, 62, 63)):
                cols[c, r : r + 1, :] = value[i : i + 1]
    for r in range(2):
        put_pair(odd, inner_ref, outer_ref, r, mixed_ref[r], mixed_ref[30 + r])
    cols_ref[...] = cols[...].astype(BF)


def scatter_kernel(
    flag_ref, slot_ref, w_ref, g_ref, own_ref, n_ref, s_ref, side_in, side_out, low_ref, band_in, band_out, *scratch
):
    top = flag_ref[0]
    east_odd = flag_ref[2] != 0
    tables, parts = scratch[:8], scratch[8]

    def clear(count):
        def one(i, carry):
            base = pl.multiple_of(i * 96, 96)
            for t in tables:
                t[pl.ds(base, 96), :] = jnp.zeros((96, 128), F32)
            return carry

        lax.fori_loop(0, count // 96, one, 0)

    @pl.when(top == 0)
    def _():
        clear(20 * NEAR)

    @pl.when(top != 0)
    def _():
        clear(32 * BAND)

    sign = lane_sign()
    wt = w_ref[...].T
    for row in range(32):
        g = g_ref[row * 64 : row * 64 + 64, :].astype(F32)
        for k in range(4):
            q = row * 4 + k
            parts[q * 64 : q * 64 + 64, :] = jnp.maximum(wt[:, q : q + 1] * sign, 0.0) * g

    def step(row, carry):
        base = pl.multiple_of(row * 256, 256)
        for u in range(64):
            for k in range(4):
                at = slot_ref[row * 4 + k, u]
                t = tables[k + u % 2 * 4]
                t[pl.ds(at, 1), :] = t[pl.ds(at, 1), :] + parts[pl.ds(base + k * 64 + u, 1), :]
        return carry

    lax.fori_loop(0, 32, step, 0)

    def total(start, size):
        where = pl.ds(start, size)
        pairs = [tables[k][where, :] + tables[k + 4][where, :] for k in range(4)]
        return ((pairs[0] + pairs[1]) + (pairs[2] + pairs[3])).astype(BF)

    @pl.when(top == 0)
    def _():
        for r in range(20):
            rows = total(r * NEAR, 64)
            if r < 16:
                own_ref[r] = rows
            elif r < 18:
                n_ref[r - 16] = rows
            else:
                s_ref[r - 18] = rows
            put_pair(east_odd, side_in, side_out, r, total(r * NEAR + 64, 2), total(r * NEAR + 66, 2))

    @pl.when(top != 0)
    def _():
        for r in range(2):
            n_ref[r] = jnp.zeros((64, 128), BF)
            s_ref[r] = jnp.zeros((64, 128), BF)
        side_in[...] = jnp.zeros_like(side_in)
        side_out[...] = jnp.zeros_like(side_out)
        for r in range(32):
            base = r * BAND
            if r < 16:
                low_ref[r] = total(base, 64)
            else:
                own_ref[r - 16] = total(base, 64)
            put_pair(east_odd, band_in, band_out, r, total(base + 64, 64), total(base + 128, 64))


def entry_slots(source_row, source_col, weight, is_top, row_count, col_count):
    nx = col_count * lax.axis_size("lon")
    row = source_row - lax.axis_index("lat") * row_count
    col = jnp.remainder(source_col - lax.axis_index("lon") * col_count + nx // 2, nx) - nx // 2
    half = row_count // 2
    inside = (row >= 0) & (row < row_count)
    wrapped = row & (row_count - 1)
    packed = wrapped & (half - 1)
    upper = wrapped >= half
    near_row = jnp.where(inside, packed, jnp.where(row < 0, packed + 4, packed + half))
    near_col = jnp.where((col >= 0) & (col < col_count), col, jnp.where(col < 0, col + col_count + 2, col + 2))
    band_row = jnp.where(row >= 0, packed + half, packed)
    band_col = jnp.where((col >= 0) & (col < col_count), col, jnp.where(col < 0, col + 2 * col_count, col + col_count))
    slot = jnp.where(is_top, band_row * BAND + band_col, near_row * NEAR + near_col)
    signed = jnp.where(upper, -weight, weight)
    order = lambda x: jnp.transpose(x, (0, 2, 1)).reshape(-1, col_count)
    return order(slot), order(signed)


def body(
    atmos_state,
    atmos_weights,
    flux_project,
    source_row,
    source_col,
    intersection_weight,
    ocean_state,
    flux_inject,
    ocean_mask,
    ocean_weights,
    out_cotangent,
):
    row_count, col_count, chans = atmos_state.shape
    flux_chans = flux_project.shape[1]
    cells = row_count * col_count
    half = cells // 2
    lats = lax.axis_size("lat")
    is_top = lax.axis_index("lat") == lats - 1
    core = lax.rem(lax.axis_index("lat"), 2)
    flags = jnp.stack([is_top.astype(jnp.int32), core, lax.rem(lax.axis_index("lon"), 2)])
    struct = lambda *shape: (shape, BF)
    stored = lambda *shape: (shape, BF, True)
    block = lambda shape, at: pl.BlockSpec(shape, lambda i: (at[0], at[1], 0))
    row = (1, 64, 256)
    inner, outer = call(
        rows_kernel,
        "rows",
        (struct(2, 64, 256), struct(2, 64, 256)),
        (flags, atmos_state, atmos_state, out_cotangent, out_cotangent, ocean_mask),
        specs=[SMEM, block(row, (0, 0)), block(row, (31, 0)), block(row, (0, 0)), block(row, (31, 0)), VMEM],
        grid=(1,),
    )
    inner, outer = lat_pairs(inner, outer, True)
    slab = (32, 16, 256)
    inner, outer, south, north = call(
        edges_kernel,
        "edges",
        (struct(2, 34, 256), struct(2, 34, 256), struct(2, 64, 256), struct(2, 64, 256)),
        (flags, atmos_state, atmos_state, out_cotangent, out_cotangent, ocean_mask, inner, outer),
        [pltpu.VMEM((4, 34, 256), F32)],
        specs=[SMEM, block(slab, (0, 0)), block(slab, (0, 3)), block(slab, (0, 0)), block(slab, (0, 3))] + [VMEM] * 3,
        grid=(1,),
    )
    side_in, side_out = lon_pairs(inner, outer)
    project = flux_project.T
    atmos_w = atmos_weights.reshape(3, 3 * chans, chans)
    ocean_w = ocean_weights.reshape(3, 3 * chans, chans)
    act, slope, own, inner, outer, first, last = call(
        atmos_kernel,
        "atmos",
        (stored(cells, chans), stored(cells, chans), struct(16, 64, 128), struct(2, 64, 128), struct(2, 64, 128),
         struct(16, 2, 128), struct(16, 2, 128)),
        (flags, atmos_state, south, north, side_in, side_out, atmos_w, project),
        [pltpu.VMEM((34 * 64, 768), BF)],
        scalars=1,
    )
    low_tile = lax.ppermute(own, "lat", [(lats - 2, lats - 1)])
    inner, outer = lat_pairs(inner, outer, False)
    two, inner, outer = lax.optimization_barrier((jnp.concatenate([low_tile, own], 0), inner, outer))
    band_in, band_out = lon_pairs(two, two, lats - 1)
    flux_south, flux_north, inner, outer = call(
        flux_edges_kernel,
        "flux_edges",
        (struct(2, 64, 128), struct(2, 64, 128), struct(20, 2, 128), struct(20, 2, 128)),
        (flags, first, last, inner, outer),
        scalars=1,
    )
    flux_in, flux_out = lon_pairs(inner, outer, 0, lats - 1)
    late = lax.optimization_barrier((own, source_row, source_col, intersection_weight, ocean_weights))
    slots, signed = entry_slots(*late[1:4], is_top, row_count, col_count)
    back_w = jnp.transpose(late[4], (0, 2, 1)).reshape(3, 3 * chans, chans)
    remapped, mixed, cols, inner, outer = call(
        gather_kernel,
        "gather_mix",
        (struct(cells, 128), stored(32, 64, 256), struct(4, 32, 256), struct(2, 64, 256), struct(2, 64, 256)),
        (flags, slots, signed, flux_north, flux_south, flux_in, flux_out, low_tile, own, band_in, band_out,
         ocean_state, ocean_mask, flux_inject),
        [pltpu.VMEM((32 * BAND, 128), F32), pltpu.VMEM((8192, 128), F32), pltpu.VMEM((4, 32, 256), F32)],
        scalars=2,
    )
    inner, outer = lat_pairs(inner, outer, True)
    inner, outer, first, last, mixed_south, mixed_north = call(
        mixed_edges_kernel,
        "mixed_edges",
        (struct(2, 36, 256), struct(2, 36, 256), struct(36, 256), struct(36, 256), struct(2, 64, 256), struct(2, 64, 256)),
        (flags, cols, inner, outer),
        [pltpu.VMEM((4, 36, 256), F32)],
        scalars=1,
    )
    mixed_in, mixed_out = lon_pairs(inner, outer)
    halves = ((GRAD_ROWS, 128), F32), ((GRAD_ROWS, 128), BF)
    ocean_out, remap_grad, deltas, back = call(
        ocean_kernel,
        "ocean",
        (struct(32, 64, 256), struct(cells, 128), stored(cells, 256), stored(cells, 256)),
        (
            flags, mixed, mixed_south, mixed_north, first, last, mixed_in, mixed_out,
            out_cotangent, south, north, side_in, side_out, ocean_mask, ocean_w, back_w, flux_inject,
        ),
        [
            pltpu.VMEM((36 * 64, 768), BF),
            pltpu.VMEM((2, 48, 768), F32),
            pltpu.VMEM((64, 768), BF),
            pltpu.VMEM((64, 768), BF),
            pltpu.VMEM((34 * 64, 768), BF),
            pltpu.VMEM((2, 40, 256), F32),
        ],
        scalars=1,
    )
    own, to_north, to_south, inner, outer, low_tile, band_in, band_out = call(
        scatter_kernel,
        "scatter_rows",
        (struct(16, 64, 128), struct(2, 64, 128), struct(2, 64, 128), struct(20, 2, 128), struct(20, 2, 128),
         struct(16, 64, 128), struct(32, 64, 128), struct(32, 64, 128)),
        (flags, slots, signed, remap_grad),
        [pltpu.VMEM((32 * BAND, 128), F32)] * 8 + [pltpu.VMEM((8192, 128), F32)],
        scalars=2,
    )
    deltas, back, inner, outer, band_in, band_out = lax.optimization_barrier((deltas, back, inner, outer, band_in, band_out))
    ocean_keep, ocean_send = call(
        ocean_grads_kernel,
        "ocean_grads",
        halves,
        (flags, mixed, mixed_south, mixed_north, mixed_in, mixed_out, deltas, back, remapped),
        [pltpu.VMEM((34 * 64, 768), BF)],
        scalars=1,
    )
    band_in, band_out = lon_pairs(band_in, band_out, lats - 1)
    credit_in, credit_out = lon_pairs(inner, outer, 0, lats - 1)
    credit_in, credit_out, ocean_keep, ocean_send = lax.optimization_barrier(
        (credit_in, credit_out, ocean_keep, ocean_send)
    )
    inner, outer = call(
        credit_rows_kernel,
        "credit_rows",
        (struct(2, 64, 128),) * 2,
        (flags, to_north, to_south, credit_in, credit_out),
        [pltpu.VMEM((2, 64, 128), F32)] * 2,
        scalars=1,
    )
    rows_in, rows_out = lat_pairs(inner, outer, False)
    band_in, band_out, _ = lax.optimization_barrier((band_in, band_out, inner))
    low_tile = low_tile.astype(F32) + band_in[:16].astype(F32) + band_out[:16].astype(F32)
    from_band = lax.ppermute(low_tile.astype(BF), "lat", [(lats - 1, lats - 2)])
    atmos_keep, atmos_send = call(
        atmos_back_kernel,
        "atmos_back",
        halves,
        (flags, atmos_state, south, north, side_in, side_out, act, slope, own, credit_in, credit_out, rows_in, rows_out,
         band_in, band_out, from_band, project),
        [pltpu.VMEM((34 * 64, 768), BF), pltpu.VMEM((cells, 256), BF), pltpu.VMEM((64, 128), F32), pltpu.VMEM((half, 128), BF)],
        scalars=1,
    )
    ocean = ocean_keep + exchange(ocean_send, 1).astype(F32)
    ocean, atmos = lax.optimization_barrier((ocean, atmos_keep + exchange(atmos_send, 1).astype(F32)))
    cut = 1600
    rest = GRAD_ROWS - cut
    sums = reduce_streams(
        [ocean[:cut], jnp.concatenate([ocean[cut:], atmos[:rest]]), atmos[rest:]], ((0, 1, 2), (1, 2, 0), (2, 0, 1))
    )
    ocean = jnp.concatenate([sums[0], sums[1][:rest]])
    atmos = jnp.concatenate([sums[1][rest:], sums[2]])

    def joined(mine):
        other = exchange(mine, 1)

        def rows(start, stop):
            a, b = mine[start:stop], other[start:stop]
            return jnp.concatenate([jnp.where(core == 0, a, b), jnp.where(core == 0, b, a)], 1).astype(F32)

        return rows(0, 9 * chans).reshape(9, chans, chans), rows(9 * chans, 9 * chans + flux_chans)

    grad_ocean, grad_inject = joined(ocean)
    grad_atmos, grad_project = joined(atmos)
    return (ocean_out, grad_atmos, grad_ocean, grad_project.T, grad_inject)


def solution(mesh):
    return jax.shard_map(
        body,
        mesh=mesh,
        in_specs=(
            P("lat", "lon", None),
            P(),
            P(),
            P("lat", "lon", None),
            P("lat", "lon", None),
            P("lat", "lon", None),
            P("lat", "lon", None),
            P(),
            P("lat", "lon"),
            P(),
            P("lat", "lon", None),
        ),
        out_specs=(P("lat", "lon", None), P(), P(), P(), P()),
        check_vma=False,
    )
```
